128 devices in a mesh: dom: 16 (over y_hi, z, core), blk: 8 (over x, y_lo).
Axes of the slice: x: 4, y: 4 (y_hi: 2, y_lo: 2; y = y_hi * 2 + y_lo), z: 4, core: 2. Of those that a mesh axis runs over, the one named last changes fastest.
Arguments:
- images: bfloat16 [1024, 128, 256], P('dom', 'blk'), may hold values from -4.5 to 6.5
- ref_store: bfloat16 [16, 16, 4, 128, 256], P('dom', None, None, 'blk'), may hold values from -0.03125 to 0.03125
- block_owner: int32 [16], replicated, may hold values from 0 to 15, as said below
- class_gain: float32 [64], replicated, may hold values from 0.5 to 2
- precision: float32 [1024], P('dom'), may hold values from 0.5 to 80
Outputs:
- class_sums: float32 [16, 1, 4, 128, 256], P('dom', None, None, 'blk')
The draws below stay inside these ranges and needn't reach their ends.
Inputs may be any that keep to these rules, and one draw needn't show every extreme that they name: `block_owner`: each index d of dom owns exactly 1 block.
All inputs are finite; a program needn't handle non-finite values.
Results may differ from the reference program's by a relative error of at most 0.0049.
Values may be sent and summed in bfloat16 or wider, within the bound.
No kernel may reach another device: no remote copies, remote signals or barrier semaphores. Data moves between devices by JAX's collectives and lax.ppermute only.
A program may use at most 64 MiB of HBM per device.

```python
import math
import jax
import jax.numpy as jnp

R = 128
A = 256
S = 64
K = 64
NBLK = 16
KB = 4
BLK_PER = 1
PARTICLES = 1024
ROT_STEP = 4
N_DOM = 16


def draw_block_owner(key, part):
    shuffled = jax.random.permutation(key, NBLK)
    return (shuffled // BLK_PER).astype(jnp.int32)


def draw_images(key, part):
    cycle_key = jax.random.fold_in(key, 11)
    noise_key = jax.random.fold_in(key, 12)
    cycle_level = jax.random.uniform(cycle_key, (1, R, 1), jnp.float32, 0.5, 1.5)
    noise = jax.random.truncated_normal(noise_key, -5.0, 5.0, (PARTICLES, R, A), jnp.float32)
    return (noise + cycle_level).astype(jnp.bfloat16)


def draw_precision(key, part):
    base_key = jax.random.fold_in(key, 21)
    fraction = jax.random.uniform(base_key, (PARTICLES,), jnp.float32)
    values = jnp.exp(math.log(0.8) + fraction * (math.log(1.6) - math.log(0.8)))
    return values.astype(jnp.float32)


def block_levels(key, shape, shards, smallest, top_value):
    loudness = 1.0
    for dim, shards_of in shards:
        draws = jax.random.uniform(jax.random.fold_in(jax.random.fold_in(key, 6), dim), (shards_of,), jnp.float32, smallest / len(shards), top_value / len(shards))
        loudness = loudness * jnp.repeat(jnp.exp(draws), shape[dim] // shards_of).reshape((-1,) + (1,) * (len(shape) - 1 - dim))
    return loudness


def normal_values(rng, extent, scale, reach, cuts=(), kind=jnp.bfloat16):
    level = block_levels(rng, extent, cuts, -0.22, 0.18) if cuts else 1.0
    array = jax.random.normal(rng, extent, jnp.float32) * scale * level
    return jnp.minimum(jnp.maximum(array, -reach), reach).astype(kind)


def setup_inputs(seed: int = 0) -> dict:
    streams_of = jax.random.split(jax.random.key(seed), 6)
    images = draw_images(jax.random.fold_in(streams_of[5], 71), 0)
    ref_store = normal_values(streams_of[1], (N_DOM, NBLK, KB, R, A), (R * A) ** -0.5, 0.03125, ((0, 16), (3, 8)))
    block_owner = draw_block_owner(jax.random.fold_in(streams_of[5], 71), 0)
    class_gain = jnp.clip(jnp.exp(jax.random.uniform(streams_of[3], (K,), jnp.float32, math.log(0.5), math.log(2.0))), 0.5, 2.0)
    precision = draw_precision(jax.random.fold_in(streams_of[5], 71), 0)
    return dict(images=images, ref_store=ref_store, block_owner=block_owner, class_gain=class_gain, precision=precision)


def reference(images, ref_store, block_owner, class_gain, precision):
    block_ids = jnp.arange(NBLK, dtype=jnp.int32)
    stored = ref_store[block_owner, block_ids]
    references = (stored.astype(jnp.float32) * class_gain.reshape(NBLK, KB, 1, 1)).astype(jnp.bfloat16)
    ref_float = references.astype(jnp.float32).reshape(K, R, A)
    norm_sums = jnp.sum(ref_float * ref_float, axis=(1, 2))
    image_float = images.astype(jnp.float32)
    image_spec = jnp.fft.rfft(image_float, axis=-1)
    ref_spec = jnp.fft.rfft(ref_float, axis=-1)
    cross_spec = jnp.einsum('prf,krf->pkf', jnp.conj(image_spec), ref_spec)
    correlation = jnp.fft.irfft(cross_spec, n=A, axis=-1)[:, :, ::ROT_STEP]
    logits = precision[:, None, None] * (correlation - 0.5 * norm_sums[None, :, None])
    flat_logits = logits.reshape(PARTICLES, K * S)
    row_max = jnp.max(flat_logits, axis=1, keepdims=True)
    exponent = jnp.exp(flat_logits - row_max)
    weights = exponent / jnp.sum(exponent, axis=1, keepdims=True)
    weight_float = weights.reshape(PARTICLES, K, S)
    weight_full = jnp.zeros((PARTICLES, K, A), jnp.float32).at[:, :, ::ROT_STEP].set(weight_float)
    weight_spec = jnp.fft.rfft(weight_full, axis=-1)
    total_spec = jnp.einsum('pkf,prf->krf', weight_spec, image_spec)
    totals = jnp.fft.irfft(total_spec, n=A, axis=-1).astype(jnp.float32)
    owner_order = jnp.argsort(block_owner, stable=True).astype(jnp.int32)
    blocked = totals.reshape(NBLK, KB, R, A)[owner_order]
    return blocked.reshape(N_DOM, BLK_PER, KB, R, A)
```

```python
import jax
import jax.numpy as jnp
from jax import lax
from jax.experimental import pallas as pl
from jax.experimental.pallas import tpu as pltpu
from jax.sharding import Mesh, PartitionSpec as P

BF = jnp.bfloat16
F32 = jnp.float32
VM = pltpu.VMEM
N1 = 8
N2 = 8


def spec(space=VM):
    return pl.BlockSpec(memory_space=space)


def scratch(rows, angles):
    return VM((angles // 128, rows, 128), F32)


def fill(scr, value):
    for h in range(scr.shape[0]):
        scr[h] = value[:, h * 128 : (h + 1) * 128]


def take_cycle(scr, r, rows, cycles):
    pieces = [scr.at[h][pl.ds(r, rows, stride=cycles), :] for h in range(scr.shape[0])]
    return jnp.concatenate(pieces, axis=1)


def params():
    return pltpu.CompilerParams(vmem_limit_bytes=56 * 1024 * 1024)


def pick_block(me, block_owner, class_gain, ref_store, copies):
    nblk, kb, cycles, angles = ref_store.shape

    def body(me_ref, owner_ref, gain_ref, store_ref, out_ref, buf, sem):
        block = jnp.int32(0)
        for b in range(nblk):
            block = jnp.where(owner_ref[b] == me_ref[0], jnp.int32(b), block)
        copy = pltpu.make_async_copy(store_ref.at[block], buf, sem)
        copy.start()
        copy.wait()
        for i in range(kb):
            piece = (buf[i].astype(F32) * gain_ref[block * kb + i]).astype(BF)
            for c in range(copies):
                out_ref[c, i * cycles : (i + 1) * cycles, :] = piece

    return pl.pallas_call(
        body,
        out_shape=jax.ShapeDtypeStruct((copies, kb * cycles, angles), BF),
        in_specs=[spec(pltpu.SMEM), spec(pltpu.SMEM), spec(pltpu.SMEM), spec(pl.ANY)],
        out_specs=spec(),
        scratch_shapes=[VM((kb, cycles, angles), BF), pltpu.SemaphoreType.DMA],
        compiler_params=params(),
        name="pick_block",
    )(me, block_owner, class_gain, ref_store)


def rotate_images(own, other, nb, step):
    particles, cycles, angles = own.shape
    per = particles // nb

    def body(own_ref, other_ref, out_ref, a_scr, b_scr):
        fill(a_scr, own_ref[...].astype(F32).reshape(particles * cycles, angles))
        fill(b_scr, other_ref[...].astype(F32).reshape(particles * cycles, angles))

        def cycle(r, carry):
            lanes = pl.ds(pl.multiple_of(r * angles, angles), angles)
            a = take_cycle(a_scr, r, particles, cycles).reshape(nb, per, angles)
            b = take_cycle(b_scr, r, particles, cycles).reshape(nb, per, angles)
            both = jnp.concatenate([a, b], axis=1).reshape(nb * 2 * per, angles)
            for s in range(N1):
                turned = pltpu.roll(both, step * s, 1) if s else both
                out_ref[:, s, :, lanes] = turned.astype(BF).reshape(nb, 2 * per, angles)
            return carry

        lax.fori_loop(0, cycles, cycle, 0)

    return pl.pallas_call(
        body,
        out_shape=jax.ShapeDtypeStruct((nb, N1, 2 * per, cycles * angles), BF),
        in_specs=[spec(), spec()],
        out_specs=spec(),
        scratch_shapes=[scratch(particles * cycles, angles)] * 2,
        compiler_params=params(),
        name="rotate_images",
    )(own, other)


def correlate(turned, refs, cycles, step):
    nb, n1, rows, depth = turned.shape
    angles = depth // cycles
    classes = refs.shape[0] * refs.shape[1] // cycles
    cols = N2 * classes

    def body(x_ref, r_ref, out_ref, scr, rr):
        fill(scr, r_ref[...].astype(F32).reshape(classes * cycles, angles))
        square = jnp.zeros((classes, angles), F32)
        for r in range(cycles):
            piece = take_cycle(scr, r, classes, cycles)
            square = square + piece * piece
            for s in range(N2):
                shift = (angles - step * s) % angles
                turned_ref = pltpu.roll(piece, shift, 1) if s else piece
                rr[s * classes : (s + 1) * classes, r * angles : (r + 1) * angles] = (
                    turned_ref.astype(BF)
                )
        half = 0.5 * jnp.sum(square, axis=1, keepdims=True)
        half = jnp.concatenate([half] * N2, axis=0)
        for j in range(0, nb, 2):
            x = x_ref[j : j + 2].reshape(2 * n1 * rows, depth)
            part = lax.dot_general(
                x, rr[...], (((1,), (1,)), ((), ())), preferred_element_type=F32
            )
            for i in range(2):
                piece = part[i * n1 * rows : (i + 1) * n1 * rows]
                out_ref[j + i] = (piece.T - half).astype(BF)

    return pl.pallas_call(
        body,
        out_shape=jax.ShapeDtypeStruct((nb, cols, n1 * rows), BF),
        in_specs=[spec(), spec()],
        out_specs=spec(),
        scratch_shapes=[scratch(classes * cycles, angles), VM((cols, depth), BF)],
        compiler_params=params(),
        name="correlate",
    )(turned, refs)


def local_softmax(me, scores, scale):
    nb, cols, lanes = scores.shape
    group = lanes // N1

    def across(op, row):
        width = group
        while width < lanes:
            row = op(row, pltpu.roll(row, width, 1))
            width *= 2
        return row

    def body(me_ref, x_ref, scale_ref, e_ref, stat_ref):
        total = x_ref[0].astype(F32)
        for i in range(1, nb):
            total = total + x_ref[i].astype(F32)
        logits = total * scale_ref[pl.ds(me_ref[0], 1), :]
        top = across(jnp.maximum, jnp.max(logits, axis=0, keepdims=True))
        e = jnp.exp(logits - top)
        e_ref[...] = e
        stat_ref[0:1, :] = top
        stat_ref[1:2, :] = across(jnp.add, jnp.sum(e, axis=0, keepdims=True))

    return pl.pallas_call(
        body,
        out_shape=(
            jax.ShapeDtypeStruct((cols, lanes), F32),
            jax.ShapeDtypeStruct((2, lanes), F32),
        ),
        in_specs=[spec(pltpu.SMEM), spec(), spec()],
        out_specs=(spec(), spec()),
        compiler_params=params(),
        name="local_softmax",
    )(me, scores, scale)


def normalize(e, mine, theirs, copies, half):
    cols, lanes = e.shape

    def body(e_ref, a_ref, b_ref, out_ref):
        b = pltpu.roll(b_ref[...], half, 1)
        top_a, sum_a = a_ref[0:1, :], a_ref[1:2, :]
        top_b, sum_b = b[0:1, :], b[1:2, :]
        top = jnp.maximum(top_a, top_b)
        part = jnp.exp(top_a - top)
        factor = part / (sum_a * part + sum_b * jnp.exp(top_b - top))
        w = (e_ref[...] * factor).astype(BF)
        for c in range(copies):
            out_ref[c] = w

    return pl.pallas_call(
        body,
        out_shape=jax.ShapeDtypeStruct((copies, cols, lanes), BF),
        in_specs=[spec(), spec(), spec()],
        out_specs=spec(),
        compiler_params=params(),
        name="normalize",
    )(e, mine, theirs)


def accumulate(weights, turned, cycles, owners, step):
    nb, cols, lanes = weights.shape
    depth = turned.shape[-1]
    angles = depth // cycles
    classes = cols // N2

    def body(w_ref, x_ref, out_ref, scr):
        w = jnp.concatenate([w_ref[j] for j in range(nb)], axis=1)

        def cycle(r, carry):
            x = x_ref[:, pl.ds(pl.multiple_of(r * angles, angles), angles)]
            spread = jnp.dot(w, x, preferred_element_type=F32)
            total = spread[0:classes]
            for s in range(1, N2):
                total = total + pltpu.roll(
                    spread[s * classes : (s + 1) * classes], step * s, 1
                )
            for h in range(angles // 128):
                piece = total[:, h * 128 : (h + 1) * 128]
                scr.at[h][pl.ds(r, classes, stride=cycles), :] = piece
            return carry

        lax.fori_loop(0, cycles, cycle, 0)
        whole = jnp.concatenate([scr[h] for h in range(angles // 128)], axis=1)
        out_ref[...] = whole.reshape(out_ref.shape).astype(BF)

    return pl.pallas_call(
        body,
        out_shape=jax.ShapeDtypeStruct((owners, classes // owners * cycles, angles), BF),
        in_specs=[spec(), spec()],
        out_specs=spec(),
        scratch_shapes=[scratch(classes * cycles, angles)],
        compiler_params=params(),
        name="accumulate",
    )(weights, turned.reshape(nb * lanes, depth))


def add_up(parts):
    def body(x_ref, out_ref):
        total = x_ref[0].astype(F32)
        for i in range(1, parts.shape[0]):
            total = total + x_ref[i].astype(F32)
        out_ref[...] = total

    return pl.pallas_call(
        body,
        out_shape=jax.ShapeDtypeStruct(parts.shape[1:], F32),
        in_specs=[spec()],
        out_specs=spec(),
        compiler_params=params(),
        name="add_up",
    )(parts)


def solution(mesh):
    dom, nb = mesh.devices.shape
    nd = dom // 2
    view = Mesh(mesh.devices.reshape(nd, 2, nb), ("dh", "core", "blk"))
    swap = [(0, 1), (1, 0)]

    def shards(images, ref_store, block_owner, class_gain, precision):
        particles, cycles, angles = images.shape
        kb = ref_store.shape[2]
        rot = angles // (N1 * N2)
        half = particles // nb
        other = lax.ppermute(images, "core", swap)
        other_precision = lax.ppermute(precision, "core", swap)
        me = (lax.axis_index("dh") * 2 + lax.axis_index("core"))[None].astype(jnp.int32)
        j = lax.axis_index("blk")[None].astype(jnp.int32)
        mine = pick_block(me, block_owner, class_gain, ref_store[0], nd)
        refs = lax.all_to_all(mine, "dh", 0, 0)
        turned = rotate_images(images, other, nb, rot)
        scores = correlate(turned, refs, cycles, rot * N1)
        scores = lax.all_to_all(scores, "blk", 0, 0)
        both = jnp.concatenate(
            [precision.reshape(nb, half), other_precision.reshape(nb, half)], axis=1
        )
        e, stats = local_softmax(j, scores, jnp.tile(both, (1, N1)))
        theirs = lax.ppermute(stats, "core", swap)
        weights = normalize(e, stats, theirs, nb, half)
        weights = lax.all_to_all(weights, "blk", 0, 0)
        totals = accumulate(weights, turned, cycles, nd, rot * N1)
        totals = lax.all_to_all(totals, "dh", 0, 0)
        return add_up(totals).reshape(1, 1, kb, cycles, angles)

    dom_axes = ("dh", "core")
    return jax.shard_map(
        shards,
        mesh=view,
        in_specs=(
            P(dom_axes, "blk", None),
            P(dom_axes, None, None, "blk", None),
            P(),
            P(),
            P(dom_axes),
        ),
        out_specs=P(dom_axes, None, None, "blk", None),
        check_vma=False,
    )
```

```python
import jax
import jax.numpy as jnp
from jax import lax
from jax.experimental import pallas as pl
from jax.experimental.pallas import tpu as pltpu
from jax.sharding import Mesh, PartitionSpec as P

BF = jnp.bfloat16
F32 = jnp.float32
VM = pltpu.VMEM
LANES = 128
N1 = 4
N2 = 8


def spec(space=VM):
    return pl.BlockSpec(memory_space=space)


def params(mib=24):
    return pltpu.CompilerParams(vmem_limit_bytes=mib * 1024 * 1024)


def here(x):
    return pltpu.with_memory_space_constraint(x, VM)


def away(x):
    return pltpu.with_memory_space_constraint(x, pltpu.HBM)


def fill(scr, value):
    for h in range(scr.shape[0]):
        scr[h] = value[:, h * LANES : (h + 1) * LANES]


def take_cycle(scr, r, rows, cycles):
    return [scr.at[h][pl.ds(r, rows, stride=cycles), :] for h in range(2)]


def narrow(x):
    wide = x * 65537.0
    return wide - (wide - x)


def narrow_sum(x):
    near = narrow(x)
    lane = lax.broadcasted_iota(jnp.int32, x.shape, 1)
    rest = jnp.sum(x - near, axis=1, keepdims=True)
    return jnp.where(lane == 0, near + rest, near)


def turn(plus, minus, t):
    t = t % (2 * LANES)
    if t == 0:
        return plus, minus
    if t >= LANES:
        return turn(plus, -minus, t - LANES)
    lane = lax.broadcasted_iota(jnp.int32, minus.shape, 1)
    minus = pltpu.roll(minus, t, 1)
    return pltpu.roll(plus, t, 1), jnp.where(lane < t, -minus, minus)


def pick_block(me, block_owner, class_gain, ref_store, copies):
    nblk, kb, cycles, angles = ref_store.shape

    def body(me_ref, owner_ref, gain_ref, store_ref, out_ref, buf, sem):
        block = jnp.int32(0)
        for b in range(nblk):
            block = jnp.where(owner_ref[b] == me_ref[0], jnp.int32(b), block)
        copy = pltpu.make_async_copy(store_ref.at[block], buf, sem)
        copy.start()
        copy.wait()
        for i in range(kb):
            piece = (buf[i].astype(F32) * gain_ref[block * kb + i]).astype(BF).astype(F32)
            a, b = piece[:, :LANES], piece[:, LANES:]
            piece = jnp.concatenate([narrow_sum(a + b), narrow(a - b)], axis=1).astype(BF)
            for c in range(copies):
                out_ref[c, i * cycles : (i + 1) * cycles, :] = piece

    return pl.pallas_call(
        body,
        out_shape=jax.ShapeDtypeStruct((copies, kb * cycles, angles), BF),
        in_specs=[spec(pltpu.SMEM), spec(pltpu.SMEM), spec(pltpu.SMEM), spec(pltpu.HBM)],
        out_specs=spec(),
        scratch_shapes=[VM((kb, cycles, angles), BF), pltpu.SemaphoreType.DMA],
        compiler_params=params(60),
        name="pick_block",
    )(me, block_owner, class_gain, away(ref_store))


def rotate_images(own, other, nb, step):
    particles, cycles, angles = own.shape
    per = particles // nb
    rows = N1 * 2 * per

    def body(own_ref, other_ref, out_ref, a_scr, b_scr):
        fill(a_scr, own_ref[...].astype(F32).reshape(per * cycles, angles))
        fill(b_scr, other_ref[...].astype(F32).reshape(per * cycles, angles))
        for r in range(cycles):
            a = take_cycle(a_scr, r, per, cycles)
            b = take_cycle(b_scr, r, per, cycles)
            plus = narrow(jnp.concatenate([a[0] + a[1], b[0] + b[1]], axis=0)).astype(BF)
            minus = narrow(jnp.concatenate([a[0] - a[1], b[0] - b[1]], axis=0)).astype(BF)
            for s in range(N1):
                p, m = turn(plus, minus, step * s)
                at = slice(s * 2 * per, (s + 1) * 2 * per)
                out_ref[0, r, at, :] = p
                out_ref[1, r, at, :] = m

    block = pl.BlockSpec((per, cycles, angles), lambda j: (j, 0, 0))
    return pl.pallas_call(
        body,
        grid=(nb,),
        out_shape=pltpu.HBM((2, cycles, nb * rows, LANES), BF),
        in_specs=[block, block],
        out_specs=pl.BlockSpec((2, cycles, rows, LANES), lambda j: (0, 0, j, 0)),
        scratch_shapes=[VM((2, per * cycles, LANES), F32)] * 2,
        compiler_params=params(),
        name="rotate_images",
    )(away(own), other)


def correlate(turned, refs, cycles, nb, step):
    total = turned.shape[2]
    rows = total // nb
    classes = refs.shape[0] * refs.shape[1] // cycles
    cols = N2 * classes
    angles = 2 * LANES

    def body(x_hbm, r_ref, out_ref, scr, rr, x, sems):
        copies = [pltpu.make_async_copy(x_hbm.at[i], x.at[i], sems.at[i]) for i in range(2)]
        for copy in copies:
            copy.start()
        fill(scr, r_ref[...].astype(F32).reshape(classes * cycles, angles))
        square = jnp.zeros((classes, LANES), F32)
        for r in range(cycles):
            plus, minus = take_cycle(scr, r, classes, cycles)
            square = square + 0.5 * (plus * plus + minus * minus)
            plus, minus = plus.astype(BF), minus.astype(BF)
            for s in range(N2):
                p, m = turn(plus, minus, angles - step * s)
                rr[0, r, s * classes : (s + 1) * classes, :] = p
                rr[1, r, s * classes : (s + 1) * classes, :] = m
        norm = jnp.broadcast_to(jnp.sum(square, axis=1, keepdims=True), (classes, cols))
        k = lax.broadcasted_iota(jnp.int32, (classes, cols), 0)
        lane = lax.broadcasted_iota(jnp.int32, (classes, cols), 1)
        norm = jnp.sum(jnp.where(lane % classes == k, norm, 0.0), axis=0, keepdims=True)
        for i in range(2):
            copies[i].wait()
            left = jnp.concatenate([x[i, r] for r in range(cycles)], axis=1)
            right = jnp.concatenate([rr[i, r] for r in range(cycles)], axis=1)
            part = lax.dot_general(
                left, right, (((1,), (1,)), ((), ())), preferred_element_type=F32
            )
            if i == 0:
                part = part - norm
            for t in range(cols // LANES):
                tile = part[:, t * LANES : (t + 1) * LANES].astype(BF)
                out_ref[:, t, i * rows : (i + 1) * rows, :] = tile.reshape(nb, rows, LANES)

    return pl.pallas_call(
        body,
        out_shape=jax.ShapeDtypeStruct((nb, cols // LANES, 2 * rows, LANES), BF),
        in_specs=[spec(pltpu.HBM), spec()],
        out_specs=spec(),
        scratch_shapes=[
            VM((2, classes * cycles, LANES), F32),
            VM((2, cycles, cols, LANES), BF),
            VM((2, cycles, total, LANES), BF),
            pltpu.SemaphoreType.DMA((2,)),
        ],
        compiler_params=params(),
        name="correlate",
    )(away(turned), here(refs))


def local_softmax(me, scores, precision, others):
    nb, tiles, rows, _ = scores.shape
    cols = tiles * LANES
    half = rows // 2
    group = half // N1
    own = group // 2

    def across(op, x):
        pieces = [x[i * group : (i + 1) * group] for i in range(N1)]
        return op(op(pieces[0], pieces[1]), op(pieces[2], pieces[3]))

    def body(me_ref, x_ref, a_ref, b_ref, e_ref, stat_ref):
        total = x_ref[0].astype(F32)
        for i in range(1, nb):
            total = total + x_ref[i].astype(F32)
        total = jnp.concatenate([total[t] for t in range(tiles)], axis=1)
        plus, minus = total[:half], total[half:]
        row = lax.broadcasted_iota(jnp.int32, (own, own), 0)
        col = lax.broadcasted_iota(jnp.int32, (own, own), 1)
        scale = [
            jnp.sum(jnp.where(row == col, ref[pl.ds(me_ref[0], 1), :], 0.0), axis=1, keepdims=True)
            for ref in (a_ref, b_ref)
        ]
        scale = jnp.concatenate(scale * N1, axis=0) * 0.5
        near, far = scale * (plus + minus), scale * (plus - minus)
        top = jnp.max(jnp.maximum(near, far), axis=1, keepdims=True)
        top = across(jnp.maximum, top)
        tops = jnp.concatenate([top] * N1, axis=0)
        near, far = jnp.exp(near - tops), jnp.exp(far - tops)
        e_ref[0] = near
        e_ref[1] = far
        amount = across(jnp.add, jnp.sum(near + far, axis=1, keepdims=True))
        stat_ref[0] = jnp.broadcast_to(top, (group, LANES))
        stat_ref[1] = jnp.broadcast_to(amount, (group, LANES))

    return pl.pallas_call(
        body,
        out_shape=(VM((2, half, cols), F32), VM((2, group, LANES), F32)),
        in_specs=[spec(pltpu.SMEM), spec(), spec(), spec()],
        out_specs=(spec(), spec()),
        compiler_params=params(),
        name="local_softmax",
    )(me, here(scores), here(precision), here(others))


def normalize(e, mine, theirs, copies):
    _, half, cols = e.shape
    group = mine.shape[1]

    def body(e_ref, a_ref, b_ref, out_ref):
        def flipped(x):
            return jnp.concatenate([x[group // 2 :], x[: group // 2]], axis=0)

        top_a, sum_a = a_ref[0], a_ref[1]
        top_b, sum_b = flipped(b_ref[0]), flipped(b_ref[1])
        top = jnp.maximum(top_a, top_b)
        part = jnp.exp(top_a - top)
        factor = part / (sum_a * part + sum_b * jnp.exp(top_b - top))
        factor = jnp.concatenate([jnp.concatenate([factor] * N1, axis=0)] * (cols // LANES), axis=1)
        near, far = e_ref[0] * factor, e_ref[1] * factor
        w = jnp.concatenate([near + far, near - far], axis=0).T.astype(BF)
        for c in range(copies):
            out_ref[c] = w

    return pl.pallas_call(
        body,
        out_shape=VM((copies, cols, 2 * half), BF),
        in_specs=[spec(), spec(), spec()],
        out_specs=spec(),
        compiler_params=params(),
        name="normalize",
    )(here(e), here(mine), here(theirs))


def accumulate(weights, turned, cycles, owners, step):
    nb, cols, lanes = weights.shape
    total = turned.shape[2]
    classes = cols // N2
    pair = 2 * LANES

    def body(w_ref, x_hbm, out_ref, scr, x, sems):
        copies = [pltpu.make_async_copy(x_hbm.at[i], x.at[i], sems.at[i]) for i in range(2)]
        for copy in copies:
            copy.start()
        left = lax.broadcasted_iota(jnp.int32, (cols, lanes), 1) < lanes // 2
        near, far = [], []
        for j in range(0, nb, 2):
            a, b = w_ref[j], w_ref[j + 1]
            near.append(jnp.where(left, a, pltpu.roll(b, lanes // 2, 1)))
            far.append(jnp.where(left, pltpu.roll(a, lanes // 2, 1), b))
        w = [jnp.concatenate(v, axis=1) for v in (near, far)]
        for copy in copies:
            copy.wait()
        for c in range(0, cycles, 2):
            spread = []
            for i in range(2):
                both = jnp.concatenate([x[i, c], x[i, c + 1]], axis=1)
                spread.append(jnp.dot(w[i], both, preferred_element_type=F32))
            for d in range(2):
                plus = minus = None
                for s in range(N2):
                    p, m = (
                        v[s * classes : (s + 1) * classes, d * LANES : (d + 1) * LANES]
                        for v in spread
                    )
                    p, m = turn(p, m, step * s)
                    plus = plus + p if s else p
                    minus = minus + m if s else m
                rows = pl.ds(c + d, classes, stride=cycles)
                scr.at[0][rows, :] = 0.5 * (plus + minus)
                scr.at[1][rows, :] = 0.5 * (plus - minus)
        whole = jnp.concatenate([scr[0], scr[1]], axis=1)
        out_ref[...] = whole.reshape(out_ref.shape).astype(BF)

    return pl.pallas_call(
        body,
        out_shape=VM((owners, classes // owners * cycles, pair), BF),
        in_specs=[spec(), spec(pltpu.HBM)],
        out_specs=spec(),
        scratch_shapes=[
            VM((2, classes * cycles, LANES), F32),
            VM((2, cycles, total, LANES), BF),
            pltpu.SemaphoreType.DMA((2,)),
        ],
        compiler_params=params(),
        name="accumulate",
    )(here(weights), away(turned))


def add_up(parts):
    def body(x_ref, out_ref):
        total = x_ref[0].astype(F32)
        for i in range(1, parts.shape[0]):
            total = total + x_ref[i].astype(F32)
        out_ref[...] = total

    return pl.pallas_call(
        body,
        out_shape=jax.ShapeDtypeStruct(parts.shape[1:], F32),
        in_specs=[spec()],
        out_specs=spec(),
        compiler_params=params(),
        name="add_up",
    )(here(parts))


def solution(mesh):
    dom, nb = mesh.devices.shape
    nd = dom // 2
    view = Mesh(mesh.devices.reshape(nd, 2, nb), ("dh", "core", "blk"))
    swap = [(0, 1), (1, 0)]

    def shards(images, ref_store, block_owner, class_gain, precision):
        particles, cycles, angles = images.shape
        kb = ref_store.shape[2]
        rot = angles // (2 * N1 * N2)
        half = particles // nb
        other = lax.ppermute(images, "core", swap)
        other_precision = lax.ppermute(precision, "core", swap)
        me = (lax.axis_index("dh") * 2 + lax.axis_index("core"))[None].astype(jnp.int32)
        j = lax.axis_index("blk")[None].astype(jnp.int32)
        mine = pick_block(me, block_owner, class_gain, ref_store[0], nd)
        refs = lax.all_to_all(mine, "dh", 0, 0)
        turned = rotate_images(images, other, nb, rot)
        scores = correlate(turned, refs, cycles, nb, rot * N1)
        scores = lax.all_to_all(scores, "blk", 0, 0)
        e, stats = local_softmax(
            j, scores, precision.reshape(nb, half), other_precision.reshape(nb, half)
        )
        theirs = lax.ppermute(stats, "core", swap)
        weights = normalize(e, stats, theirs, nb)
        weights = lax.all_to_all(weights, "blk", 0, 0)
        totals = accumulate(weights, turned, cycles, nd, rot * N1)
        totals = lax.all_to_all(totals, "dh", 0, 0)
        return add_up(totals).reshape(1, 1, kb, cycles, angles)

    dom_axes = ("dh", "core")
    return jax.shard_map(
        shards,
        mesh=view,
        in_specs=(
            P(dom_axes, "blk", None),
            P(dom_axes, None, None, "blk", None),
            P(),
            P(),
            P(dom_axes),
        ),
        out_specs=P(dom_axes, None, None, "blk", None),
        check_vma=False,
    )
```

```python
import jax
import jax.numpy as jnp
from jax import lax
from jax.experimental import pallas as pl
from jax.experimental.pallas import tpu as pltpu
from jax.sharding import Mesh, PartitionSpec as P

BF = jnp.bfloat16
F32 = jnp.float32
VM = pltpu.VMEM
LANES = 128
N1 = 4
N2 = 8


def spec(space=VM):
    return pl.BlockSpec(memory_space=space)


def params(mib=24):
    return pltpu.CompilerParams(vmem_limit_bytes=mib * 1024 * 1024)


def here(x):
    return pltpu.with_memory_space_constraint(x, VM)


def away(x):
    return pltpu.with_memory_space_constraint(x, pltpu.HBM)


def fill(scr, value):
    for h in range(scr.shape[0]):
        scr[h] = value[:, h * LANES : (h + 1) * LANES]


def take_cycle(scr, r, rows, cycles):
    return [scr.at[h][pl.ds(r, rows, stride=cycles), :] for h in range(2)]


def narrow(x):
    wide = x * 65537.0
    return wide - (wide - x)


def narrow_sum(x):
    near = narrow(x)
    lane = lax.broadcasted_iota(jnp.int32, x.shape, 1)
    rest = jnp.sum(x - near, axis=1, keepdims=True)
    return jnp.where(lane == 0, near + rest, near)


def turn(plus, minus, t):
    t = t % (2 * LANES)
    if t == 0:
        return plus, minus
    if t >= LANES:
        return turn(plus, -minus, t - LANES)
    lane = lax.broadcasted_iota(jnp.int32, minus.shape, 1)
    minus = pltpu.roll(minus, t, 1)
    return pltpu.roll(plus, t, 1), jnp.where(lane < t, -minus, minus)


def pick_block(me, block_owner, class_gain, ref_store, copies):
    nblk, kb, cycles, angles = ref_store.shape

    def body(me_ref, owner_ref, gain_ref, store_ref, out_ref, buf, sem):
        block = jnp.int32(0)
        for b in range(nblk):
            block = jnp.where(owner_ref[b] == me_ref[0], jnp.int32(b), block)
        copy = pltpu.make_async_copy(store_ref.at[block], buf, sem)
        copy.start()
        copy.wait()
        for i in range(kb):
            piece = (buf[i].astype(F32) * gain_ref[block * kb + i]).astype(BF).astype(F32)
            a, b = piece[:, :LANES], piece[:, LANES:]
            piece = jnp.concatenate([narrow_sum(a + b), narrow(a - b)], axis=1).astype(BF)
            for c in range(copies):
                out_ref[c, i * cycles : (i + 1) * cycles, :] = piece

    return pl.pallas_call(
        body,
        out_shape=jax.ShapeDtypeStruct((copies, kb * cycles, angles), BF),
        in_specs=[spec(pltpu.SMEM), spec(pltpu.SMEM), spec(pltpu.SMEM), spec(pltpu.HBM)],
        out_specs=spec(),
        scratch_shapes=[VM((kb, cycles, angles), BF), pltpu.SemaphoreType.DMA],
        compiler_params=params(60),
        name="pick_block",
    )(me, block_owner, class_gain, away(ref_store))


def halve_images(own, other, nb):
    particles, cycles, angles = own.shape
    per = particles // nb

    def body(own_ref, other_ref, out_ref, a_scr, b_scr):
        fill(a_scr, own_ref[...].astype(F32).reshape(particles * cycles, angles))
        fill(b_scr, other_ref[...].astype(F32).reshape(particles * cycles, angles))
        for r in range(cycles):
            a = take_cycle(a_scr, r, particles, cycles)
            b = take_cycle(b_scr, r, particles, cycles)
            for i, op in enumerate((jnp.add, jnp.subtract)):
                x, y = op(a[0], a[1]), op(b[0], b[1])
                both = [v.reshape(nb, per, LANES) for v in (x, y)]
                both = jnp.concatenate(both, axis=1).reshape(2 * particles, LANES)
                out_ref[i, r] = narrow(both).astype(BF)

    return pl.pallas_call(
        body,
        out_shape=VM((2, cycles, 2 * particles, LANES), BF),
        in_specs=[spec(), spec()],
        out_specs=spec(),
        scratch_shapes=[VM((2, particles * cycles, LANES), F32)] * 2,
        compiler_params=params(),
        name="halve_images",
    )(own, here(other))


def rotate_images(x_ref, r, nb, step):
    plus, minus = x_ref[0, r], x_ref[1, r]
    per = plus.shape[0] // nb
    turned = [turn(plus, minus, step * s) for s in range(N1)]
    return [
        jnp.concatenate(
            [t[i][j * per : (j + 1) * per] for j in range(nb) for t in turned], axis=0
        )
        for i in range(2)
    ]


def correlate(images, refs, nb, step):
    _, cycles, particles, _ = images.shape
    total = N1 * particles
    rows = total // nb
    classes = refs.shape[0] * refs.shape[1] // cycles
    cols = N2 * classes
    angles = 2 * LANES

    def body(x_ref, r_ref, out_ref, scr, rr, x):
        fill(scr, r_ref[...].astype(F32).reshape(classes * cycles, angles))
        square = jnp.zeros((classes, LANES), F32)
        for r in range(cycles):
            plus, minus = take_cycle(scr, r, classes, cycles)
            square = square + 0.5 * (plus * plus + minus * minus)
            plus, minus = plus.astype(BF), minus.astype(BF)
            x[0, r], x[1, r] = rotate_images(x_ref, r, nb, step)
            for s in range(N2):
                p, m = turn(plus, minus, angles - step * N1 * s)
                rr[0, r, s * classes : (s + 1) * classes, :] = p
                rr[1, r, s * classes : (s + 1) * classes, :] = m
        norm = jnp.broadcast_to(jnp.sum(square, axis=1, keepdims=True), (classes, cols))
        k = lax.broadcasted_iota(jnp.int32, (classes, cols), 0)
        lane = lax.broadcasted_iota(jnp.int32, (classes, cols), 1)
        norm = jnp.sum(jnp.where(lane % classes == k, norm, 0.0), axis=0, keepdims=True)
        for i in range(2):
            left = jnp.concatenate([x[i, r] for r in range(cycles)], axis=1)
            right = jnp.concatenate([rr[i, r] for r in range(cycles)], axis=1)
            part = lax.dot_general(
                left, right, (((1,), (1,)), ((), ())), preferred_element_type=F32
            )
            if i == 0:
                part = part - norm
            for t in range(cols // LANES):
                tile = part[:, t * LANES : (t + 1) * LANES].astype(BF)
                out_ref[:, t, i * rows : (i + 1) * rows, :] = tile.reshape(nb, rows, LANES)

    return pl.pallas_call(
        body,
        out_shape=jax.ShapeDtypeStruct((nb, cols // LANES, 2 * rows, LANES), BF),
        in_specs=[spec(), spec()],
        out_specs=spec(),
        scratch_shapes=[
            VM((2, classes * cycles, LANES), F32),
            VM((2, cycles, cols, LANES), BF),
            VM((2, cycles, total, LANES), BF),
        ],
        compiler_params=params(),
        name="correlate",
    )(here(images), here(refs))


def local_softmax(me, scores, precision, others):
    nb, tiles, rows, _ = scores.shape
    cols = tiles * LANES
    half = rows // 2
    group = half // N1
    own = group // 2

    def across(op, x):
        pieces = [x[i * group : (i + 1) * group] for i in range(N1)]
        return op(op(pieces[0], pieces[1]), op(pieces[2], pieces[3]))

    def body(me_ref, x_ref, a_ref, b_ref, e_ref, stat_ref):
        total = x_ref[0].astype(F32)
        for i in range(1, nb):
            total = total + x_ref[i].astype(F32)
        total = jnp.concatenate([total[t] for t in range(tiles)], axis=1)
        plus, minus = total[:half], total[half:]
        row = lax.broadcasted_iota(jnp.int32, (own, own), 0)
        col = lax.broadcasted_iota(jnp.int32, (own, own), 1)
        scale = [
            jnp.sum(jnp.where(row == col, ref[pl.ds(me_ref[0], 1), :], 0.0), axis=1, keepdims=True)
            for ref in (a_ref, b_ref)
        ]
        scale = jnp.concatenate(scale * N1, axis=0) * 0.5
        near, far = scale * (plus + minus), scale * (plus - minus)
        top = jnp.max(jnp.maximum(near, far), axis=1, keepdims=True)
        top = across(jnp.maximum, top)
        tops = jnp.concatenate([top] * N1, axis=0)
        near, far = jnp.exp(near - tops), jnp.exp(far - tops)
        e_ref[0] = near
        e_ref[1] = far
        amount = across(jnp.add, jnp.sum(near + far, axis=1, keepdims=True))
        stat_ref[0] = jnp.broadcast_to(top, (group, LANES))
        stat_ref[1] = jnp.broadcast_to(amount, (group, LANES))

    return pl.pallas_call(
        body,
        out_shape=(VM((2, half, cols), F32), VM((2, group, LANES), F32)),
        in_specs=[spec(pltpu.SMEM), spec(), spec(), spec()],
        out_specs=(spec(), spec()),
        compiler_params=params(),
        name="local_softmax",
    )(me, here(scores), here(precision), here(others))


def normalize(e, mine, theirs, copies):
    _, half, cols = e.shape
    group = mine.shape[1]

    def body(e_ref, a_ref, b_ref, out_ref):
        def flipped(x):
            return jnp.concatenate([x[group // 2 :], x[: group // 2]], axis=0)

        top_a, sum_a = a_ref[0], a_ref[1]
        top_b, sum_b = flipped(b_ref[0]), flipped(b_ref[1])
        top = jnp.maximum(top_a, top_b)
        part = jnp.exp(top_a - top)
        factor = part / (sum_a * part + sum_b * jnp.exp(top_b - top))
        factor = jnp.concatenate([jnp.concatenate([factor] * N1, axis=0)] * (cols // LANES), axis=1)
        near, far = e_ref[0] * factor, e_ref[1] * factor
        w = jnp.concatenate([near + far, near - far], axis=0).T.astype(BF)
        for c in range(copies):
            out_ref[c] = w

    return pl.pallas_call(
        body,
        out_shape=VM((copies, cols, 2 * half), BF),
        in_specs=[spec(), spec(), spec()],
        out_specs=spec(),
        compiler_params=params(),
        name="normalize",
    )(here(e), here(mine), here(theirs))


def accumulate(weights, images, owners, step):
    nb, cols, lanes = weights.shape
    cycles = images.shape[1]
    classes = cols // N2
    pair = 2 * LANES

    def body(w_ref, x_ref, out_ref, scr):
        left = lax.broadcasted_iota(jnp.int32, (cols, lanes), 1) < lanes // 2
        near, far = [], []
        for j in range(0, nb, 2):
            a, b = w_ref[j], w_ref[j + 1]
            near.append(jnp.where(left, a, pltpu.roll(b, lanes // 2, 1)))
            far.append(jnp.where(left, pltpu.roll(a, lanes // 2, 1), b))
        w = [jnp.concatenate(v, axis=1) for v in (near, far)]
        for c in range(0, cycles, 2):
            turned = [rotate_images(x_ref, c + d, nb, step) for d in range(2)]
            spread = []
            for i in range(2):
                both = jnp.concatenate([turned[0][i], turned[1][i]], axis=1)
                spread.append(jnp.dot(w[i], both, preferred_element_type=F32))
            for d in range(2):
                plus = minus = None
                for s in range(N2):
                    p, m = (
                        v[s * classes : (s + 1) * classes, d * LANES : (d + 1) * LANES]
                        for v in spread
                    )
                    p, m = turn(p, m, step * N1 * s)
                    plus = plus + p if s else p
                    minus = minus + m if s else m
                rows = pl.ds(c + d, classes, stride=cycles)
                scr.at[0][rows, :] = 0.5 * (plus + minus)
                scr.at[1][rows, :] = 0.5 * (plus - minus)
        whole = jnp.concatenate([scr[0], scr[1]], axis=1)
        out_ref[...] = whole.reshape(out_ref.shape).astype(BF)

    return pl.pallas_call(
        body,
        out_shape=VM((owners, classes // owners * cycles, pair), BF),
        in_specs=[spec(), spec()],
        out_specs=spec(),
        scratch_shapes=[VM((2, classes * cycles, LANES), F32)],
        compiler_params=params(),
        name="accumulate",
    )(here(weights), here(images))


def add_up(parts):
    def body(x_ref, out_ref):
        total = x_ref[0].astype(F32)
        for i in range(1, parts.shape[0]):
            total = total + x_ref[i].astype(F32)
        out_ref[...] = total

    return pl.pallas_call(
        body,
        out_shape=jax.ShapeDtypeStruct(parts.shape[1:], F32),
        in_specs=[spec()],
        out_specs=spec(),
        compiler_params=params(),
        name="add_up",
    )(here(parts))


def solution(mesh):
    dom, nb = mesh.devices.shape
    nd = dom // 2
    view = Mesh(mesh.devices.reshape(nd, 2, nb), ("dh", "core", "blk"))
    swap = [(0, 1), (1, 0)]

    def shards(images, ref_store, block_owner, class_gain, precision):
        particles, cycles, angles = images.shape
        kb = ref_store.shape[2]
        rot = angles // (2 * N1 * N2)
        half = particles // nb
        other = lax.ppermute(images, "core", swap)
        other_precision = lax.ppermute(precision, "core", swap)
        me = (lax.axis_index("dh") * 2 + lax.axis_index("core"))[None].astype(jnp.int32)
        j = lax.axis_index("blk")[None].astype(jnp.int32)
        mine = pick_block(me, block_owner, class_gain, ref_store[0], nd)
        refs = lax.all_to_all(mine, "dh", 0, 0)
        halves = halve_images(images, other, nb)
        scores = correlate(halves, refs, nb, rot)
        scores = lax.all_to_all(scores, "blk", 0, 0)
        e, stats = local_softmax(
            j, scores, precision.reshape(nb, half), other_precision.reshape(nb, half)
        )
        theirs = lax.ppermute(stats, "core", swap)
        weights = normalize(e, stats, theirs, nb)
        weights = lax.all_to_all(weights, "blk", 0, 0)
        totals = accumulate(weights, halves, nd, rot)
        totals = lax.all_to_all(totals, "dh", 0, 0)
        return add_up(totals).reshape(1, 1, kb, cycles, angles)

    dom_axes = ("dh", "core")
    return jax.shard_map(
        shards,
        mesh=view,
        in_specs=(
            P(dom_axes, "blk", None),
            P(dom_axes, None, None, "blk", None),
            P(),
            P(),
            P(dom_axes),
        ),
        out_specs=P(dom_axes, None, None, "blk", None),
        check_vma=False,
    )
```

```python
import jax
import jax.numpy as jnp
from jax import lax
from jax.experimental import pallas as pl
from jax.experimental.pallas import tpu as pltpu
from jax.sharding import Mesh, PartitionSpec as P

BF = jnp.bfloat16
F32 = jnp.float32
VM = pltpu.VMEM
LANES = 128
N1 = 4
N2 = 8


def spec(space=VM):
    return pl.BlockSpec(memory_space=space)


def params(mib=24):
    return pltpu.CompilerParams(vmem_limit_bytes=mib * 1024 * 1024)


def here(x):
    return pltpu.with_memory_space_constraint(x, VM)


def away(x):
    return pltpu.with_memory_space_constraint(x, pltpu.HBM)


def fill(scr, value):
    for h in range(scr.shape[0]):
        scr[h] = value[:, h * LANES : (h + 1) * LANES]


def take_cycle(scr, r, rows, cycles):
    return [scr.at[h][pl.ds(r, rows, stride=cycles), :] for h in range(2)]


def narrow(x):
    wide = x * 65537.0
    return wide - (wide - x)


def narrow_sum(x):
    near = narrow(x)
    lane = lax.broadcasted_iota(jnp.int32, x.shape, 1)
    rest = jnp.sum(x - near, axis=1, keepdims=True)
    return jnp.where(lane == 0, near + rest, near)


def turn(plus, minus, t):
    t = t % (2 * LANES)
    if t == 0:
        return plus, minus
    if t >= LANES:
        return turn(plus, -minus, t - LANES)
    lane = lax.broadcasted_iota(jnp.int32, minus.shape, 1)
    minus = pltpu.roll(minus, t, 1)
    return pltpu.roll(plus, t, 1), jnp.where(lane < t, -minus, minus)


def pick_block(me, block_owner, class_gain, ref_store):
    nblk, kb, cycles, angles = ref_store.shape

    def body(me_ref, owner_ref, gain_ref, store_ref, out_ref, buf, sem):
        block = jnp.int32(0)
        for b in range(nblk):
            block = jnp.where(owner_ref[b] == me_ref[0], jnp.int32(b), block)
        copy = pltpu.make_async_copy(store_ref.at[block], buf, sem)
        copy.start()
        copy.wait()
        for i in range(kb):
            piece = (buf[i].astype(F32) * gain_ref[block * kb + i]).astype(BF).astype(F32)
            a, b = piece[:, :LANES], piece[:, LANES:]
            piece = jnp.concatenate([narrow_sum(a + b), narrow(a - b)], axis=1).astype(BF)
            out_ref[i * cycles : (i + 1) * cycles, :] = piece

    return pl.pallas_call(
        body,
        out_shape=VM((kb * cycles, angles), BF),
        in_specs=[spec(pltpu.SMEM), spec(pltpu.SMEM), spec(pltpu.SMEM), spec(pltpu.HBM)],
        out_specs=spec(),
        scratch_shapes=[VM((kb, cycles, angles), BF), pltpu.SemaphoreType.DMA],
        compiler_params=params(60),
        name="pick_block",
    )(me, block_owner, class_gain, away(ref_store))


def halve_images(own, other, nb):
    particles, cycles, angles = own.shape
    per = particles // nb

    def body(own_ref, other_ref, out_ref, a_scr, b_scr):
        fill(a_scr, own_ref[...].astype(F32).reshape(particles * cycles, angles))
        fill(b_scr, other_ref[...].astype(F32).reshape(particles * cycles, angles))
        for r in range(cycles):
            a = take_cycle(a_scr, r, particles, cycles)
            b = take_cycle(b_scr, r, particles, cycles)
            for i, op in enumerate((jnp.add, jnp.subtract)):
                x, y = op(a[0], a[1]), op(b[0], b[1])
                both = [v.reshape(nb, per, LANES) for v in (x, y)]
                both = jnp.concatenate(both, axis=1).reshape(2 * particles, LANES)
                out_ref[i, r] = narrow(both).astype(BF)

    return pl.pallas_call(
        body,
        out_shape=VM((2, cycles, 2 * particles, LANES), BF),
        in_specs=[spec(), spec()],
        out_specs=spec(),
        scratch_shapes=[VM((2, particles * cycles, LANES), F32)] * 2,
        compiler_params=params(),
        name="halve_images",
    )(own, here(other))


def rotate_images(x_ref, r, nb, step):
    plus, minus = x_ref[0, r], x_ref[1, r]
    per = plus.shape[0] // nb
    turned = [turn(plus, minus, step * s) for s in range(N1)]
    return [
        jnp.concatenate(
            [t[i][j * per : (j + 1) * per] for j in range(nb) for t in turned], axis=0
        )
        for i in range(2)
    ]


def correlate(images, refs, nb, step):
    _, cycles, particles, _ = images.shape
    total = N1 * particles
    rows = total // nb
    near, far = refs[0].shape[:2]
    classes = len(refs) * near * far // cycles
    cols = N2 * classes
    angles = 2 * LANES

    def body(x_ref, *args):
        r_refs, (out_ref, scr, rr, x) = args[: len(refs)], args[len(refs) :]
        blocks = [r_ref[d].astype(F32) for r_ref in r_refs for d in range(near)]
        fill(scr, jnp.concatenate(blocks, axis=0))
        square = jnp.zeros((classes, LANES), F32)
        for r in range(cycles):
            plus, minus = take_cycle(scr, r, classes, cycles)
            square = square + 0.5 * (plus * plus + minus * minus)
            plus, minus = plus.astype(BF), minus.astype(BF)
            x[0, r], x[1, r] = rotate_images(x_ref, r, nb, step)
            for s in range(N2):
                p, m = turn(plus, minus, angles - step * N1 * s)
                rr[0, r, s * classes : (s + 1) * classes, :] = p
                rr[1, r, s * classes : (s + 1) * classes, :] = m
        norm = jnp.broadcast_to(jnp.sum(square, axis=1, keepdims=True), (classes, cols))
        k = lax.broadcasted_iota(jnp.int32, (classes, cols), 0)
        lane = lax.broadcasted_iota(jnp.int32, (classes, cols), 1)
        norm = jnp.sum(jnp.where(lane % classes == k, norm, 0.0), axis=0, keepdims=True)
        for i in range(2):
            left = jnp.concatenate([x[i, r] for r in range(cycles)], axis=1)
            right = jnp.concatenate([rr[i, r] for r in range(cycles)], axis=1)
            part = lax.dot_general(
                left, right, (((1,), (1,)), ((), ())), preferred_element_type=F32
            )
            if i == 0:
                part = part - norm
            for t in range(cols // LANES):
                tile = part[:, t * LANES : (t + 1) * LANES].astype(BF)
                out_ref[:, t, i * rows : (i + 1) * rows, :] = tile.reshape(nb, rows, LANES)

    return pl.pallas_call(
        body,
        out_shape=jax.ShapeDtypeStruct((nb, cols // LANES, 2 * rows, LANES), BF),
        in_specs=[spec()] * (1 + len(refs)),
        out_specs=spec(),
        scratch_shapes=[
            VM((2, classes * cycles, LANES), F32),
            VM((2, cycles, cols, LANES), BF),
            VM((2, cycles, total, LANES), BF),
        ],
        compiler_params=params(),
        name="correlate",
    )(here(images), *[here(r) for r in refs])


def local_softmax(me, scores, precision, others):
    nb, tiles, rows, _ = scores.shape
    cols = tiles * LANES
    half = rows // 2
    group = half // N1
    own = group // 2

    def across(op, x):
        pieces = [x[i * group : (i + 1) * group] for i in range(N1)]
        return op(op(pieces[0], pieces[1]), op(pieces[2], pieces[3]))

    def body(me_ref, x_ref, a_ref, b_ref, e_ref, stat_ref):
        total = x_ref[0].astype(F32)
        for i in range(1, nb):
            total = total + x_ref[i].astype(F32)
        total = jnp.concatenate([total[t] for t in range(tiles)], axis=1)
        plus, minus = total[:half], total[half:]
        row = lax.broadcasted_iota(jnp.int32, (own, own), 0)
        col = lax.broadcasted_iota(jnp.int32, (own, own), 1)
        scale = [
            jnp.sum(jnp.where(row == col, ref[pl.ds(me_ref[0], 1), :], 0.0), axis=1, keepdims=True)
            for ref in (a_ref, b_ref)
        ]
        scale = jnp.concatenate(scale * N1, axis=0) * 0.5
        near, far = scale * (plus + minus), scale * (plus - minus)
        top = jnp.max(jnp.maximum(near, far), axis=1, keepdims=True)
        top = across(jnp.maximum, top)
        tops = jnp.concatenate([top] * N1, axis=0)
        near, far = jnp.exp(near - tops), jnp.exp(far - tops)
        e_ref[0] = near
        e_ref[1] = far
        amount = across(jnp.add, jnp.sum(near + far, axis=1, keepdims=True))
        stat_ref[0] = jnp.broadcast_to(top, (group, LANES))
        stat_ref[1] = jnp.broadcast_to(amount, (group, LANES))

    return pl.pallas_call(
        body,
        out_shape=(VM((2, half, cols), F32), VM((2, group, LANES), F32)),
        in_specs=[spec(pltpu.SMEM), spec(), spec(), spec()],
        out_specs=(spec(), spec()),
        compiler_params=params(),
        name="local_softmax",
    )(me, here(scores), here(precision), here(others))


def normalize(e, mine, theirs, copies):
    _, half, cols = e.shape
    group = mine.shape[1]

    def body(e_ref, a_ref, b_ref, out_ref):
        def flipped(x):
            return jnp.concatenate([x[group // 2 :], x[: group // 2]], axis=0)

        top_a, sum_a = a_ref[0], a_ref[1]
        top_b, sum_b = flipped(b_ref[0]), flipped(b_ref[1])
        top = jnp.maximum(top_a, top_b)
        part = jnp.exp(top_a - top)
        factor = part / (sum_a * part + sum_b * jnp.exp(top_b - top))
        factor = jnp.concatenate([jnp.concatenate([factor] * N1, axis=0)] * (cols // LANES), axis=1)
        near, far = e_ref[0] * factor, e_ref[1] * factor
        w = jnp.concatenate([near + far, near - far], axis=0).T.astype(BF)
        for c in range(copies):
            out_ref[c] = w

    return pl.pallas_call(
        body,
        out_shape=VM((copies, cols, 2 * half), BF),
        in_specs=[spec(), spec(), spec()],
        out_specs=spec(),
        compiler_params=params(),
        name="normalize",
    )(here(e), here(mine), here(theirs))


def accumulate(me, weights, images, ny, nz, step):
    owners = ny * nz
    nb, cols, lanes = weights.shape
    cycles = images.shape[1]
    classes = cols // N2
    pair = 2 * LANES

    def body(me_ref, w_ref, x_ref, out_ref, scr):
        left = lax.broadcasted_iota(jnp.int32, (cols, lanes), 1) < lanes // 2
        near, far = [], []
        for j in range(0, nb, 2):
            a, b = w_ref[j], w_ref[j + 1]
            near.append(jnp.where(left, a, pltpu.roll(b, lanes // 2, 1)))
            far.append(jnp.where(left, pltpu.roll(a, lanes // 2, 1), b))
        w = [jnp.concatenate(v, axis=1) for v in (near, far)]
        for c in range(0, cycles, 2):
            turned = [rotate_images(x_ref, c + d, nb, step) for d in range(2)]
            spread = []
            for i in range(2):
                both = jnp.concatenate([turned[0][i], turned[1][i]], axis=1)
                spread.append(jnp.dot(w[i], both, preferred_element_type=F32))
            for d in range(2):
                plus = minus = None
                for s in range(N2):
                    p, m = (
                        v[s * classes : (s + 1) * classes, d * LANES : (d + 1) * LANES]
                        for v in spread
                    )
                    p, m = turn(p, m, step * N1 * s)
                    plus = plus + p if s else p
                    minus = minus + m if s else m
                rows = pl.ds(c + d, classes, stride=cycles)
                scr.at[0][rows, :] = 0.5 * (plus + minus)
                scr.at[1][rows, :] = 0.5 * (plus - minus)
        whole = jnp.concatenate([scr[0], scr[1]], axis=1)
        whole = whole.reshape(out_ref.shape).astype(BF)
        place = me_ref[0] // 2
        y, z = place // nz, place % nz
        for slot in range(owners):
            dz, dy = slot // ny, slot % ny
            out_ref[(y + dy) % ny * nz + (z + nz - dz) % nz] = whole[slot]

    return pl.pallas_call(
        body,
        out_shape=VM((owners, classes // owners * cycles, pair), BF),
        in_specs=[spec(pltpu.SMEM), spec(), spec()],
        out_specs=spec(),
        scratch_shapes=[VM((2, classes * cycles, LANES), F32)],
        compiler_params=params(),
        name="accumulate",
    )(me, here(weights), here(images))


def add_up(parts):
    def body(x_ref, out_ref):
        total = x_ref[0].astype(F32)
        for i in range(1, parts.shape[0]):
            total = total + x_ref[i].astype(F32)
        out_ref[...] = total

    return pl.pallas_call(
        body,
        out_shape=jax.ShapeDtypeStruct(parts.shape[1:], F32),
        in_specs=[spec()],
        out_specs=spec(),
        compiler_params=params(),
        name="add_up",
    )(here(parts))


def solution(mesh):
    dom, nb = mesh.devices.shape
    ny, nz = 2, dom // 4
    view = Mesh(mesh.devices.reshape(ny, nz, 2, nb), ("yh", "z", "core", "blk"))
    swap = [(0, 1), (1, 0)]

    def shards(images, ref_store, block_owner, class_gain, precision):
        particles, cycles, angles = images.shape
        kb = ref_store.shape[2]
        rot = angles // (2 * N1 * N2)
        half = particles // nb
        other = lax.ppermute(images, "core", swap)
        other_precision = lax.ppermute(precision, "core", swap)
        y, z = lax.axis_index("yh"), lax.axis_index("z")
        me = ((y * nz + z) * 2 + lax.axis_index("core"))[None].astype(jnp.int32)
        j = lax.axis_index("blk")[None].astype(jnp.int32)
        mine = pick_block(me, block_owner, class_gain, ref_store[0])
        refs = [jnp.stack([mine, lax.ppermute(mine, "yh", swap)])]
        for d in range(1, nz):
            ring = [(i, (i + d) % nz) for i in range(nz)]
            refs.append(lax.ppermute(refs[0], "z", ring))
        halves = halve_images(images, other, nb)
        scores = correlate(halves, refs, nb, rot)
        scores = lax.all_to_all(scores, "blk", 0, 0)
        e, stats = local_softmax(
            j, scores, precision.reshape(nb, half), other_precision.reshape(nb, half)
        )
        theirs = lax.ppermute(stats, "core", swap)
        weights = normalize(e, stats, theirs, nb)
        weights = lax.all_to_all(weights, "blk", 0, 0)
        totals = accumulate(me, weights, halves, ny, nz, rot)
        totals = lax.all_to_all(totals, ("yh", "z"), 0, 0)
        return add_up(totals).reshape(1, 1, kb, cycles, angles)

    dom_axes = ("yh", "z", "core")
    return jax.shard_map(
        shards,
        mesh=view,
        in_specs=(
            P(dom_axes, "blk", None),
            P(dom_axes, None, None, "blk", None),
            P(),
            P(),
            P(dom_axes),
        ),
        out_specs=P(dom_axes, None, None, "blk", None),
        check_vma=False,
    )
```

```python
import jax
import jax.numpy as jnp
from jax import lax
from jax.experimental import pallas as pl
from jax.experimental.pallas import tpu as pltpu
from jax.sharding import Mesh, PartitionSpec as P

BF = jnp.bfloat16
F32 = jnp.float32
VM = pltpu.VMEM
LANES = 128
N1 = 4
N2 = 8


def spec(space=VM):
    return pl.BlockSpec(memory_space=space)


def params(mib=24):
    return pltpu.CompilerParams(vmem_limit_bytes=mib * 1024 * 1024)


def here(x):
    return pltpu.with_memory_space_constraint(x, VM)


def away(x):
    return pltpu.with_memory_space_constraint(x, pltpu.HBM)


def fill(scr, value):
    for h in range(scr.shape[0]):
        scr[h] = value[:, h * LANES : (h + 1) * LANES]


def take_cycle(scr, r, rows, cycles):
    return [scr.at[h][pl.ds(r, rows, stride=cycles), :] for h in range(2)]


def narrow(x):
    wide = x * 65537.0
    return wide - (wide - x)


def narrow_sum(x):
    near = narrow(x)
    lane = lax.broadcasted_iota(jnp.int32, x.shape, 1)
    rest = jnp.sum(x - near, axis=1, keepdims=True)
    return jnp.where(lane == 0, near + rest, near)


def turn(plus, minus, t):
    t = t % (2 * LANES)
    if t == 0:
        return plus, minus
    if t >= LANES:
        return turn(plus, -minus, t - LANES)
    lane = lax.broadcasted_iota(jnp.int32, minus.shape, 1)
    minus = pltpu.roll(minus, t, 1)
    return pltpu.roll(plus, t, 1), jnp.where(lane < t, -minus, minus)


def pick_block(me, block_owner, class_gain, ref_store):
    nblk, kb, cycles, angles = ref_store.shape

    def body(me_ref, owner_ref, gain_ref, store_ref, out_ref, buf, sem):
        block = jnp.int32(0)
        for b in range(nblk):
            block = jnp.where(owner_ref[b] == me_ref[0], jnp.int32(b), block)
        copy = pltpu.make_async_copy(store_ref.at[block], buf, sem)
        copy.start()
        copy.wait()
        for i in range(kb):
            piece = (buf[i].astype(F32) * gain_ref[block * kb + i]).astype(BF).astype(F32)
            a, b = piece[:, :LANES], piece[:, LANES:]
            piece = jnp.concatenate([narrow_sum(a + b), narrow(a - b)], axis=1).astype(BF)
            out_ref[i * cycles : (i + 1) * cycles, :] = piece

    return pl.pallas_call(
        body,
        out_shape=VM((kb * cycles, angles), BF),
        in_specs=[spec(pltpu.SMEM), spec(pltpu.SMEM), spec(pltpu.SMEM), spec(pltpu.HBM)],
        out_specs=spec(),
        scratch_shapes=[VM((kb, cycles, angles), BF), pltpu.SemaphoreType.DMA],
        compiler_params=params(60),
        name="pick_block",
    )(me, block_owner, class_gain, away(ref_store))


def halve_images(own, other, nb):
    particles, cycles, angles = own.shape
    per = particles // nb

    def body(own_ref, other_ref, out_ref, a_scr, b_scr):
        fill(a_scr, own_ref[...].astype(F32).reshape(particles * cycles, angles))
        fill(b_scr, other_ref[...].astype(F32).reshape(particles * cycles, angles))
        for r in range(cycles):
            a = take_cycle(a_scr, r, particles, cycles)
            b = take_cycle(b_scr, r, particles, cycles)
            for i, op in enumerate((jnp.add, jnp.subtract)):
                x, y = op(a[0], a[1]), op(b[0], b[1])
                both = [v.reshape(nb, per, LANES) for v in (x, y)]
                both = jnp.concatenate(both, axis=1).reshape(2 * particles, LANES)
                out_ref[i, r] = narrow(both).astype(BF)

    return pl.pallas_call(
        body,
        out_shape=VM((2, cycles, 2 * particles, LANES), BF),
        in_specs=[spec(), spec()],
        out_specs=spec(),
        scratch_shapes=[VM((2, particles * cycles, LANES), F32)] * 2,
        compiler_params=params(),
        name="halve_images",
    )(own, here(other))


def pair_up(mine, theirs, halves):
    def body(a_ref, b_ref, _, out_ref):
        out_ref[0] = a_ref[...]
        out_ref[1] = b_ref[...]

    return pl.pallas_call(
        body,
        out_shape=VM((2,) + mine.shape, BF),
        in_specs=[spec()] * 3,
        out_specs=spec(),
        compiler_params=params(),
        name="pair_up",
    )(here(mine), here(theirs), here(halves))


def rotate_images(x_ref, r, nb, step):
    plus, minus = x_ref[0, r], x_ref[1, r]
    per = plus.shape[0] // nb
    turned = [turn(plus, minus, step * s) for s in range(N1)]
    return [
        jnp.concatenate(
            [t[i][j * per : (j + 1) * per] for j in range(nb) for t in turned], axis=0
        )
        for i in range(2)
    ]


def correlate(images, refs, nb, step):
    _, cycles, particles, _ = images.shape
    total = N1 * particles
    rows = total // nb
    near, far = refs[0].shape[:2]
    classes = len(refs) * near * far // cycles
    cols = N2 * classes
    angles = 2 * LANES

    def body(x_ref, *args):
        r_refs, (out_ref, scr, rr, x) = args[: len(refs)], args[len(refs) :]
        blocks = [r_ref[d].astype(F32) for r_ref in r_refs for d in range(near)]
        fill(scr, jnp.concatenate(blocks, axis=0))
        square = jnp.zeros((classes, LANES), F32)
        for r in range(cycles):
            plus, minus = take_cycle(scr, r, classes, cycles)
            square = square + 0.5 * (plus * plus + minus * minus)
            plus, minus = plus.astype(BF), minus.astype(BF)
            x[0, r], x[1, r] = rotate_images(x_ref, r, nb, step)
            for s in range(N2):
                p, m = turn(plus, minus, angles - step * N1 * s)
                rr[0, r, s * classes : (s + 1) * classes, :] = p
                rr[1, r, s * classes : (s + 1) * classes, :] = m
        norm = jnp.broadcast_to(jnp.sum(square, axis=1, keepdims=True), (classes, cols))
        k = lax.broadcasted_iota(jnp.int32, (classes, cols), 0)
        lane = lax.broadcasted_iota(jnp.int32, (classes, cols), 1)
        norm = jnp.sum(jnp.where(lane % classes == k, norm, 0.0), axis=0, keepdims=True)
        for i in range(2):
            left = jnp.concatenate([x[i, r] for r in range(cycles)], axis=1)
            right = jnp.concatenate([rr[i, r] for r in range(cycles)], axis=1)
            part = lax.dot_general(
                left, right, (((1,), (1,)), ((), ())), preferred_element_type=F32
            )
            if i == 0:
                part = part - norm
            for t in range(cols // LANES):
                tile = part[:, t * LANES : (t + 1) * LANES].astype(BF)
                out_ref[:, t, i * rows : (i + 1) * rows, :] = tile.reshape(nb, rows, LANES)

    return pl.pallas_call(
        body,
        out_shape=jax.ShapeDtypeStruct((nb, cols // LANES, 2 * rows, LANES), BF),
        in_specs=[spec()] * (1 + len(refs)),
        out_specs=spec(),
        scratch_shapes=[
            VM((2, classes * cycles, LANES), F32),
            VM((2, cycles, cols, LANES), BF),
            VM((2, cycles, total, LANES), BF),
        ],
        compiler_params=params(),
        name="correlate",
    )(here(images), *[here(r) for r in refs])


def local_softmax(me, scores, precision, others):
    nb, tiles, rows, _ = scores.shape
    cols = tiles * LANES
    half = rows // 2
    group = half // N1
    own = group // 2

    def across(op, x):
        pieces = [x[i * group : (i + 1) * group] for i in range(N1)]
        return op(op(pieces[0], pieces[1]), op(pieces[2], pieces[3]))

    def body(me_ref, x_ref, a_ref, b_ref, e_ref, stat_ref):
        total = x_ref[0].astype(F32)
        for i in range(1, nb):
            total = total + x_ref[i].astype(F32)
        total = jnp.concatenate([total[t] for t in range(tiles)], axis=1)
        plus, minus = total[:half], total[half:]
        row = lax.broadcasted_iota(jnp.int32, (own, own), 0)
        col = lax.broadcasted_iota(jnp.int32, (own, own), 1)
        scale = [
            jnp.sum(jnp.where(row == col, ref[pl.ds(me_ref[0], 1), :], 0.0), axis=1, keepdims=True)
            for ref in (a_ref, b_ref)
        ]
        scale = jnp.concatenate(scale * N1, axis=0) * 0.5
        near, far = scale * (plus + minus), scale * (plus - minus)
        top = jnp.max(jnp.maximum(near, far), axis=1, keepdims=True)
        top = across(jnp.maximum, top)
        tops = jnp.concatenate([top] * N1, axis=0)
        near, far = jnp.exp(near - tops), jnp.exp(far - tops)
        e_ref[0] = near
        e_ref[1] = far
        amount = across(jnp.add, jnp.sum(near + far, axis=1, keepdims=True))
        stat_ref[0] = jnp.broadcast_to(top, (group, LANES))
        stat_ref[1] = jnp.broadcast_to(amount, (group, LANES))

    return pl.pallas_call(
        body,
        out_shape=(VM((2, half, cols), F32), VM((2, group, LANES), F32)),
        in_specs=[spec(pltpu.SMEM), spec(), spec(), spec()],
        out_specs=(spec(), spec()),
        compiler_params=params(),
        name="local_softmax",
    )(me, here(scores), here(precision), here(others))


def normalize(e, mine, theirs, copies):
    _, half, cols = e.shape
    group = mine.shape[1]

    def body(e_ref, a_ref, b_ref, out_ref):
        def flipped(x):
            return jnp.concatenate([x[group // 2 :], x[: group // 2]], axis=0)

        top_a, sum_a = a_ref[0], a_ref[1]
        top_b, sum_b = flipped(b_ref[0]), flipped(b_ref[1])
        top = jnp.maximum(top_a, top_b)
        part = jnp.exp(top_a - top)
        factor = part / (sum_a * part + sum_b * jnp.exp(top_b - top))
        factor = jnp.concatenate([jnp.concatenate([factor] * N1, axis=0)] * (cols // LANES), axis=1)
        near, far = e_ref[0] * factor, e_ref[1] * factor
        w = jnp.concatenate([near + far, near - far], axis=0).T.astype(BF)
        for c in range(copies):
            out_ref[c] = w

    return pl.pallas_call(
        body,
        out_shape=VM((copies, cols, 2 * half), BF),
        in_specs=[spec(), spec(), spec()],
        out_specs=spec(),
        compiler_params=params(),
        name="normalize",
    )(here(e), here(mine), here(theirs))


def accumulate(me, weights, images, ny, nz, step):
    owners = ny * nz
    nb, cols, lanes = weights.shape
    cycles = images.shape[1]
    classes = cols // N2
    pair = 2 * LANES

    def body(me_ref, w_ref, x_ref, out_ref, scr, x):
        for r in range(cycles):
            x[0, r], x[1, r] = rotate_images(x_ref, r, nb, step)
        left = lax.broadcasted_iota(jnp.int32, (cols, lanes), 1) < lanes // 2
        near, far = [], []
        for j in range(0, nb, 2):
            a, b = w_ref[j], w_ref[j + 1]
            near.append(jnp.where(left, a, pltpu.roll(b, lanes // 2, 1)))
            far.append(jnp.where(left, pltpu.roll(a, lanes // 2, 1), b))
        w = [jnp.concatenate(v, axis=1) for v in (near, far)]
        for c in range(0, cycles, 2):
            spread = []
            for i in range(2):
                both = jnp.concatenate([x[i, c], x[i, c + 1]], axis=1)
                spread.append(jnp.dot(w[i], both, preferred_element_type=F32))
            for d in range(2):
                plus = minus = None
                for s in range(N2):
                    p, m = (
                        v[s * classes : (s + 1) * classes, d * LANES : (d + 1) * LANES]
                        for v in spread
                    )
                    p, m = turn(p, m, step * N1 * s)
                    plus = plus + p if s else p
                    minus = minus + m if s else m
                rows = pl.ds(c + d, classes, stride=cycles)
                scr.at[0][rows, :] = 0.5 * (plus + minus)
                scr.at[1][rows, :] = 0.5 * (plus - minus)
        whole = jnp.concatenate([scr[0], scr[1]], axis=1)
        whole = whole.reshape(out_ref.shape).astype(BF)
        place = me_ref[0] // 2
        y, z = place // nz, place % nz
        for slot in range(owners):
            dz, dy = slot // ny, slot % ny
            out_ref[(y + dy) % ny * nz + (z + nz - dz) % nz] = whole[slot]

    return pl.pallas_call(
        body,
        out_shape=VM((owners, classes // owners * cycles, pair), BF),
        in_specs=[spec(pltpu.SMEM), spec(), spec()],
        out_specs=spec(),
        scratch_shapes=[
            VM((2, classes * cycles, LANES), F32),
            VM((2, cycles, N1 * images.shape[2], LANES), BF),
        ],
        compiler_params=params(),
        name="accumulate",
    )(me, here(weights), here(images))


def add_up(parts):
    def body(x_ref, out_ref):
        total = x_ref[0].astype(F32)
        for i in range(1, parts.shape[0]):
            total = total + x_ref[i].astype(F32)
        out_ref[...] = total

    return pl.pallas_call(
        body,
        out_shape=jax.ShapeDtypeStruct(parts.shape[1:], F32),
        in_specs=[spec()],
        out_specs=spec(),
        compiler_params=params(),
        name="add_up",
    )(here(parts))


def solution(mesh):
    dom, nb = mesh.devices.shape
    ny, nz = 2, dom // 4
    view = Mesh(mesh.devices.reshape(ny, nz, 2, nb), ("yh", "z", "core", "blk"))
    swap = [(0, 1), (1, 0)]

    def shards(images, ref_store, block_owner, class_gain, precision):
        particles, cycles, angles = images.shape
        kb = ref_store.shape[2]
        rot = angles // (2 * N1 * N2)
        half = particles // nb
        other = lax.ppermute(images, "core", swap)
        other_precision = lax.ppermute(precision, "core", swap)
        y, z = lax.axis_index("yh"), lax.axis_index("z")
        me = ((y * nz + z) * 2 + lax.axis_index("core"))[None].astype(jnp.int32)
        j = lax.axis_index("blk")[None].astype(jnp.int32)
        mine = pick_block(me, block_owner, class_gain, ref_store[0])
        theirs = lax.ppermute(mine, "yh", swap)
        halves = halve_images(images, other, nb)
        refs = [pair_up(mine, theirs, halves)]
        for d in range(1, nz):
            ring = [(i, (i + d) % nz) for i in range(nz)]
            refs.append(lax.ppermute(refs[0], "z", ring))
        scores = correlate(halves, refs, nb, rot)
        scores = lax.all_to_all(scores, "blk", 0, 0)
        e, stats = local_softmax(
            j, scores, precision.reshape(nb, half), other_precision.reshape(nb, half)
        )
        theirs = lax.ppermute(stats, "core", swap)
        weights = normalize(e, stats, theirs, nb)
        weights = lax.all_to_all(weights, "blk", 0, 0)
        totals = accumulate(me, weights, halves, ny, nz, rot)
        totals = lax.all_to_all(totals, ("yh", "z"), 0, 0)
        return add_up(totals).reshape(1, 1, kb, cycles, angles)

    dom_axes = ("yh", "z", "core")
    return jax.shard_map(
        shards,
        mesh=view,
        in_specs=(
            P(dom_axes, "blk", None),
            P(dom_axes, None, None, "blk", None),
            P(),
            P(),
            P(dom_axes),
        ),
        out_specs=P(dom_axes, None, None, "blk", None),
        check_vma=False,
    )
```

```python
import jax
import jax.numpy as jnp
from jax import lax
from jax.experimental import pallas as pl
from jax.experimental.pallas import tpu as pltpu
from jax.sharding import Mesh, PartitionSpec as P

BF = jnp.bfloat16
F32 = jnp.float32
VM = pltpu.VMEM
LANES = 128
N1 = 4
N2 = 8


def spec(space=VM):
    return pl.BlockSpec(memory_space=space)


def params(mib=24):
    return pltpu.CompilerParams(vmem_limit_bytes=mib * 1024 * 1024)


def here(x):
    return pltpu.with_memory_space_constraint(x, VM)


def away(x):
    return pltpu.with_memory_space_constraint(x, pltpu.HBM)


def fill(scr, value):
    for h in range(scr.shape[0]):
        scr[h] = value[:, h * LANES : (h + 1) * LANES]


def take_cycle(scr, r, rows, cycles):
    return [scr.at[h][pl.ds(r, rows, stride=cycles), :] for h in range(2)]


def narrow(x):
    wide = x * 65537.0
    return wide - (wide - x)


def narrow_sum(x):
    near = narrow(x)
    lane = lax.broadcasted_iota(jnp.int32, x.shape, 1)
    rest = jnp.sum(x - near, axis=1, keepdims=True)
    return jnp.where(lane == 0, near + rest, near)


def turn(plus, minus, t):
    t = t % (2 * LANES)
    if t == 0:
        return plus, minus
    if t >= LANES:
        return turn(plus, -minus, t - LANES)
    lane = lax.broadcasted_iota(jnp.int32, minus.shape, 1)
    minus = pltpu.roll(minus, t, 1)
    return pltpu.roll(plus, t, 1), jnp.where(lane < t, -minus, minus)


def pick_block(me, block_owner, class_gain, ref_store):
    nblk, kb, cycles, angles = ref_store.shape

    def body(me_ref, owner_ref, gain_ref, store_ref, out_ref, buf, sem):
        block = jnp.int32(0)
        for b in range(nblk):
            block = jnp.where(owner_ref[b] == me_ref[0], jnp.int32(b), block)
        copy = pltpu.make_async_copy(store_ref.at[block], buf, sem)
        copy.start()
        copy.wait()
        for i in range(kb):
            piece = (buf[i].astype(F32) * gain_ref[block * kb + i]).astype(BF).astype(F32)
            a, b = piece[:, :LANES], piece[:, LANES:]
            piece = jnp.concatenate([narrow_sum(a + b), narrow(a - b)], axis=1).astype(BF)
            out_ref[i * cycles : (i + 1) * cycles, :] = piece

    return pl.pallas_call(
        body,
        out_shape=VM((kb * cycles, angles), BF),
        in_specs=[spec(pltpu.SMEM), spec(pltpu.SMEM), spec(pltpu.SMEM), spec(pltpu.HBM)],
        out_specs=spec(),
        scratch_shapes=[VM((kb, cycles, angles), BF), pltpu.SemaphoreType.DMA],
        compiler_params=params(60),
        name="pick_block",
    )(me, block_owner, class_gain, away(ref_store))


def halve_images(own, other, nb):
    particles, cycles, angles = own.shape
    per = particles // nb

    def body(own_ref, other_ref, out_ref, a_scr, b_scr):
        fill(a_scr, own_ref[...].astype(F32).reshape(particles * cycles, angles))
        fill(b_scr, other_ref[...].astype(F32).reshape(particles * cycles, angles))
        for r in range(cycles):
            a = take_cycle(a_scr, r, particles, cycles)
            b = take_cycle(b_scr, r, particles, cycles)
            for i, op in enumerate((jnp.add, jnp.subtract)):
                x, y = op(a[0], a[1]), op(b[0], b[1])
                both = [v.reshape(nb, per, LANES) for v in (x, y)]
                both = jnp.concatenate(both, axis=1).reshape(2 * particles, LANES)
                out_ref[i, r] = narrow(both).astype(BF)

    return pl.pallas_call(
        body,
        out_shape=VM((2, cycles, 2 * particles, LANES), BF),
        in_specs=[spec(), spec()],
        out_specs=spec(),
        scratch_shapes=[VM((2, particles * cycles, LANES), F32)] * 2,
        compiler_params=params(),
        name="halve_images",
    )(own, here(other))


def pair_up(mine, theirs, halves):
    def body(a_ref, b_ref, _, out_ref):
        out_ref[0] = a_ref[...]
        out_ref[1] = b_ref[...]

    return pl.pallas_call(
        body,
        out_shape=VM((2,) + mine.shape, BF),
        in_specs=[spec()] * 3,
        out_specs=spec(),
        compiler_params=params(),
        name="pair_up",
    )(here(mine), here(theirs), here(halves))


def rotate_images(x_ref, r, nb, step):
    plus, minus = x_ref[0, r], x_ref[1, r]
    per = plus.shape[0] // nb
    turned = [turn(plus, minus, step * s) for s in range(N1)]
    return [
        jnp.concatenate(
            [t[i][j * per : (j + 1) * per] for j in range(nb) for t in turned], axis=0
        )
        for i in range(2)
    ]


def correlate(images, refs, nb, step):
    _, cycles, particles, _ = images.shape
    total = N1 * particles
    rows = total // nb
    near, far = refs[0].shape[:2]
    classes = len(refs) * near * far // cycles
    cols = N2 * classes
    angles = 2 * LANES

    def body(x_ref, *args):
        r_refs, (out_ref, scr, rr, x) = args[: len(refs)], args[len(refs) :]
        blocks = [r_ref[d].astype(F32) for r_ref in r_refs for d in range(near)]
        fill(scr, jnp.concatenate(blocks, axis=0))
        square = jnp.zeros((classes, LANES), F32)
        for r in range(cycles):
            plus, minus = take_cycle(scr, r, classes, cycles)
            square = square + 0.5 * (plus * plus + minus * minus)
            plus, minus = plus.astype(BF), minus.astype(BF)
            x[0, r], x[1, r] = rotate_images(x_ref, r, nb, step)
            for s in range(N2):
                p, m = turn(plus, minus, angles - step * N1 * s)
                rr[0, r, s * classes : (s + 1) * classes, :] = p
                rr[1, r, s * classes : (s + 1) * classes, :] = m
        norm = jnp.broadcast_to(jnp.sum(square, axis=1, keepdims=True), (classes, cols))
        k = lax.broadcasted_iota(jnp.int32, (classes, cols), 0)
        lane = lax.broadcasted_iota(jnp.int32, (classes, cols), 1)
        norm = jnp.sum(jnp.where(lane % classes == k, norm, 0.0), axis=0, keepdims=True)
        for i in range(2):
            left = jnp.concatenate([x[i, r] for r in range(cycles)], axis=1)
            right = jnp.concatenate([rr[i, r] for r in range(cycles)], axis=1)
            part = lax.dot_general(
                left, right, (((1,), (1,)), ((), ())), preferred_element_type=F32
            )
            if i == 0:
                part = part - norm
            for t in range(cols // LANES):
                tile = part[:, t * LANES : (t + 1) * LANES].astype(BF)
                out_ref[:, t, i * rows : (i + 1) * rows, :] = tile.reshape(nb, rows, LANES)

    return pl.pallas_call(
        body,
        out_shape=jax.ShapeDtypeStruct((nb, cols // LANES, 2 * rows, LANES), BF),
        in_specs=[spec()] * (1 + len(refs)),
        out_specs=spec(),
        scratch_shapes=[
            VM((2, classes * cycles, LANES), F32),
            VM((2, cycles, cols, LANES), BF),
            VM((2, cycles, total, LANES), BF),
        ],
        compiler_params=params(),
        name="correlate",
    )(here(images), *[here(r) for r in refs])


def local_softmax(me, scores, precision, others):
    nb, tiles, rows, _ = scores.shape
    cols = tiles * LANES
    half = rows // 2
    group = half // N1
    own = group // 2

    def across(op, x):
        pieces = [x[i * group : (i + 1) * group] for i in range(N1)]
        return op(op(pieces[0], pieces[1]), op(pieces[2], pieces[3]))

    def body(me_ref, x_ref, a_ref, b_ref, e_ref, stat_ref):
        total = x_ref[0].astype(F32)
        for i in range(1, nb):
            total = total + x_ref[i].astype(F32)
        total = jnp.concatenate([total[t] for t in range(tiles)], axis=1)
        plus, minus = total[:half], total[half:]
        row = lax.broadcasted_iota(jnp.int32, (own, own), 0)
        col = lax.broadcasted_iota(jnp.int32, (own, own), 1)
        scale = [
            jnp.sum(jnp.where(row == col, ref[pl.ds(me_ref[0], 1), :], 0.0), axis=1, keepdims=True)
            for ref in (a_ref, b_ref)
        ]
        scale = jnp.concatenate(scale * N1, axis=0) * 0.5
        near, far = scale * (plus + minus), scale * (plus - minus)
        top = jnp.max(jnp.maximum(near, far), axis=1, keepdims=True)
        top = across(jnp.maximum, top)
        tops = jnp.concatenate([top] * N1, axis=0)
        near, far = jnp.exp(near - tops), jnp.exp(far - tops)
        e_ref[0] = near
        e_ref[1] = far
        amount = across(jnp.add, jnp.sum(near + far, axis=1, keepdims=True))
        stat_ref[0] = jnp.broadcast_to(top, (group, LANES))
        stat_ref[1] = jnp.broadcast_to(amount, (group, LANES))

    return pl.pallas_call(
        body,
        out_shape=(VM((2, half, cols), F32), VM((2, group, LANES), F32)),
        in_specs=[spec(pltpu.SMEM), spec(), spec(), spec()],
        out_specs=(spec(), spec()),
        compiler_params=params(),
        name="local_softmax",
    )(me, here(scores), here(precision), here(others))


def normalize(e, mine, theirs, copies):
    _, half, cols = e.shape
    group = mine.shape[1]

    def body(e_ref, a_ref, b_ref, out_ref):
        def flipped(x):
            return jnp.concatenate([x[group // 2 :], x[: group // 2]], axis=0)

        top_a, sum_a = a_ref[0], a_ref[1]
        top_b, sum_b = flipped(b_ref[0]), flipped(b_ref[1])
        top = jnp.maximum(top_a, top_b)
        part = jnp.exp(top_a - top)
        factor = part / (sum_a * part + sum_b * jnp.exp(top_b - top))
        factor = jnp.concatenate([jnp.concatenate([factor] * N1, axis=0)] * (cols // LANES), axis=1)
        near, far = e_ref[0] * factor, e_ref[1] * factor
        w = jnp.concatenate([near + far, near - far], axis=0).T.astype(BF)
        for c in range(copies):
            out_ref[c] = w

    return pl.pallas_call(
        body,
        out_shape=VM((copies, cols, 2 * half), BF),
        in_specs=[spec(), spec(), spec()],
        out_specs=spec(),
        compiler_params=params(),
        name="normalize",
    )(here(e), here(mine), here(theirs))


def accumulate(order, weights, images, step):
    owners = order.shape[0]
    nb, cols, lanes = weights.shape
    cycles = images.shape[1]
    classes = cols // N2
    pair = 2 * LANES

    def body(order_ref, w_ref, x_ref, out_ref, scr, x):
        for r in range(cycles):
            x[0, r], x[1, r] = rotate_images(x_ref, r, nb, step)
        left = lax.broadcasted_iota(jnp.int32, (cols, lanes), 1) < lanes // 2
        near, far = [], []
        for j in range(0, nb, 2):
            a, b = w_ref[j], w_ref[j + 1]
            near.append(jnp.where(left, a, pltpu.roll(b, lanes // 2, 1)))
            far.append(jnp.where(left, pltpu.roll(a, lanes // 2, 1), b))
        w = [jnp.concatenate(v, axis=1) for v in (near, far)]
        for c in range(0, cycles, 2):
            spread = []
            for i in range(2):
                both = jnp.concatenate([x[i, c], x[i, c + 1]], axis=1)
                spread.append(jnp.dot(w[i], both, preferred_element_type=F32))
            for d in range(2):
                plus = minus = None
                for s in range(N2):
                    p, m = (
                        v[s * classes : (s + 1) * classes, d * LANES : (d + 1) * LANES]
                        for v in spread
                    )
                    p, m = turn(p, m, step * N1 * s)
                    plus = plus + p if s else p
                    minus = minus + m if s else m
                rows = pl.ds(c + d, classes, stride=cycles)
                scr.at[0][rows, :] = 0.5 * (plus + minus)
                scr.at[1][rows, :] = 0.5 * (plus - minus)
        whole = jnp.concatenate([scr[0], scr[1]], axis=1)
        whole = whole.reshape(out_ref.shape).astype(BF)
        for slot in range(owners):
            out_ref[order_ref[slot]] = whole[slot]

    return pl.pallas_call(
        body,
        out_shape=VM((owners, classes // owners * cycles, pair), BF),
        in_specs=[spec(pltpu.SMEM), spec(), spec()],
        out_specs=spec(),
        scratch_shapes=[
            VM((2, classes * cycles, LANES), F32),
            VM((2, cycles, N1 * images.shape[2], LANES), BF),
        ],
        compiler_params=params(),
        name="accumulate",
    )(order, here(weights), here(images))


def add_up(parts):
    def body(x_ref, out_ref):
        total = x_ref[0].astype(F32)
        for i in range(1, parts.shape[0]):
            total = total + x_ref[i].astype(F32)
        out_ref[...] = total

    return pl.pallas_call(
        body,
        out_shape=jax.ShapeDtypeStruct(parts.shape[1:], F32),
        in_specs=[spec()],
        out_specs=spec(),
        compiler_params=params(),
        name="add_up",
    )(here(parts))


def solution(mesh):
    dom, nb = mesh.devices.shape
    ny, nz = 2, dom // 4
    view = Mesh(mesh.devices.reshape(ny, nz, 2, nb), ("yh", "z", "core", "blk"))
    swap = [(0, 1), (1, 0)]

    def shards(images, ref_store, block_owner, class_gain, precision):
        particles, cycles, angles = images.shape
        kb = ref_store.shape[2]
        rot = angles // (2 * N1 * N2)
        half = particles // nb
        other = lax.ppermute(images, "core", swap)
        other_precision = lax.ppermute(precision, "core", swap)
        y, z = lax.axis_index("yh"), lax.axis_index("z")
        me = ((y * nz + z) * 2 + lax.axis_index("core"))[None].astype(jnp.int32)
        j = lax.axis_index("blk")[None].astype(jnp.int32)
        mine = pick_block(me, block_owner, class_gain, ref_store[0])
        theirs = lax.ppermute(mine, "yh", swap)
        halves = halve_images(images, other, nb)
        refs = [pair_up(mine, theirs, halves)]
        for d in range(1, nz):
            ring = [(i, (i + d) % nz) for i in range(nz)]
            refs.append(lax.ppermute(refs[0], "z", ring))
        scores = correlate(halves, refs, nb, rot)
        scores = lax.all_to_all(scores, "blk", 0, 0)
        e, stats = local_softmax(
            j, scores, precision.reshape(nb, half), other_precision.reshape(nb, half)
        )
        theirs = lax.ppermute(stats, "core", swap)
        weights = normalize(e, stats, theirs, nb)
        weights = lax.all_to_all(weights, "blk", 0, 0)
        slot = jnp.arange(ny * nz, dtype=jnp.int32)
        order = (y + slot % ny) % ny * nz + (z + nz - slot // ny) % nz
        totals = accumulate(order.astype(jnp.int32), weights, halves, rot)
        totals = lax.all_to_all(totals, ("yh", "z"), 0, 0)
        return add_up(totals).reshape(1, 1, kb, cycles, angles)

    dom_axes = ("yh", "z", "core")
    return jax.shard_map(
        shards,
        mesh=view,
        in_specs=(
            P(dom_axes, "blk", None),
            P(dom_axes, None, None, "blk", None),
            P(),
            P(),
            P(dom_axes),
        ),
        out_specs=P(dom_axes, None, None, "blk", None),
        check_vma=False,
    )
```

```python
import jax
import jax.numpy as jnp
from jax import lax
from jax.experimental import pallas as pl
from jax.experimental.pallas import tpu as pltpu
from jax.sharding import Mesh, PartitionSpec as P

BF = jnp.bfloat16
F32 = jnp.float32
VM = pltpu.VMEM
LANES = 128
N1 = 4
N2 = 8


def spec(space=VM):
    return pl.BlockSpec(memory_space=space)


def params(mib=24):
    return pltpu.CompilerParams(vmem_limit_bytes=mib * 1024 * 1024)


def here(x):
    return pltpu.with_memory_space_constraint(x, VM)


def away(x):
    return pltpu.with_memory_space_constraint(x, pltpu.HBM)


def fill(scr, value):
    for h in range(scr.shape[0]):
        scr[h] = value[:, h * LANES : (h + 1) * LANES]


def take_cycle(scr, r, rows, cycles):
    return [scr.at[h][pl.ds(r, rows, stride=cycles), :] for h in range(2)]


def narrow(x):
    wide = x * 65537.0
    return wide - (wide - x)


def narrow_sum(x):
    near = narrow(x)
    lane = lax.broadcasted_iota(jnp.int32, x.shape, 1)
    rest = jnp.sum(x - near, axis=1, keepdims=True)
    return jnp.where(lane == 0, near + rest, near)


def turn(plus, minus, t):
    t = t % (2 * LANES)
    if t == 0:
        return plus, minus
    if t >= LANES:
        return turn(plus, -minus, t - LANES)
    lane = lax.broadcasted_iota(jnp.int32, minus.shape, 1)
    minus = pltpu.roll(minus, t, 1)
    return pltpu.roll(plus, t, 1), jnp.where(lane < t, -minus, minus)


def pick_block(me, block_owner, class_gain, ref_store):
    nblk, kb, cycles, angles = ref_store.shape

    def body(me_ref, owner_ref, gain_ref, store_ref, out_ref, buf, sem):
        block = jnp.int32(0)
        for b in range(nblk):
            block = jnp.where(owner_ref[b] == me_ref[0], jnp.int32(b), block)
        copy = pltpu.make_async_copy(store_ref.at[block], buf, sem)
        copy.start()
        copy.wait()
        for i in range(kb):
            piece = (buf[i].astype(F32) * gain_ref[block * kb + i]).astype(BF).astype(F32)
            a, b = piece[:, :LANES], piece[:, LANES:]
            piece = jnp.concatenate([narrow_sum(a + b), narrow(a - b)], axis=1).astype(BF)
            out_ref[i * cycles : (i + 1) * cycles, :] = piece

    return pl.pallas_call(
        body,
        out_shape=VM((kb * cycles, angles), BF),
        in_specs=[spec(pltpu.SMEM), spec(pltpu.SMEM), spec(pltpu.SMEM), spec(pltpu.HBM)],
        out_specs=spec(),
        scratch_shapes=[VM((kb, cycles, angles), BF), pltpu.SemaphoreType.DMA],
        compiler_params=params(60),
        name="pick_block",
    )(me, block_owner, class_gain, away(ref_store))


def halve_images(own, other, nb):
    particles, cycles, angles = own.shape
    per = particles // nb

    def body(own_ref, other_ref, out_ref, a_scr, b_scr):
        fill(a_scr, own_ref[...].astype(F32).reshape(particles * cycles, angles))
        fill(b_scr, other_ref[...].astype(F32).reshape(particles * cycles, angles))
        for r in range(cycles):
            a = take_cycle(a_scr, r, particles, cycles)
            b = take_cycle(b_scr, r, particles, cycles)
            for i, op in enumerate((jnp.add, jnp.subtract)):
                x, y = op(a[0], a[1]), op(b[0], b[1])
                both = [v.reshape(nb, per, LANES) for v in (x, y)]
                both = jnp.concatenate(both, axis=1).reshape(2 * particles, LANES)
                out_ref[i, r] = narrow(both).astype(BF)

    return pl.pallas_call(
        body,
        out_shape=VM((2, cycles, 2 * particles, LANES), BF),
        in_specs=[spec(), spec()],
        out_specs=spec(),
        scratch_shapes=[VM((2, particles * cycles, LANES), F32)] * 2,
        compiler_params=params(),
        name="halve_images",
    )(own, here(other))


def pair_up(mine, theirs, halves):
    def body(a_ref, b_ref, _, out_ref):
        out_ref[0] = a_ref[...]
        out_ref[1] = b_ref[...]

    return pl.pallas_call(
        body,
        out_shape=VM((2,) + mine.shape, BF),
        in_specs=[spec()] * 3,
        out_specs=spec(),
        compiler_params=params(),
        name="pair_up",
    )(here(mine), here(theirs), here(halves))


def rotate_images(x_ref, r, nb, step):
    plus, minus = x_ref[0, r], x_ref[1, r]
    per = plus.shape[0] // nb
    turned = [turn(plus, minus, step * s) for s in range(N1)]
    return [
        jnp.concatenate(
            [t[i][j * per : (j + 1) * per] for j in range(nb) for t in turned], axis=0
        )
        for i in range(2)
    ]


def correlate(images, refs, nb, step, before=()):
    _, cycles, particles, _ = images.shape
    total = N1 * particles
    rows = total // nb
    near, far = refs[0].shape[:2]
    classes = len(refs) * near * far // cycles
    cols = N2 * classes
    angles = 2 * LANES
    first = sum(b.shape[1] for b in before)
    tiles = first + cols // LANES

    def body(x_ref, *args):
        r_refs, args = args[: len(refs)], args[len(refs) :]
        b_refs, (out_ref, scr, rr, x) = args[: len(before)], args[len(before) :]
        at = 0
        for b_ref in b_refs:
            out_ref[:, at : at + b_ref.shape[1]] = b_ref[...]
            at += b_ref.shape[1]
        blocks = [r_ref[d].astype(F32) for r_ref in r_refs for d in range(near)]
        fill(scr, jnp.concatenate(blocks, axis=0))
        square = jnp.zeros((classes, LANES), F32)
        for r in range(cycles):
            plus, minus = take_cycle(scr, r, classes, cycles)
            square = square + 0.5 * (plus * plus + minus * minus)
            plus, minus = plus.astype(BF), minus.astype(BF)
            x[0, r], x[1, r] = rotate_images(x_ref, r, nb, step)
            for s in range(N2):
                p, m = turn(plus, minus, angles - step * N1 * s)
                rr[0, r, s * classes : (s + 1) * classes, :] = p
                rr[1, r, s * classes : (s + 1) * classes, :] = m
        norm = jnp.broadcast_to(jnp.sum(square, axis=1, keepdims=True), (classes, cols))
        k = lax.broadcasted_iota(jnp.int32, (classes, cols), 0)
        lane = lax.broadcasted_iota(jnp.int32, (classes, cols), 1)
        norm = jnp.sum(jnp.where(lane % classes == k, norm, 0.0), axis=0, keepdims=True)
        for i in range(2):
            left = jnp.concatenate([x[i, r] for r in range(cycles)], axis=1)
            right = jnp.concatenate([rr[i, r] for r in range(cycles)], axis=1)
            part = lax.dot_general(
                left, right, (((1,), (1,)), ((), ())), preferred_element_type=F32
            )
            if i == 0:
                part = part - norm
            for t in range(cols // LANES):
                tile = part[:, t * LANES : (t + 1) * LANES].astype(BF)
                at = slice(i * rows, (i + 1) * rows)
                out_ref[:, first + t, at, :] = tile.reshape(nb, rows, LANES)

    out_shape = jax.ShapeDtypeStruct if before else VM
    return pl.pallas_call(
        body,
        out_shape=out_shape((nb, tiles, 2 * rows, LANES), BF),
        in_specs=[spec()] * (1 + len(refs) + len(before)),
        out_specs=spec(),
        scratch_shapes=[
            VM((2, classes * cycles, LANES), F32),
            VM((2, cycles, cols, LANES), BF),
            VM((2, cycles, total, LANES), BF),
        ],
        compiler_params=params(),
        name="correlate",
    )(here(images), *[here(r) for r in (*refs, *before)])


def local_softmax(me, scores, precision, others):
    nb, tiles, rows, _ = scores.shape
    cols = tiles * LANES
    half = rows // 2
    group = half // N1
    own = group // 2

    def across(op, x):
        pieces = [x[i * group : (i + 1) * group] for i in range(N1)]
        return op(op(pieces[0], pieces[1]), op(pieces[2], pieces[3]))

    def body(me_ref, x_ref, a_ref, b_ref, e_ref, stat_ref):
        total = x_ref[0].astype(F32)
        for i in range(1, nb):
            total = total + x_ref[i].astype(F32)
        total = jnp.concatenate([total[t] for t in range(tiles)], axis=1)
        plus, minus = total[:half], total[half:]
        row = lax.broadcasted_iota(jnp.int32, (own, own), 0)
        col = lax.broadcasted_iota(jnp.int32, (own, own), 1)
        scale = [
            jnp.sum(jnp.where(row == col, ref[pl.ds(me_ref[0], 1), :], 0.0), axis=1, keepdims=True)
            for ref in (a_ref, b_ref)
        ]
        scale = jnp.concatenate(scale * N1, axis=0) * 0.5
        near, far = scale * (plus + minus), scale * (plus - minus)
        top = jnp.max(jnp.maximum(near, far), axis=1, keepdims=True)
        top = across(jnp.maximum, top)
        tops = jnp.concatenate([top] * N1, axis=0)
        near, far = jnp.exp(near - tops), jnp.exp(far - tops)
        e_ref[0] = near
        e_ref[1] = far
        amount = across(jnp.add, jnp.sum(near + far, axis=1, keepdims=True))
        stat_ref[0] = jnp.broadcast_to(top, (group, LANES))
        stat_ref[1] = jnp.broadcast_to(amount, (group, LANES))

    return pl.pallas_call(
        body,
        out_shape=(VM((2, half, cols), F32), VM((2, group, LANES), F32)),
        in_specs=[spec(pltpu.SMEM), spec(), spec(), spec()],
        out_specs=(spec(), spec()),
        compiler_params=params(),
        name="local_softmax",
    )(me, here(scores), here(precision), here(others))


def normalize(e, mine, theirs, copies):
    _, half, cols = e.shape
    group = mine.shape[1]

    def body(e_ref, a_ref, b_ref, out_ref):
        def flipped(x):
            return jnp.concatenate([x[group // 2 :], x[: group // 2]], axis=0)

        top_a, sum_a = a_ref[0], a_ref[1]
        top_b, sum_b = flipped(b_ref[0]), flipped(b_ref[1])
        top = jnp.maximum(top_a, top_b)
        part = jnp.exp(top_a - top)
        factor = part / (sum_a * part + sum_b * jnp.exp(top_b - top))
        factor = jnp.concatenate([jnp.concatenate([factor] * N1, axis=0)] * (cols // LANES), axis=1)
        near, far = e_ref[0] * factor, e_ref[1] * factor
        w = jnp.concatenate([near + far, near - far], axis=0).T.astype(BF)
        for c in range(copies):
            out_ref[c] = w

    return pl.pallas_call(
        body,
        out_shape=VM((copies, cols, 2 * half), BF),
        in_specs=[spec(), spec(), spec()],
        out_specs=spec(),
        compiler_params=params(),
        name="normalize",
    )(here(e), here(mine), here(theirs))


def accumulate(me, weights, images, ny, nz, step):
    owners = ny * nz
    nb, cols, lanes = weights.shape
    cycles = images.shape[1]
    classes = cols // N2
    per = LANES // N2
    pair = 2 * LANES

    def body(me_ref, w_ref, x_ref, out_ref, scr, x):
        for r in range(cycles):
            x[0, r], x[1, r] = rotate_images(x_ref, r, nb, step)
        left = lax.broadcasted_iota(jnp.int32, (cols, lanes), 1) < lanes // 2
        near, far = [], []
        for j in range(0, nb, 2):
            a, b = w_ref[j], w_ref[j + 1]
            near.append(jnp.where(left, a, pltpu.roll(b, lanes // 2, 1)))
            far.append(jnp.where(left, pltpu.roll(a, lanes // 2, 1), b))
        w = [jnp.concatenate(v, axis=1) for v in (near, far)]
        for c in range(0, cycles, 2):
            spread = []
            for i in range(2):
                both = jnp.concatenate([x[i, c], x[i, c + 1]], axis=1)
                spread.append(jnp.dot(w[i], both, preferred_element_type=F32))
            for d in range(2):
                plus = minus = None
                for s in range(N2):
                    p, m = (
                        jnp.concatenate(
                            [
                                v[t + s * per : t + (s + 1) * per, d * LANES : (d + 1) * LANES]
                                for t in range(0, cols, LANES)
                            ],
                            axis=0,
                        )
                        for v in spread
                    )
                    p, m = turn(p, m, step * N1 * s)
                    plus = plus + p if s else p
                    minus = minus + m if s else m
                rows = pl.ds(c + d, classes, stride=cycles)
                scr.at[0][rows, :] = 0.5 * (plus + minus)
                scr.at[1][rows, :] = 0.5 * (plus - minus)
        whole = jnp.concatenate([scr[0], scr[1]], axis=1)
        whole = whole.reshape(out_ref.shape).astype(BF)
        place = me_ref[0] // 2
        y, z = place // nz, place % nz
        for slot in range(owners):
            dz, dy = (0, 1, 3, 2)[slot // ny], slot % ny
            out_ref[(y ^ dy) * nz + (z ^ dz)] = whole[slot]

    return pl.pallas_call(
        body,
        out_shape=VM((owners, classes // owners * cycles, pair), BF),
        in_specs=[spec(pltpu.SMEM), spec(), spec()],
        out_specs=spec(),
        scratch_shapes=[
            VM((2, classes * cycles, LANES), F32),
            VM((2, cycles, N1 * images.shape[2], LANES), BF),
        ],
        compiler_params=params(),
        name="accumulate",
    )(me, here(weights), here(images))


def add_up(parts):
    def body(x_ref, out_ref):
        total = x_ref[0].astype(F32)
        for i in range(1, parts.shape[0]):
            total = total + x_ref[i].astype(F32)
        out_ref[...] = total

    return pl.pallas_call(
        body,
        out_shape=jax.ShapeDtypeStruct(parts.shape[1:], F32),
        in_specs=[spec()],
        out_specs=spec(),
        compiler_params=params(),
        name="add_up",
    )(here(parts))


def solution(mesh):
    dom, nb = mesh.devices.shape
    ny, nz = 2, dom // 4
    view = Mesh(mesh.devices.reshape(ny, nz, 2, nb), ("yh", "z", "core", "blk"))
    swap = [(0, 1), (1, 0)]

    def shards(images, ref_store, block_owner, class_gain, precision):
        particles, cycles, angles = images.shape
        kb = ref_store.shape[2]
        rot = angles // (2 * N1 * N2)
        half = particles // nb
        other = lax.ppermute(images, "core", swap)
        other_precision = lax.ppermute(precision, "core", swap)
        y, z = lax.axis_index("yh"), lax.axis_index("z")
        me = ((y * nz + z) * 2 + lax.axis_index("core"))[None].astype(jnp.int32)
        j = lax.axis_index("blk")[None].astype(jnp.int32)
        mine = pick_block(me, block_owner, class_gain, ref_store[0])
        theirs = lax.ppermute(mine, "yh", swap)
        halves = halve_images(images, other, nb)
        refs = [pair_up(mine, theirs, halves)]
        for d in (1, 3, 2):
            ring = [(i, i ^ d) for i in range(nz)]
            refs.append(lax.ppermute(refs[0], "z", ring))
        early = correlate(halves, refs[:2], nb, rot)
        scores = correlate(halves, refs[2:], nb, rot, (early,))
        scores = lax.all_to_all(scores, "blk", 0, 0)
        e, stats = local_softmax(
            j, scores, precision.reshape(nb, half), other_precision.reshape(nb, half)
        )
        theirs = lax.ppermute(stats, "core", swap)
        weights = normalize(e, stats, theirs, nb)
        weights = lax.all_to_all(weights, "blk", 0, 0)
        totals = accumulate(me, weights, halves, ny, nz, rot)
        totals = lax.all_to_all(totals, ("yh", "z"), 0, 0)
        return add_up(totals).reshape(1, 1, kb, cycles, angles)

    dom_axes = ("yh", "z", "core")
    return jax.shard_map(
        shards,
        mesh=view,
        in_specs=(
            P(dom_axes, "blk", None),
            P(dom_axes, None, None, "blk", None),
            P(),
            P(),
            P(dom_axes),
        ),
        out_specs=P(dom_axes, None, None, "blk", None),
        check_vma=False,
    )
```

```python
import jax
import jax.numpy as jnp
from jax import lax
from jax.experimental import pallas as pl
from jax.experimental.pallas import tpu as pltpu
from jax.sharding import Mesh, PartitionSpec as P

BF = jnp.bfloat16
F32 = jnp.float32
VM = pltpu.VMEM
LANES = 128
N1 = 4
N2 = 8
FAR_FIRST = (0, 2, 1, 3)


def spec(space=VM):
    return pl.BlockSpec(memory_space=space)


def params(mib=24):
    return pltpu.CompilerParams(vmem_limit_bytes=mib * 1024 * 1024)


def here(x):
    return pltpu.with_memory_space_constraint(x, VM)


def away(x):
    return pltpu.with_memory_space_constraint(x, pltpu.HBM)


def fill(scr, value):
    for h in range(scr.shape[0]):
        scr[h] = value[:, h * LANES : (h + 1) * LANES]


def take_cycle(scr, r, rows, cycles):
    return [scr.at[h][pl.ds(r, rows, stride=cycles), :] for h in range(2)]


def narrow(x):
    wide = x * 65537.0
    return wide - (wide - x)


def narrow_sum(x):
    near = narrow(x)
    lane = lax.broadcasted_iota(jnp.int32, x.shape, 1)
    rest = jnp.sum(x - near, axis=1, keepdims=True)
    return jnp.where(lane == 0, near + rest, near)


def turn(plus, minus, t):
    t = t % (2 * LANES)
    if t == 0:
        return plus, minus
    if t >= LANES:
        return turn(plus, -minus, t - LANES)
    lane = lax.broadcasted_iota(jnp.int32, minus.shape, 1)
    minus = pltpu.roll(minus, t, 1)
    return pltpu.roll(plus, t, 1), jnp.where(lane < t, -minus, minus)


def pick_block(me, block_owner, class_gain, ref_store):
    nblk, kb, cycles, angles = ref_store.shape

    def body(me_ref, owner_ref, gain_ref, store_ref, out_ref, buf, sem):
        block = jnp.int32(0)
        for b in range(nblk):
            block = jnp.where(owner_ref[b] == me_ref[0], jnp.int32(b), block)
        copy = pltpu.make_async_copy(store_ref.at[block], buf, sem)
        copy.start()
        copy.wait()
        for i in range(kb):
            piece = (buf[i].astype(F32) * gain_ref[block * kb + i]).astype(BF).astype(F32)
            a, b = piece[:, :LANES], piece[:, LANES:]
            piece = jnp.concatenate([narrow_sum(a + b), narrow(a - b)], axis=1).astype(BF)
            out_ref[i * cycles : (i + 1) * cycles, :] = piece

    return pl.pallas_call(
        body,
        out_shape=VM((kb * cycles, angles), BF),
        in_specs=[spec(pltpu.SMEM), spec(pltpu.SMEM), spec(pltpu.SMEM), spec(pltpu.HBM)],
        out_specs=spec(),
        scratch_shapes=[VM((kb, cycles, angles), BF), pltpu.SemaphoreType.DMA],
        compiler_params=params(60),
        name="pick_block",
    )(me, block_owner, class_gain, away(ref_store))


def halve_images(own, other, nb):
    particles, cycles, angles = own.shape
    per = particles // nb

    def body(own_ref, other_ref, out_ref, a_scr, b_scr):
        fill(a_scr, own_ref[...].astype(F32).reshape(particles * cycles, angles))
        fill(b_scr, other_ref[...].astype(F32).reshape(particles * cycles, angles))
        for r in range(cycles):
            a = take_cycle(a_scr, r, particles, cycles)
            b = take_cycle(b_scr, r, particles, cycles)
            for i, op in enumerate((jnp.add, jnp.subtract)):
                x, y = op(a[0], a[1]), op(b[0], b[1])
                both = [v.reshape(nb, per, LANES) for v in (x, y)]
                both = jnp.concatenate(both, axis=1).reshape(2 * particles, LANES)
                out_ref[i, r] = narrow(both).astype(BF)

    return pl.pallas_call(
        body,
        out_shape=VM((2, cycles, 2 * particles, LANES), BF),
        in_specs=[spec(), spec()],
        out_specs=spec(),
        scratch_shapes=[VM((2, particles * cycles, LANES), F32)] * 2,
        compiler_params=params(),
        name="halve_images",
    )(own, here(other))


def pair_up(mine, theirs, *others):
    def body(a_ref, b_ref, *refs):
        out_ref = refs[-1]
        out_ref[0] = a_ref[...]
        out_ref[1] = b_ref[...]

    return pl.pallas_call(
        body,
        out_shape=VM((2,) + mine.shape, BF),
        in_specs=[spec()] * (2 + len(others)),
        out_specs=spec(),
        compiler_params=params(),
        name="pair_up",
    )(here(mine), here(theirs), *[here(o) for o in others])


def rotate_images(x_ref, r, nb, step):
    plus, minus = x_ref[0, r], x_ref[1, r]
    per = plus.shape[0] // nb
    turned = [turn(plus, minus, step * s) for s in range(N1)]
    return [
        jnp.concatenate(
            [t[i][j * per : (j + 1) * per] for j in range(nb) for t in turned], axis=0
        )
        for i in range(2)
    ]


def correlate(images, refs, nb, step, before=()):
    _, cycles, particles, _ = images.shape
    total = N1 * particles
    rows = total // nb
    near, far = refs[0].shape[:2]
    classes = len(refs) * near * far // cycles
    cols = N2 * classes
    angles = 2 * LANES
    first = sum(b.shape[1] for b in before)
    tiles = first + cols // LANES

    def body(x_ref, *args):
        r_refs, args = args[: len(refs)], args[len(refs) :]
        b_refs, (out_ref, scr, rr, x) = args[: len(before)], args[len(before) :]
        at = 0
        for b_ref in b_refs:
            out_ref[:, at : at + b_ref.shape[1]] = b_ref[...]
            at += b_ref.shape[1]
        blocks = [r_ref[d].astype(F32) for r_ref in r_refs for d in range(near)]
        fill(scr, jnp.concatenate(blocks, axis=0))
        square = jnp.zeros((classes, LANES), F32)
        for r in range(cycles):
            plus, minus = take_cycle(scr, r, classes, cycles)
            square = square + 0.5 * (plus * plus + minus * minus)
            plus, minus = plus.astype(BF), minus.astype(BF)
            x[0, r], x[1, r] = rotate_images(x_ref, r, nb, step)
            for s in range(N2):
                p, m = turn(plus, minus, angles - step * N1 * s)
                rr[0, r, s * classes : (s + 1) * classes, :] = p
                rr[1, r, s * classes : (s + 1) * classes, :] = m
        norm = jnp.broadcast_to(jnp.sum(square, axis=1, keepdims=True), (classes, cols))
        k = lax.broadcasted_iota(jnp.int32, (classes, cols), 0)
        lane = lax.broadcasted_iota(jnp.int32, (classes, cols), 1)
        norm = jnp.sum(jnp.where(lane % classes == k, norm, 0.0), axis=0, keepdims=True)
        for i in range(2):
            left = jnp.concatenate([x[i, r] for r in range(cycles)], axis=1)
            right = jnp.concatenate([rr[i, r] for r in range(cycles)], axis=1)
            part = lax.dot_general(
                left, right, (((1,), (1,)), ((), ())), preferred_element_type=F32
            )
            if i == 0:
                part = part - norm
            for t in range(cols // LANES):
                tile = part[:, t * LANES : (t + 1) * LANES].astype(BF)
                at = slice(i * rows, (i + 1) * rows)
                out_ref[:, first + t, at, :] = tile.reshape(nb, rows, LANES)

    out_shape = jax.ShapeDtypeStruct if before else VM
    return pl.pallas_call(
        body,
        out_shape=out_shape((nb, tiles, 2 * rows, LANES), BF),
        in_specs=[spec()] * (1 + len(refs) + len(before)),
        out_specs=spec(),
        scratch_shapes=[
            VM((2, classes * cycles, LANES), F32),
            VM((2, cycles, cols, LANES), BF),
            VM((2, cycles, total, LANES), BF),
        ],
        compiler_params=params(),
        name="correlate",
    )(here(images), *[here(r) for r in (*refs, *before)])


def local_softmax(me, scores, precision, others):
    nb, tiles, rows, _ = scores.shape
    cols = tiles * LANES
    half = rows // 2
    group = half // N1
    own = group // 2

    def across(op, x):
        pieces = [x[i * group : (i + 1) * group] for i in range(N1)]
        return op(op(pieces[0], pieces[1]), op(pieces[2], pieces[3]))

    def body(me_ref, x_ref, a_ref, b_ref, e_ref, stat_ref):
        total = x_ref[0].astype(F32)
        for i in range(1, nb):
            total = total + x_ref[i].astype(F32)
        total = jnp.concatenate([total[t] for t in range(tiles)], axis=1)
        plus, minus = total[:half], total[half:]
        row = lax.broadcasted_iota(jnp.int32, (own, own), 0)
        col = lax.broadcasted_iota(jnp.int32, (own, own), 1)
        scale = [
            jnp.sum(jnp.where(row == col, ref[pl.ds(me_ref[0], 1), :], 0.0), axis=1, keepdims=True)
            for ref in (a_ref, b_ref)
        ]
        scale = jnp.concatenate(scale * N1, axis=0) * 0.5
        near, far = scale * (plus + minus), scale * (plus - minus)
        top = jnp.max(jnp.maximum(near, far), axis=1, keepdims=True)
        top = across(jnp.maximum, top)
        tops = jnp.concatenate([top] * N1, axis=0)
        near, far = jnp.exp(near - tops), jnp.exp(far - tops)
        e_ref[0] = near
        e_ref[1] = far
        amount = across(jnp.add, jnp.sum(near + far, axis=1, keepdims=True))
        stat_ref[0] = jnp.broadcast_to(top, (group, LANES))
        stat_ref[1] = jnp.broadcast_to(amount, (group, LANES))

    return pl.pallas_call(
        body,
        out_shape=(VM((2, half, cols), F32), VM((2, group, LANES), F32)),
        in_specs=[spec(pltpu.SMEM), spec(), spec(), spec()],
        out_specs=(spec(), spec()),
        compiler_params=params(),
        name="local_softmax",
    )(me, here(scores), here(precision), here(others))


def normalize(e, mine, theirs, copies):
    _, half, cols = e.shape
    group = mine.shape[1]

    def body(e_ref, a_ref, b_ref, out_ref):
        def flipped(x):
            return jnp.concatenate([x[group // 2 :], x[: group // 2]], axis=0)

        top_a, sum_a = a_ref[0], a_ref[1]
        top_b, sum_b = flipped(b_ref[0]), flipped(b_ref[1])
        top = jnp.maximum(top_a, top_b)
        part = jnp.exp(top_a - top)
        factor = part / (sum_a * part + sum_b * jnp.exp(top_b - top))
        factor = jnp.concatenate([jnp.concatenate([factor] * N1, axis=0)] * (cols // LANES), axis=1)
        near, far = e_ref[0] * factor, e_ref[1] * factor
        w = jnp.concatenate([near + far, near - far], axis=0).T.astype(BF)
        for c in range(copies):
            out_ref[c] = w

    return pl.pallas_call(
        body,
        out_shape=VM((copies, cols, 2 * half), BF),
        in_specs=[spec(), spec(), spec()],
        out_specs=spec(),
        compiler_params=params(),
        name="normalize",
    )(here(e), here(mine), here(theirs))


def accumulate(me, weights, images, ny, nz, step):
    owners = ny * nz
    nb, cols, lanes = weights.shape
    cycles = images.shape[1]
    classes = cols // N2
    per = LANES // N2
    pair = 2 * LANES

    def body(me_ref, w_ref, x_ref, out_ref, scr, x):
        for r in range(cycles):
            x[0, r], x[1, r] = rotate_images(x_ref, r, nb, step)
        left = lax.broadcasted_iota(jnp.int32, (cols, lanes), 1) < lanes // 2
        near, far = [], []
        for j in range(0, nb, 2):
            a, b = w_ref[j], w_ref[j + 1]
            near.append(jnp.where(left, a, pltpu.roll(b, lanes // 2, 1)))
            far.append(jnp.where(left, pltpu.roll(a, lanes // 2, 1), b))
        w = [jnp.concatenate(v, axis=1) for v in (near, far)]
        for c in range(0, cycles, 2):
            spread = []
            for i in range(2):
                both = jnp.concatenate([x[i, c], x[i, c + 1]], axis=1)
                spread.append(jnp.dot(w[i], both, preferred_element_type=F32))
            for d in range(2):
                plus = minus = None
                for s in range(N2):
                    p, m = (
                        jnp.concatenate(
                            [
                                v[t + s * per : t + (s + 1) * per, d * LANES : (d + 1) * LANES]
                                for t in range(0, cols, LANES)
                            ],
                            axis=0,
                        )
                        for v in spread
                    )
                    p, m = turn(p, m, step * N1 * s)
                    plus = plus + p if s else p
                    minus = minus + m if s else m
                rows = pl.ds(c + d, classes, stride=cycles)
                scr.at[0][rows, :] = 0.5 * (plus + minus)
                scr.at[1][rows, :] = 0.5 * (plus - minus)
        whole = jnp.concatenate([scr[0], scr[1]], axis=1)
        whole = whole.reshape(out_ref.shape).astype(BF)
        place = me_ref[0] // 2
        y, z = place // nz, place % nz
        for slot in range(owners):
            dz, dy = FAR_FIRST[slot // ny], slot % ny
            out_ref[(y ^ dy) * nz + (z ^ dz)] = whole[slot]

    return pl.pallas_call(
        body,
        out_shape=VM((owners, classes // owners * cycles, pair), BF),
        in_specs=[spec(pltpu.SMEM), spec(), spec()],
        out_specs=spec(),
        scratch_shapes=[
            VM((2, classes * cycles, LANES), F32),
            VM((2, cycles, N1 * images.shape[2], LANES), BF),
        ],
        compiler_params=params(),
        name="accumulate",
    )(me, here(weights), here(images))


def add_up(parts):
    def body(x_ref, out_ref):
        total = x_ref[0].astype(F32)
        for i in range(1, parts.shape[0]):
            total = total + x_ref[i].astype(F32)
        out_ref[...] = total

    return pl.pallas_call(
        body,
        out_shape=jax.ShapeDtypeStruct(parts.shape[1:], F32),
        in_specs=[spec()],
        out_specs=spec(),
        compiler_params=params(),
        name="add_up",
    )(here(parts))


def solution(mesh):
    dom, nb = mesh.devices.shape
    ny, nz = 2, dom // 4
    view = Mesh(mesh.devices.reshape(ny, nz, 2, nb), ("yh", "z", "core", "blk"))
    swap = [(0, 1), (1, 0)]

    def shards(images, ref_store, block_owner, class_gain, precision):
        particles, cycles, angles = images.shape
        kb = ref_store.shape[2]
        rot = angles // (2 * N1 * N2)
        half = particles // nb
        other = lax.ppermute(images, "core", swap)
        other_precision = lax.ppermute(precision, "core", swap)
        y, z = lax.axis_index("yh"), lax.axis_index("z")
        me = ((y * nz + z) * 2 + lax.axis_index("core"))[None].astype(jnp.int32)
        j = lax.axis_index("blk")[None].astype(jnp.int32)
        mine = pick_block(me, block_owner, class_gain, ref_store[0])
        theirs = lax.ppermute(mine, "yh", swap)
        halves = halve_images(images, other, nb)
        refs = [pair_up(mine, theirs, halves, other_precision)]
        for d in FAR_FIRST[1:]:
            ring = [(i, i ^ d) for i in range(nz)]
            refs.append(lax.ppermute(refs[0], "z", ring))
        early = correlate(halves, refs[:2], nb, rot)
        scores = correlate(halves, refs[2:], nb, rot, (early,))
        scores = lax.all_to_all(scores, "blk", 0, 0)
        e, stats = local_softmax(
            j, scores, precision.reshape(nb, half), other_precision.reshape(nb, half)
        )
        theirs = lax.ppermute(stats, "core", swap)
        weights = normalize(e, stats, theirs, nb)
        weights = lax.all_to_all(weights, "blk", 0, 0)
        totals = accumulate(me, weights, halves, ny, nz, rot)
        totals = lax.all_to_all(totals, ("yh", "z"), 0, 0)
        return add_up(totals).reshape(1, 1, kb, cycles, angles)

    dom_axes = ("yh", "z", "core")
    return jax.shard_map(
        shards,
        mesh=view,
        in_specs=(
            P(dom_axes, "blk", None),
            P(dom_axes, None, None, "blk", None),
            P(),
            P(),
            P(dom_axes),
        ),
        out_specs=P(dom_axes, None, None, "blk", None),
        check_vma=False,
    )
```

```python
import jax
import jax.numpy as jnp
from jax import lax
from jax.experimental import pallas as pl
from jax.experimental.pallas import tpu as pltpu
from jax.sharding import Mesh, PartitionSpec as P


BF = jnp.bfloat16
F32 = jnp.float32
VM = pltpu.VMEM
LANES = 128
N1 = 4
N2 = 8
PARTNERS = (0, 1, 3, 2)


def spec(space=VM):
    return pl.BlockSpec(memory_space=space)


def params(mib=24):
    return pltpu.CompilerParams(vmem_limit_bytes=mib * 1024 * 1024)


def here(x):
    return pltpu.with_memory_space_constraint(x, VM)


def away(x):
    return pltpu.with_memory_space_constraint(x, pltpu.HBM)


def fill(scr, value):
    for h in range(scr.shape[0]):
        scr[h] = value[:, h * LANES : (h + 1) * LANES]


def take_cycle(scr, r, rows, cycles):
    return [scr.at[h][pl.ds(r, rows, stride=cycles), :] for h in range(2)]


def narrow(x):
    wide = x * 65537.0
    return wide - (wide - x)


def narrow_sum(x):
    near = narrow(x)
    lane = lax.broadcasted_iota(jnp.int32, x.shape, 1)
    rest = jnp.sum(x - near, axis=1, keepdims=True)
    return jnp.where(lane == 0, near + rest, near)


def turn(plus, minus, t):
    t = t % (2 * LANES)
    if t == 0:
        return plus, minus
    if t >= LANES:
        return turn(plus, -minus, t - LANES)
    lane = lax.broadcasted_iota(jnp.int32, minus.shape, 1)
    minus = pltpu.roll(minus, t, 1)
    return pltpu.roll(plus, t, 1), jnp.where(lane < t, -minus, minus)


def pick_block(me, block_owner, class_gain, ref_store):
    nblk, kb, cycles, angles = ref_store.shape

    def body(me_ref, owner_ref, gain_ref, store_ref, out_ref, buf, sem):
        block = jnp.int32(0)
        for b in range(nblk):
            block = jnp.where(owner_ref[b] == me_ref[0], jnp.int32(b), block)
        copy = pltpu.make_async_copy(store_ref.at[block], buf, sem)
        copy.start()
        copy.wait()
        for i in range(kb):
            piece = (buf[i].astype(F32) * gain_ref[block * kb + i]).astype(BF).astype(F32)
            a, b = piece[:, :LANES], piece[:, LANES:]
            piece = jnp.concatenate([narrow_sum(a + b), narrow(a - b)], axis=1).astype(BF)
            out_ref[i * cycles : (i + 1) * cycles, :] = piece

    return pl.pallas_call(
        body,
        out_shape=VM((kb * cycles, angles), BF),
        in_specs=[spec(pltpu.SMEM), spec(pltpu.SMEM), spec(pltpu.SMEM), spec(pltpu.HBM)],
        out_specs=spec(),
        scratch_shapes=[VM((kb, cycles, angles), BF), pltpu.SemaphoreType.DMA],
        compiler_params=params(60),
        name="pick_block",
    )(me, block_owner, class_gain, away(ref_store))


def halve_images(own, other, nb):
    particles, cycles, angles = own.shape
    per = particles // nb

    def body(own_ref, other_ref, out_ref, a_scr, b_scr):
        fill(a_scr, own_ref[...].astype(F32).reshape(particles * cycles, angles))
        fill(b_scr, other_ref[...].astype(F32).reshape(particles * cycles, angles))
        for r in range(cycles):
            a = take_cycle(a_scr, r, particles, cycles)
            b = take_cycle(b_scr, r, particles, cycles)
            for i, op in enumerate((jnp.add, jnp.subtract)):
                x, y = op(a[0], a[1]), op(b[0], b[1])
                both = [v.reshape(nb, per, LANES) for v in (x, y)]
                both = jnp.concatenate(both, axis=1).reshape(2 * particles, LANES)
                out_ref[i, r] = narrow(both).astype(BF)

    return pl.pallas_call(
        body,
        out_shape=VM((2, cycles, 2 * particles, LANES), BF),
        in_specs=[spec(), spec()],
        out_specs=spec(),
        scratch_shapes=[VM((2, particles * cycles, LANES), F32)] * 2,
        compiler_params=params(),
        name="halve_images",
    )(own, here(other))


def pair_up(mine, theirs, *others):
    def body(a_ref, b_ref, *refs):
        out_ref = refs[-1]
        out_ref[0] = a_ref[...]
        out_ref[1] = b_ref[...]

    return pl.pallas_call(
        body,
        out_shape=VM((2,) + mine.shape, BF),
        in_specs=[spec()] * (2 + len(others)),
        out_specs=spec(),
        compiler_params=params(),
        name="pair_up",
    )(here(mine), here(theirs), *[here(o) for o in others])


def rotate_images(x_ref, r, nb, step):
    plus, minus = x_ref[0, r], x_ref[1, r]
    per = plus.shape[0] // nb
    turned = [turn(plus, minus, step * s) for s in range(N1)]
    return [
        jnp.concatenate(
            [t[i][j * per : (j + 1) * per] for j in range(nb) for t in turned], axis=0
        )
        for i in range(2)
    ]


def correlate(images, refs, nb, step, tile, tiles, before=()):
    _, cycles, particles, _ = images.shape
    total = N1 * particles
    rows = total // nb
    near, far = refs[0].shape[:2]
    classes = len(refs) * near * far // cycles
    cols = N2 * classes
    angles = 2 * LANES

    def body(x_ref, *args):
        r_refs, (out_ref, scr, rr, x, o, sems) = args[: len(refs)], args[-6:]
        copies = []
        blocks = [r_ref[d].astype(F32) for r_ref in r_refs for d in range(near)]
        fill(scr, jnp.concatenate(blocks, axis=0))
        square = jnp.zeros((classes, LANES), F32)
        for r in range(cycles):
            plus, minus = take_cycle(scr, r, classes, cycles)
            square = square + 0.5 * (plus * plus + minus * minus)
            plus, minus = plus.astype(BF), minus.astype(BF)
            x[0, r], x[1, r] = rotate_images(x_ref, r, nb, step)
            for s in range(N2):
                p, m = turn(plus, minus, angles - step * N1 * s)
                rr[0, r, s * classes : (s + 1) * classes, :] = p
                rr[1, r, s * classes : (s + 1) * classes, :] = m
        norm = jnp.broadcast_to(jnp.sum(square, axis=1, keepdims=True), (classes, cols))
        k = lax.broadcasted_iota(jnp.int32, (classes, cols), 0)
        lane = lax.broadcasted_iota(jnp.int32, (classes, cols), 1)
        norm = jnp.sum(jnp.where(lane % classes == k, norm, 0.0), axis=0, keepdims=True)
        for i in range(2):
            left = jnp.concatenate([x[i, r] for r in range(cycles)], axis=1)
            right = jnp.concatenate([rr[i, r] for r in range(cycles)], axis=1)
            part = lax.dot_general(
                left, right, (((1,), (1,)), ((), ())), preferred_element_type=F32
            )
            if i == 0:
                part = part - norm
            at = slice(i * rows, (i + 1) * rows)
            o[:, at, :] = part.astype(BF).reshape(nb, rows, LANES)
            copy = pltpu.make_async_copy(o.at[:, at, :], out_ref.at[:, tile, at, :], sems.at[i])
            copy.start()
            copies.append(copy)
        for copy in copies:
            copy.wait()

    return pl.pallas_call(
        body,
        out_shape=pltpu.HBM((nb, tiles, 2 * rows, LANES), BF),
        in_specs=[spec()] * (1 + len(refs)) + [spec(pltpu.HBM)] * len(before),
        out_specs=spec(pltpu.HBM),
        input_output_aliases={1 + len(refs): 0} if before else {},
        scratch_shapes=[
            VM((2, classes * cycles, LANES), F32),
            VM((2, cycles, cols, LANES), BF),
            VM((2, cycles, total, LANES), BF),
            VM((nb, 2 * rows, LANES), BF),
            pltpu.SemaphoreType.DMA((2,)),
        ],
        compiler_params=params(),
        name="correlate",
    )(here(images), *[here(r) for r in refs], *[away(b) for b in before])


def local_softmax(me, scores, precision, others):
    nb, tiles, rows, _ = scores.shape
    cols = tiles * LANES
    half = rows // 2
    group = half // N1
    own = group // 2

    def across(op, x):
        pieces = [x[i * group : (i + 1) * group] for i in range(N1)]
        return op(op(pieces[0], pieces[1]), op(pieces[2], pieces[3]))

    def body(me_ref, x_ref, a_ref, b_ref, e_ref, stat_ref):
        total = x_ref[0].astype(F32)
        for i in range(1, nb):
            total = total + x_ref[i].astype(F32)
        total = jnp.concatenate([total[t] for t in range(tiles)], axis=1)
        plus, minus = total[:half], total[half:]
        row = lax.broadcasted_iota(jnp.int32, (own, own), 0)
        col = lax.broadcasted_iota(jnp.int32, (own, own), 1)
        scale = [
            jnp.sum(jnp.where(row == col, ref[pl.ds(me_ref[0], 1), :], 0.0), axis=1, keepdims=True)
            for ref in (a_ref, b_ref)
        ]
        scale = jnp.concatenate(scale * N1, axis=0) * 0.5
        near, far = scale * (plus + minus), scale * (plus - minus)
        top = jnp.max(jnp.maximum(near, far), axis=1, keepdims=True)
        top = across(jnp.maximum, top)
        tops = jnp.concatenate([top] * N1, axis=0)
        near, far = jnp.exp(near - tops), jnp.exp(far - tops)
        e_ref[0] = near
        e_ref[1] = far
        amount = across(jnp.add, jnp.sum(near + far, axis=1, keepdims=True))
        stat_ref[0] = jnp.broadcast_to(top, (group, LANES))
        stat_ref[1] = jnp.broadcast_to(amount, (group, LANES))

    return pl.pallas_call(
        body,
        out_shape=(VM((2, half, cols), F32), VM((2, group, LANES), F32)),
        in_specs=[spec(pltpu.SMEM), spec(), spec(), spec()],
        out_specs=(spec(), spec()),
        compiler_params=params(),
        name="local_softmax",
    )(me, here(scores), here(precision), here(others))


def normalize(e, mine, theirs, copies):
    _, half, cols = e.shape
    group = mine.shape[1]

    def body(e_ref, a_ref, b_ref, out_ref):
        def flipped(x):
            return jnp.concatenate([x[group // 2 :], x[: group // 2]], axis=0)

        top_a, sum_a = a_ref[0], a_ref[1]
        top_b, sum_b = flipped(b_ref[0]), flipped(b_ref[1])
        top = jnp.maximum(top_a, top_b)
        part = jnp.exp(top_a - top)
        factor = part / (sum_a * part + sum_b * jnp.exp(top_b - top))
        factor = jnp.concatenate([jnp.concatenate([factor] * N1, axis=0)] * (cols // LANES), axis=1)
        near, far = e_ref[0] * factor, e_ref[1] * factor
        w = jnp.concatenate([near + far, near - far], axis=0).T.astype(BF)
        for c in range(copies):
            out_ref[c] = w

    return pl.pallas_call(
        body,
        out_shape=VM((copies, cols, 2 * half), BF),
        in_specs=[spec(), spec(), spec()],
        out_specs=spec(),
        compiler_params=params(),
        name="normalize",
    )(here(e), here(mine), here(theirs))


def accumulate(me, weights, images, ny, nz, step):
    owners = ny * nz
    nb, cols, lanes = weights.shape
    cycles = images.shape[1]
    classes = cols // N2
    per = LANES // N2
    pair = 2 * LANES

    def body(me_ref, w_ref, x_ref, out_ref, scr, x):
        for r in range(cycles):
            x[0, r], x[1, r] = rotate_images(x_ref, r, nb, step)
        left = lax.broadcasted_iota(jnp.int32, (cols, lanes), 1) < lanes // 2
        near, far = [], []
        for j in range(0, nb, 2):
            a, b = w_ref[j], w_ref[j + 1]
            near.append(jnp.where(left, a, pltpu.roll(b, lanes // 2, 1)))
            far.append(jnp.where(left, pltpu.roll(a, lanes // 2, 1), b))
        w = [jnp.concatenate(v, axis=1) for v in (near, far)]
        for c in range(0, cycles, 2):
            spread = []
            for i in range(2):
                both = jnp.concatenate([x[i, c], x[i, c + 1]], axis=1)
                spread.append(jnp.dot(w[i], both, preferred_element_type=F32))
            for d in range(2):
                plus = minus = None
                for s in range(N2):
                    p, m = (
                        jnp.concatenate(
                            [
                                v[t + s * per : t + (s + 1) * per, d * LANES : (d + 1) * LANES]
                                for t in range(0, cols, LANES)
                            ],
                            axis=0,
                        )
                        for v in spread
                    )
                    p, m = turn(p, m, step * N1 * s)
                    plus = plus + p if s else p
                    minus = minus + m if s else m
                rows = pl.ds(c + d, classes, stride=cycles)
                scr.at[0][rows, :] = 0.5 * (plus + minus)
                scr.at[1][rows, :] = 0.5 * (plus - minus)
        whole = jnp.concatenate([scr[0], scr[1]], axis=1)
        whole = whole.reshape(out_ref.shape).astype(BF)
        place = me_ref[0] // 2
        y, z = place // nz, place % nz
        for slot in range(owners):
            dz, dy = PARTNERS[slot // ny], slot % ny
            out_ref[(y ^ dy) * nz + (z ^ dz)] = whole[slot]

    return pl.pallas_call(
        body,
        out_shape=VM((owners, classes // owners * cycles, pair), BF),
        in_specs=[spec(pltpu.SMEM), spec(), spec()],
        out_specs=spec(),
        scratch_shapes=[
            VM((2, classes * cycles, LANES), F32),
            VM((2, cycles, N1 * images.shape[2], LANES), BF),
        ],
        compiler_params=params(),
        name="accumulate",
    )(me, here(weights), here(images))


def add_up(parts):
    def body(x_ref, out_ref):
        total = x_ref[0].astype(F32)
        for i in range(1, parts.shape[0]):
            total = total + x_ref[i].astype(F32)
        out_ref[...] = total

    return pl.pallas_call(
        body,
        out_shape=jax.ShapeDtypeStruct(parts.shape[1:], F32),
        in_specs=[spec()],
        out_specs=spec(),
        compiler_params=params(),
        name="add_up",
    )(here(parts))


def solution(mesh):
    dom, nb = mesh.devices.shape
    ny, nz = 2, dom // 4
    view = Mesh(mesh.devices.reshape(ny, nz, 2, nb), ("yh", "z", "core", "blk"))
    swap = [(0, 1), (1, 0)]

    def shards(images, ref_store, block_owner, class_gain, precision):
        particles, cycles, angles = images.shape
        kb = ref_store.shape[2]
        rot = angles // (2 * N1 * N2)
        half = particles // nb
        other = lax.ppermute(images, "core", swap)
        other_precision = lax.ppermute(precision, "core", swap)
        y, z = lax.axis_index("yh"), lax.axis_index("z")
        me = ((y * nz + z) * 2 + lax.axis_index("core"))[None].astype(jnp.int32)
        j = lax.axis_index("blk")[None].astype(jnp.int32)
        mine = pick_block(me, block_owner, class_gain, ref_store[0])
        theirs = lax.ppermute(mine, "yh", swap)
        halves = halve_images(images, other, nb)
        refs = [pair_up(mine, theirs, halves, other_precision)]
        for d in PARTNERS[1:]:
            ring = [(i, i ^ d) for i in range(nz)]
            refs.append(lax.ppermute(refs[0], "z", ring))
        scores = correlate(halves, refs[:2], nb, rot, 0, 2)
        scores = correlate(halves, refs[2:], nb, rot, 1, 2, (scores,))
        scores = lax.all_to_all(scores, "blk", 0, 0)
        e, stats = local_softmax(
            j, scores, precision.reshape(nb, half), other_precision.reshape(nb, half)
        )
        theirs = lax.ppermute(stats, "core", swap)
        weights = normalize(e, stats, theirs, nb)
        weights = lax.all_to_all(weights, "blk", 0, 0)
        totals = accumulate(me, weights, halves, ny, nz, rot)
        totals = lax.all_to_all(totals, ("yh", "z"), 0, 0)
        return add_up(totals).reshape(1, 1, kb, cycles, angles)

    dom_axes = ("yh", "z", "core")
    return jax.shard_map(
        shards,
        mesh=view,
        in_specs=(
            P(dom_axes, "blk", None),
            P(dom_axes, None, None, "blk", None),
            P(),
            P(),
            P(dom_axes),
        ),
        out_specs=P(dom_axes, None, None, "blk", None),
        check_vma=False,
    )
```

```python
import jax
import jax.numpy as jnp
from jax import lax
from jax.experimental import pallas as pl
from jax.experimental.pallas import tpu as pltpu
from jax.sharding import Mesh, PartitionSpec as P


BF = jnp.bfloat16
F32 = jnp.float32
VM = pltpu.VMEM
LANES = 128
N1 = 4
N2 = 8
PARTNERS = (0, 1, 3, 2)


def spec(space=VM):
    return pl.BlockSpec(memory_space=space)


def params(mib=24):
    return pltpu.CompilerParams(vmem_limit_bytes=mib * 1024 * 1024)


def here(x):
    return pltpu.with_memory_space_constraint(x, VM)


def away(x):
    return pltpu.with_memory_space_constraint(x, pltpu.HBM)


def fill(scr, value):
    for h in range(scr.shape[0]):
        scr[h] = value[:, h * LANES : (h + 1) * LANES]


def take_cycle(scr, r, rows, cycles):
    return [scr.at[h][pl.ds(r, rows, stride=cycles), :] for h in range(2)]


def narrow(x):
    wide = x * 65537.0
    return wide - (wide - x)


def narrow_sum(x):
    near = narrow(x)
    lane = lax.broadcasted_iota(jnp.int32, x.shape, 1)
    rest = jnp.sum(x - near, axis=1, keepdims=True)
    return jnp.where(lane == 0, near + rest, near)


def turn(plus, minus, t):
    t = t % (2 * LANES)
    if t == 0:
        return plus, minus
    if t >= LANES:
        return turn(plus, -minus, t - LANES)
    lane = lax.broadcasted_iota(jnp.int32, minus.shape, 1)
    minus = pltpu.roll(minus, t, 1)
    return pltpu.roll(plus, t, 1), jnp.where(lane < t, -minus, minus)


def pick_block(me, nb, block_owner, class_gain, ref_store):
    nblk, kb, cycles, angles = ref_store.shape

    def body(me_ref, owner_ref, gain_ref, store_ref, out_ref, buf, sem):
        block = jnp.int32(0)
        for b in range(nblk):
            block = jnp.where(owner_ref[b] == me_ref[0] // nb, jnp.int32(b), block)
        copy = pltpu.make_async_copy(store_ref.at[block], buf, sem)
        copy.start()
        copy.wait()
        for i in range(kb):
            piece = (buf[i].astype(F32) * gain_ref[block * kb + i]).astype(BF).astype(F32)
            a, b = piece[:, :LANES], piece[:, LANES:]
            piece = jnp.concatenate([narrow_sum(a + b), narrow(a - b)], axis=1).astype(BF)
            out_ref[i * cycles : (i + 1) * cycles, :] = piece

    return pl.pallas_call(
        body,
        out_shape=VM((kb * cycles, angles), BF),
        in_specs=[spec(pltpu.SMEM), spec(pltpu.SMEM), spec(pltpu.SMEM), spec(pltpu.HBM)],
        out_specs=spec(),
        scratch_shapes=[VM((kb, cycles, angles), BF), pltpu.SemaphoreType.DMA],
        compiler_params=params(60),
        name="pick_block",
    )(me, block_owner, class_gain, away(ref_store))


def halve_images(own, other, nb):
    particles, cycles, angles = own.shape
    per = particles // nb

    def body(own_ref, other_ref, out_ref, a_scr, b_scr):
        fill(a_scr, own_ref[...].astype(F32).reshape(particles * cycles, angles))
        fill(b_scr, other_ref[...].astype(F32).reshape(particles * cycles, angles))
        for r in range(cycles):
            a = take_cycle(a_scr, r, particles, cycles)
            b = take_cycle(b_scr, r, particles, cycles)
            for i, op in enumerate((jnp.add, jnp.subtract)):
                x, y = op(a[0], a[1]), op(b[0], b[1])
                both = [v.reshape(nb, per, LANES) for v in (x, y)]
                both = jnp.concatenate(both, axis=1).reshape(2 * particles, LANES)
                out_ref[i, r] = narrow(both).astype(BF)

    return pl.pallas_call(
        body,
        out_shape=VM((2, cycles, 2 * particles, LANES), BF),
        in_specs=[spec(), spec()],
        out_specs=spec(),
        scratch_shapes=[VM((2, particles * cycles, LANES), F32)] * 2,
        compiler_params=params(),
        name="halve_images",
    )(own, here(other))


def pair_up(mine, theirs, *others):
    def body(a_ref, b_ref, *refs):
        out_ref = refs[-1]
        out_ref[0] = a_ref[...]
        out_ref[1] = b_ref[...]

    return pl.pallas_call(
        body,
        out_shape=VM((2,) + mine.shape, BF),
        in_specs=[spec()] * (2 + len(others)),
        out_specs=spec(),
        compiler_params=params(),
        name="pair_up",
    )(here(mine), here(theirs), *[here(o) for o in others])


def rotate_images(x_ref, r, nb, step):
    plus, minus = x_ref[0, r], x_ref[1, r]
    per = plus.shape[0] // nb
    turned = [turn(plus, minus, step * s) for s in range(N1)]
    return [
        jnp.concatenate(
            [t[i][j * per : (j + 1) * per] for j in range(nb) for t in turned], axis=0
        )
        for i in range(2)
    ]


def correlate(images, refs, nb, step, before=()):
    _, cycles, particles, _ = images.shape
    total = N1 * particles
    rows = total // nb
    near, far = refs[0].shape[:2]
    classes = len(refs) * near * far // cycles
    cols = N2 * classes
    angles = 2 * LANES

    def body(x_ref, *args):
        r_refs, (out_ref, scr, rr, x) = args[: len(refs)], args[-4:]
        for t, b_ref in enumerate(args[len(refs) : -4]):
            out_ref[:, t] = b_ref[:, 0]
        blocks = [r_ref[d].astype(F32) for r_ref in r_refs for d in range(near)]
        fill(scr, jnp.concatenate(blocks, axis=0))
        square = jnp.zeros((classes, LANES), F32)
        for r in range(cycles):
            plus, minus = take_cycle(scr, r, classes, cycles)
            square = square + 0.5 * (plus * plus + minus * minus)
            plus, minus = plus.astype(BF), minus.astype(BF)
            x[0, r], x[1, r] = rotate_images(x_ref, r, nb, step)
            for s in range(N2):
                p, m = turn(plus, minus, angles - step * N1 * s)
                rr[0, r, s * classes : (s + 1) * classes, :] = p
                rr[1, r, s * classes : (s + 1) * classes, :] = m
        norm = jnp.broadcast_to(jnp.sum(square, axis=1, keepdims=True), (classes, cols))
        k = lax.broadcasted_iota(jnp.int32, (classes, cols), 0)
        lane = lax.broadcasted_iota(jnp.int32, (classes, cols), 1)
        norm = jnp.sum(jnp.where(lane % classes == k, norm, 0.0), axis=0, keepdims=True)
        for i in range(2):
            left = jnp.concatenate([x[i, r] for r in range(cycles)], axis=1)
            right = jnp.concatenate([rr[i, r] for r in range(cycles)], axis=1)
            part = lax.dot_general(
                left, right, (((1,), (1,)), ((), ())), preferred_element_type=F32
            )
            if i == 0:
                part = part - norm
            at = slice(i * rows, (i + 1) * rows)
            out_ref[:, len(before), at, :] = part.astype(BF).reshape(nb, rows, LANES)

    return pl.pallas_call(
        body,
        out_shape=VM((nb, 1 + len(before), 2 * rows, LANES), BF),
        in_specs=[spec()] * (1 + len(refs) + len(before)),
        out_specs=spec(),
        scratch_shapes=[
            VM((2, classes * cycles, LANES), F32),
            VM((2, cycles, cols, LANES), BF),
            VM((2, cycles, total, LANES), BF),
        ],
        compiler_params=params(),
        name="correlate",
    )(here(images), *[here(r) for r in (*refs, *before)])


def local_softmax(me, scores, precision, others):
    nb, tiles, rows, _ = scores.shape
    cols = tiles * LANES
    half = rows // 2
    group = half // N1
    own = group // 2

    def across(op, x):
        pieces = [x[i * group : (i + 1) * group] for i in range(N1)]
        return op(op(pieces[0], pieces[1]), op(pieces[2], pieces[3]))

    def body(me_ref, x_ref, a_ref, b_ref, e_ref, stat_ref):
        total = x_ref[0].astype(F32)
        for i in range(1, nb):
            total = total + x_ref[i].astype(F32)
        total = jnp.concatenate([total[t] for t in range(tiles)], axis=1)
        plus, minus = total[:half], total[half:]
        wide = (own, nb * own)
        row = lax.broadcasted_iota(jnp.int32, wide, 0) + me_ref[0] % nb * own
        mine = row == lax.broadcasted_iota(jnp.int32, wide, 1)
        scale = [
            jnp.sum(jnp.where(mine, ref[...], 0.0), axis=1, keepdims=True)
            for ref in (a_ref, b_ref)
        ]
        scale = jnp.concatenate(scale * N1, axis=0) * 0.5
        near, far = scale * (plus + minus), scale * (plus - minus)
        top = jnp.max(jnp.maximum(near, far), axis=1, keepdims=True)
        top = across(jnp.maximum, top)
        tops = jnp.concatenate([top] * N1, axis=0)
        near, far = jnp.exp(near - tops), jnp.exp(far - tops)
        e_ref[0] = near
        e_ref[1] = far
        amount = across(jnp.add, jnp.sum(near + far, axis=1, keepdims=True))
        stat_ref[0] = jnp.broadcast_to(top, (group, LANES))
        stat_ref[1] = jnp.broadcast_to(amount, (group, LANES))

    return pl.pallas_call(
        body,
        out_shape=(VM((2, half, cols), F32), VM((2, group, LANES), F32)),
        in_specs=[spec(pltpu.SMEM), spec(), spec(), spec()],
        out_specs=(spec(), spec()),
        compiler_params=params(),
        name="local_softmax",
    )(me, here(scores), here(precision), here(others))


def normalize(e, mine, theirs, copies):
    _, half, cols = e.shape
    group = mine.shape[1]

    def body(e_ref, a_ref, b_ref, out_ref):
        def flipped(x):
            return jnp.concatenate([x[group // 2 :], x[: group // 2]], axis=0)

        top_a, sum_a = a_ref[0], a_ref[1]
        top_b, sum_b = flipped(b_ref[0]), flipped(b_ref[1])
        top = jnp.maximum(top_a, top_b)
        part = jnp.exp(top_a - top)
        factor = part / (sum_a * part + sum_b * jnp.exp(top_b - top))
        factor = jnp.concatenate([jnp.concatenate([factor] * N1, axis=0)] * (cols // LANES), axis=1)
        near, far = e_ref[0] * factor, e_ref[1] * factor
        w = jnp.concatenate([near + far, near - far], axis=0).T.astype(BF)
        for c in range(copies):
            out_ref[c] = w

    return pl.pallas_call(
        body,
        out_shape=VM((copies, cols, 2 * half), BF),
        in_specs=[spec(), spec(), spec()],
        out_specs=spec(),
        compiler_params=params(),
        name="normalize",
    )(here(e), here(mine), here(theirs))


def accumulate(me, weights, images, ny, nz, step):
    owners = ny * nz
    nb, cols, lanes = weights.shape
    cycles = images.shape[1]
    classes = cols // N2
    per = LANES // N2
    pair = 2 * LANES

    def body(me_ref, w_ref, x_ref, out_ref, scr, x):
        for r in range(cycles):
            x[0, r], x[1, r] = rotate_images(x_ref, r, nb, step)
        left = lax.broadcasted_iota(jnp.int32, (cols, lanes), 1) < lanes // 2
        near, far = [], []
        for j in range(0, nb, 2):
            a, b = w_ref[j], w_ref[j + 1]
            near.append(jnp.where(left, a, pltpu.roll(b, lanes // 2, 1)))
            far.append(jnp.where(left, pltpu.roll(a, lanes // 2, 1), b))
        w = [jnp.concatenate(v, axis=1) for v in (near, far)]
        for c in range(0, cycles, 2):
            spread = []
            for i in range(2):
                both = jnp.concatenate([x[i, c], x[i, c + 1]], axis=1)
                spread.append(jnp.dot(w[i], both, preferred_element_type=F32))
            for d in range(2):
                plus = minus = None
                for s in range(N2):
                    p, m = (
                        jnp.concatenate(
                            [
                                v[t + s * per : t + (s + 1) * per, d * LANES : (d + 1) * LANES]
                                for t in range(0, cols, LANES)
                            ],
                            axis=0,
                        )
                        for v in spread
                    )
                    p, m = turn(p, m, step * N1 * s)
                    plus = plus + p if s else p
                    minus = minus + m if s else m
                rows = pl.ds(c + d, classes, stride=cycles)
                scr.at[0][rows, :] = 0.5 * (plus + minus)
                scr.at[1][rows, :] = 0.5 * (plus - minus)
        whole = jnp.concatenate([scr[0], scr[1]], axis=1)
        whole = whole.reshape(out_ref.shape).astype(BF)
        place = me_ref[0] // (2 * nb)
        y, z = place // nz, place % nz
        for slot in range(owners):
            dz, dy = PARTNERS[slot // ny], slot % ny
            out_ref[(y ^ dy) * nz + (z ^ dz)] = whole[slot]

    return pl.pallas_call(
        body,
        out_shape=VM((owners, classes // owners * cycles, pair), BF),
        in_specs=[spec(pltpu.SMEM), spec(), spec()],
        out_specs=spec(),
        scratch_shapes=[
            VM((2, classes * cycles, LANES), F32),
            VM((2, cycles, N1 * images.shape[2], LANES), BF),
        ],
        compiler_params=params(),
        name="accumulate",
    )(me, here(weights), here(images))


def add_up(parts):
    def body(x_ref, out_ref):
        total = x_ref[0].astype(F32)
        for i in range(1, parts.shape[0]):
            total = total + x_ref[i].astype(F32)
        out_ref[...] = total

    return pl.pallas_call(
        body,
        out_shape=jax.ShapeDtypeStruct(parts.shape[1:], F32),
        in_specs=[spec()],
        out_specs=spec(),
        compiler_params=params(),
        name="add_up",
    )(here(parts))


def solution(mesh):
    dom, nb = mesh.devices.shape
    ny, nz = 2, dom // 4
    view = Mesh(mesh.devices.reshape(ny, nz, 2, nb), ("yh", "z", "core", "blk"))
    swap = [(0, 1), (1, 0)]

    def shards(images, ref_store, block_owner, class_gain, precision):
        particles, cycles, angles = images.shape
        kb = ref_store.shape[2]
        rot = angles // (2 * N1 * N2)
        other = lax.ppermute(images, "core", swap)
        other_precision = lax.ppermute(precision, "core", swap)
        y, z = lax.axis_index("yh"), lax.axis_index("z")
        me = ((y * nz + z) * 2 + lax.axis_index("core")) * nb + lax.axis_index("blk")
        me = me[None].astype(jnp.int32)
        mine = pick_block(me, nb, block_owner, class_gain, ref_store[0])
        theirs = lax.ppermute(mine, "yh", swap)
        halves = halve_images(images, other, nb)
        refs = [pair_up(mine, theirs, halves, other_precision)]
        for d in PARTNERS[1:]:
            ring = [(i, i ^ d) for i in range(nz)]
            refs.append(lax.ppermute(refs[0], "z", ring))
        early = correlate(halves, refs[:2], nb, rot)
        scores = correlate(halves, refs[2:], nb, rot, (early,))
        scores = lax.all_to_all(scores, "blk", 0, 0)
        flat = (1, particles)
        e, stats = local_softmax(
            me, scores, precision.reshape(flat), other_precision.reshape(flat)
        )
        theirs = lax.ppermute(stats, "core", swap)
        weights = normalize(e, stats, theirs, nb)
        weights = lax.all_to_all(weights, "blk", 0, 0)
        totals = accumulate(me, weights, halves, ny, nz, rot)
        totals = lax.all_to_all(totals, ("yh", "z"), 0, 0)
        return add_up(totals).reshape(1, 1, kb, cycles, angles)

    dom_axes = ("yh", "z", "core")
    return jax.shard_map(
        shards,
        mesh=view,
        in_specs=(
            P(dom_axes, "blk", None),
            P(dom_axes, None, None, "blk", None),
            P(),
            P(),
            P(dom_axes),
        ),
        out_specs=P(dom_axes, None, None, "blk", None),
        check_vma=False,
    )
```

```python
import jax
import jax.numpy as jnp
from jax import lax
from jax.experimental import pallas as pl
from jax.experimental.pallas import tpu as pltpu
from jax.sharding import Mesh, PartitionSpec as P


BF = jnp.bfloat16
F32 = jnp.float32
VM = pltpu.VMEM
LANES = 128
N1 = 4
N2 = 8
PARTNERS = (0, 1, 3, 2)


def spec(space=VM):
    return pl.BlockSpec(memory_space=space)


def params(mib=24):
    return pltpu.CompilerParams(vmem_limit_bytes=mib * 1024 * 1024)


def here(x):
    return pltpu.with_memory_space_constraint(x, VM)


def away(x):
    return pltpu.with_memory_space_constraint(x, pltpu.HBM)


def fill(scr, value):
    for h in range(scr.shape[0]):
        scr[h] = value[:, h * LANES : (h + 1) * LANES]


def take_cycle(scr, r, rows, cycles):
    return [scr.at[h][pl.ds(r, rows, stride=cycles), :] for h in range(2)]


def narrow(x):
    wide = x * 65537.0
    return wide - (wide - x)


def narrow_sum(x):
    near = narrow(x)
    lane = lax.broadcasted_iota(jnp.int32, x.shape, 1)
    rest = jnp.sum(x - near, axis=1, keepdims=True)
    return jnp.where(lane == 0, near + rest, near)


def turn(plus, minus, t):
    t = t % (2 * LANES)
    if t == 0:
        return plus, minus
    if t >= LANES:
        return turn(plus, -minus, t - LANES)
    lane = lax.broadcasted_iota(jnp.int32, minus.shape, 1)
    minus = pltpu.roll(minus, t, 1)
    return pltpu.roll(plus, t, 1), jnp.where(lane < t, -minus, minus)


def pick_block(me, nb, block_owner, class_gain, ref_store):
    nblk, kb, cycles, angles = ref_store.shape

    def body(me_ref, owner_ref, gain_ref, store_ref, out_ref, buf, sem):
        block = jnp.int32(0)
        for b in range(nblk):
            block = jnp.where(owner_ref[b] == me_ref[0] // nb, jnp.int32(b), block)
        copy = pltpu.make_async_copy(store_ref.at[block], buf, sem)
        copy.start()
        copy.wait()
        for i in range(kb):
            piece = (buf[i].astype(F32) * gain_ref[block * kb + i]).astype(BF).astype(F32)
            a, b = piece[:, :LANES], piece[:, LANES:]
            piece = jnp.concatenate([narrow_sum(a + b), narrow(a - b)], axis=1).astype(BF)
            out_ref[i * cycles : (i + 1) * cycles, :] = piece

    return pl.pallas_call(
        body,
        out_shape=VM((kb * cycles, angles), BF),
        in_specs=[spec(pltpu.SMEM), spec(pltpu.SMEM), spec(pltpu.SMEM), spec(pltpu.HBM)],
        out_specs=spec(),
        scratch_shapes=[VM((kb, cycles, angles), BF), pltpu.SemaphoreType.DMA],
        compiler_params=params(60),
        name="pick_block",
    )(me, block_owner, class_gain, away(ref_store))


def halve_images(own, other, nb, after):
    particles, cycles, angles = own.shape
    per = particles // nb

    def body(own_ref, other_ref, _, out_ref, a_scr, b_scr):
        fill(a_scr, own_ref[...].astype(F32).reshape(particles * cycles, angles))
        fill(b_scr, other_ref[...].astype(F32).reshape(particles * cycles, angles))
        for r in range(cycles):
            a = take_cycle(a_scr, r, particles, cycles)
            b = take_cycle(b_scr, r, particles, cycles)
            for i, op in enumerate((jnp.add, jnp.subtract)):
                x, y = op(a[0], a[1]), op(b[0], b[1])
                both = [v.reshape(nb, per, LANES) for v in (x, y)]
                both = jnp.concatenate(both, axis=1).reshape(2 * particles, LANES)
                out_ref[i, r] = narrow(both).astype(BF)

    return pl.pallas_call(
        body,
        out_shape=VM((2, cycles, 2 * particles, LANES), BF),
        in_specs=[spec(), spec(), spec()],
        out_specs=spec(),
        scratch_shapes=[VM((2, particles * cycles, LANES), F32)] * 2,
        compiler_params=params(),
        name="halve_images",
    )(own, here(other), here(after))


def rotate_images(x_ref, r, nb, step):
    plus, minus = x_ref[0, r], x_ref[1, r]
    per = plus.shape[0] // nb
    turned = [turn(plus, minus, step * s) for s in range(N1)]
    return [
        jnp.concatenate(
            [t[i][j * per : (j + 1) * per] for j in range(nb) for t in turned], axis=0
        )
        for i in range(2)
    ]


def correlate(images, refs, nb, step, before=()):
    _, cycles, particles, _ = images.shape
    total = N1 * particles
    rows = total // nb
    classes = len(refs) * refs[0].shape[0] // cycles
    cols = N2 * classes
    angles = 2 * LANES

    def body(x_ref, *args):
        r_refs, (out_ref, scr, rr, x) = args[: len(refs)], args[-4:]
        for t, b_ref in enumerate(args[len(refs) : -4]):
            out_ref[:, t] = b_ref[:, 0]
        blocks = [r_ref[...].astype(F32) for r_ref in r_refs]
        fill(scr, jnp.concatenate(blocks, axis=0))
        square = jnp.zeros((classes, LANES), F32)
        for r in range(cycles):
            plus, minus = take_cycle(scr, r, classes, cycles)
            square = square + 0.5 * (plus * plus + minus * minus)
            plus, minus = plus.astype(BF), minus.astype(BF)
            x[0, r], x[1, r] = rotate_images(x_ref, r, nb, step)
            for s in range(N2):
                p, m = turn(plus, minus, angles - step * N1 * s)
                rr[0, r, s * classes : (s + 1) * classes, :] = p
                rr[1, r, s * classes : (s + 1) * classes, :] = m
        norm = jnp.broadcast_to(jnp.sum(square, axis=1, keepdims=True), (classes, cols))
        k = lax.broadcasted_iota(jnp.int32, (classes, cols), 0)
        lane = lax.broadcasted_iota(jnp.int32, (classes, cols), 1)
        norm = jnp.sum(jnp.where(lane % classes == k, norm, 0.0), axis=0, keepdims=True)
        for i in range(2):
            left = jnp.concatenate([x[i, r] for r in range(cycles)], axis=1)
            right = jnp.concatenate([rr[i, r] for r in range(cycles)], axis=1)
            part = lax.dot_general(
                left, right, (((1,), (1,)), ((), ())), preferred_element_type=F32
            )
            if i == 0:
                part = part - norm
            at = slice(i * rows, (i + 1) * rows)
            out_ref[:, len(before), at, :] = part.astype(BF).reshape(nb, rows, LANES)

    return pl.pallas_call(
        body,
        out_shape=VM((nb, 1 + len(before), 2 * rows, LANES), BF),
        in_specs=[spec()] * (1 + len(refs) + len(before)),
        out_specs=spec(),
        scratch_shapes=[
            VM((2, classes * cycles, LANES), F32),
            VM((2, cycles, cols, LANES), BF),
            VM((2, cycles, total, LANES), BF),
        ],
        compiler_params=params(),
        name="correlate",
    )(here(images), *[here(r) for r in (*refs, *before)])


def local_softmax(me, scores, precision, others):
    nb, tiles, rows, _ = scores.shape
    cols = tiles * LANES
    half = rows // 2
    group = half // N1
    own = group // 2

    def across(op, x):
        pieces = [x[i * group : (i + 1) * group] for i in range(N1)]
        return op(op(pieces[0], pieces[1]), op(pieces[2], pieces[3]))

    def body(me_ref, x_ref, a_ref, b_ref, e_ref, stat_ref):
        total = x_ref[0].astype(F32)
        for i in range(1, nb):
            total = total + x_ref[i].astype(F32)
        total = jnp.concatenate([total[t] for t in range(tiles)], axis=1)
        plus, minus = total[:half], total[half:]
        wide = (own, nb * own)
        row = lax.broadcasted_iota(jnp.int32, wide, 0) + me_ref[0] % nb * own
        mine = row == lax.broadcasted_iota(jnp.int32, wide, 1)
        scale = [
            jnp.sum(jnp.where(mine, ref[...], 0.0), axis=1, keepdims=True)
            for ref in (a_ref, b_ref)
        ]
        scale = jnp.concatenate(scale * N1, axis=0) * 0.5
        near, far = scale * (plus + minus), scale * (plus - minus)
        top = jnp.max(jnp.maximum(near, far), axis=1, keepdims=True)
        top = across(jnp.maximum, top)
        tops = jnp.concatenate([top] * N1, axis=0)
        near, far = jnp.exp(near - tops), jnp.exp(far - tops)
        e_ref[0] = near
        e_ref[1] = far
        amount = across(jnp.add, jnp.sum(near + far, axis=1, keepdims=True))
        stat_ref[0] = jnp.broadcast_to(top, (group, LANES))
        stat_ref[1] = jnp.broadcast_to(amount, (group, LANES))

    return pl.pallas_call(
        body,
        out_shape=(VM((2, half, cols), F32), VM((2, group, LANES), F32)),
        in_specs=[spec(pltpu.SMEM), spec(), spec(), spec()],
        out_specs=(spec(), spec()),
        compiler_params=params(),
        name="local_softmax",
    )(me, here(scores), here(precision), here(others))


def normalize(e, mine, theirs, copies):
    _, half, cols = e.shape
    group = mine.shape[1]

    def body(e_ref, a_ref, b_ref, out_ref):
        def flipped(x):
            return jnp.concatenate([x[group // 2 :], x[: group // 2]], axis=0)

        top_a, sum_a = a_ref[0], a_ref[1]
        top_b, sum_b = flipped(b_ref[0]), flipped(b_ref[1])
        top = jnp.maximum(top_a, top_b)
        part = jnp.exp(top_a - top)
        factor = part / (sum_a * part + sum_b * jnp.exp(top_b - top))
        factor = jnp.concatenate([jnp.concatenate([factor] * N1, axis=0)] * (cols // LANES), axis=1)
        near, far = e_ref[0] * factor, e_ref[1] * factor
        w = jnp.concatenate([near + far, near - far], axis=0).T.astype(BF)
        for c in range(copies):
            out_ref[c] = w

    return pl.pallas_call(
        body,
        out_shape=VM((copies, cols, 2 * half), BF),
        in_specs=[spec(), spec(), spec()],
        out_specs=spec(),
        compiler_params=params(),
        name="normalize",
    )(here(e), here(mine), here(theirs))


def accumulate(me, weights, images, ny, nz, step):
    owners = ny * nz
    nb, cols, lanes = weights.shape
    cycles = images.shape[1]
    classes = cols // N2
    per = LANES // N2
    pair = 2 * LANES

    def body(me_ref, w_ref, x_ref, out_ref, scr, x):
        for r in range(cycles):
            x[0, r], x[1, r] = rotate_images(x_ref, r, nb, step)
        left = lax.broadcasted_iota(jnp.int32, (cols, lanes), 1) < lanes // 2
        near, far = [], []
        for j in range(0, nb, 2):
            a, b = w_ref[j], w_ref[j + 1]
            near.append(jnp.where(left, a, pltpu.roll(b, lanes // 2, 1)))
            far.append(jnp.where(left, pltpu.roll(a, lanes // 2, 1), b))
        w = [jnp.concatenate(v, axis=1) for v in (near, far)]
        for c in range(0, cycles, 2):
            spread = []
            for i in range(2):
                both = jnp.concatenate([x[i, c], x[i, c + 1]], axis=1)
                spread.append(jnp.dot(w[i], both, preferred_element_type=F32))
            for d in range(2):
                plus = minus = None
                for s in range(N2):
                    p, m = (
                        jnp.concatenate(
                            [
                                v[t + s * per : t + (s + 1) * per, d * LANES : (d + 1) * LANES]
                                for t in range(0, cols, LANES)
                            ],
                            axis=0,
                        )
                        for v in spread
                    )
                    p, m = turn(p, m, step * N1 * s)
                    plus = plus + p if s else p
                    minus = minus + m if s else m
                rows = pl.ds(c + d, classes, stride=cycles)
                scr.at[0][rows, :] = 0.5 * (plus + minus)
                scr.at[1][rows, :] = 0.5 * (plus - minus)
        whole = jnp.concatenate([scr[0], scr[1]], axis=1)
        whole = whole.reshape(out_ref.shape).astype(BF)
        place = me_ref[0] // (2 * nb)
        y, z = place // nz, place % nz
        for slot in range(owners):
            dy, dz = slot // nz, PARTNERS[slot % nz]
            out_ref[(y ^ dy) * nz + (z ^ dz)] = whole[slot]

    return pl.pallas_call(
        body,
        out_shape=VM((owners, classes // owners * cycles, pair), BF),
        in_specs=[spec(pltpu.SMEM), spec(), spec()],
        out_specs=spec(),
        scratch_shapes=[
            VM((2, classes * cycles, LANES), F32),
            VM((2, cycles, N1 * images.shape[2], LANES), BF),
        ],
        compiler_params=params(),
        name="accumulate",
    )(me, here(weights), here(images))


def add_up(parts):
    def body(x_ref, out_ref):
        total = x_ref[0].astype(F32)
        for i in range(1, parts.shape[0]):
            total = total + x_ref[i].astype(F32)
        out_ref[...] = total

    return pl.pallas_call(
        body,
        out_shape=jax.ShapeDtypeStruct(parts.shape[1:], F32),
        in_specs=[spec()],
        out_specs=spec(),
        compiler_params=params(),
        name="add_up",
    )(here(parts))


def solution(mesh):
    dom, nb = mesh.devices.shape
    ny, nz = 2, dom // 4
    view = Mesh(mesh.devices.reshape(ny, nz, 2, nb), ("yh", "z", "core", "blk"))
    swap = [(0, 1), (1, 0)]

    def shards(images, ref_store, block_owner, class_gain, precision):
        particles, cycles, angles = images.shape
        kb = ref_store.shape[2]
        rot = angles // (2 * N1 * N2)
        other = lax.ppermute(images, "core", swap)
        other_precision = lax.ppermute(precision, "core", swap)
        y, z = lax.axis_index("yh"), lax.axis_index("z")
        me = ((y * nz + z) * 2 + lax.axis_index("core")) * nb + lax.axis_index("blk")
        me = me[None].astype(jnp.int32)
        mine = pick_block(me, nb, block_owner, class_gain, ref_store[0])
        refs = []
        theirs = lax.ppermute(mine, "yh", swap)
        for block in (mine, theirs):
            refs.append([block])
            for d in PARTNERS[1:]:
                ring = [(i, i ^ d) for i in range(nz)]
                refs[-1].append(lax.ppermute(block, "z", ring))
        halves = halve_images(images, other, nb, other_precision)
        early = correlate(halves, refs[0], nb, rot)
        scores = correlate(halves, refs[1], nb, rot, (early,))
        scores = lax.all_to_all(scores, "blk", 0, 0)
        flat = (1, particles)
        e, stats = local_softmax(
            me, scores, precision.reshape(flat), other_precision.reshape(flat)
        )
        theirs = lax.ppermute(stats, "core", swap)
        weights = normalize(e, stats, theirs, nb)
        weights = lax.all_to_all(weights, "blk", 0, 0)
        totals = accumulate(me, weights, halves, ny, nz, rot)
        totals = lax.all_to_all(totals, ("yh", "z"), 0, 0)
        return add_up(totals).reshape(1, 1, kb, cycles, angles)

    dom_axes = ("yh", "z", "core")
    return jax.shard_map(
        shards,
        mesh=view,
        in_specs=(
            P(dom_axes, "blk", None),
            P(dom_axes, None, None, "blk", None),
            P(),
            P(),
            P(dom_axes),
        ),
        out_specs=P(dom_axes, None, None, "blk", None),
        check_vma=False,
    )
```

```python
import jax
import jax.numpy as jnp
from jax import lax
from jax.experimental import pallas as pl
from jax.experimental.pallas import tpu as pltpu
from jax.sharding import Mesh, PartitionSpec as P


BF = jnp.bfloat16
F32 = jnp.float32
VM = pltpu.VMEM
LANES = 128
N1 = 4
N2 = 8
PARTNERS = (0, 1, 3, 2)


def spec(space=VM):
    return pl.BlockSpec(memory_space=space)


def params(mib=24):
    return pltpu.CompilerParams(vmem_limit_bytes=mib * 1024 * 1024)


def here(x):
    return pltpu.with_memory_space_constraint(x, VM)


def away(x):
    return pltpu.with_memory_space_constraint(x, pltpu.HBM)


def fill(scr, value):
    for h in range(scr.shape[0]):
        scr[h] = value[:, h * LANES : (h + 1) * LANES]


def take_cycle(scr, r, rows, cycles):
    return [scr.at[h][pl.ds(r, rows, stride=cycles), :] for h in range(2)]


def narrow(x):
    wide = x * 65537.0
    return wide - (wide - x)


def narrow_sum(x):
    near = narrow(x)
    lane = lax.broadcasted_iota(jnp.int32, x.shape, 1)
    rest = jnp.sum(x - near, axis=1, keepdims=True)
    return jnp.where(lane == 0, near + rest, near)


def turn(plus, minus, t):
    t = t % (2 * LANES)
    if t == 0:
        return plus, minus
    if t >= LANES:
        return turn(plus, -minus, t - LANES)
    lane = lax.broadcasted_iota(jnp.int32, minus.shape, 1)
    minus = pltpu.roll(minus, t, 1)
    return pltpu.roll(plus, t, 1), jnp.where(lane < t, -minus, minus)


def pick_block(me, nb, block_owner, class_gain, ref_store):
    nblk, kb, cycles, angles = ref_store.shape

    def body(me_ref, owner_ref, gain_ref, store_ref, out_ref):
        block = jnp.int32(0)
        for b in range(nblk):
            block = jnp.where(owner_ref[b] == me_ref[0] // nb, jnp.int32(b), block)
        for i in range(kb):
            piece = (store_ref[block, i].astype(F32) * gain_ref[block * kb + i]).astype(BF).astype(F32)
            a, b = piece[:, :LANES], piece[:, LANES:]
            piece = jnp.concatenate([narrow_sum(a + b), narrow(a - b)], axis=1).astype(BF)
            out_ref[i * cycles : (i + 1) * cycles, :] = piece

    return pl.pallas_call(
        body,
        out_shape=VM((kb * cycles, angles), BF),
        in_specs=[spec(pltpu.SMEM), spec(pltpu.SMEM), spec(pltpu.SMEM), spec()],
        out_specs=spec(),
        compiler_params=params(60),
        name="pick_block",
    )(me, block_owner, class_gain, away(ref_store))


def halve_images(own, other, nb):
    particles, cycles, angles = own.shape
    per = particles // nb

    def body(own_ref, other_ref, out_ref, a_scr, b_scr):
        fill(a_scr, own_ref[...].astype(F32).reshape(particles * cycles, angles))
        fill(b_scr, other_ref[...].astype(F32).reshape(particles * cycles, angles))
        for r in range(cycles):
            a = take_cycle(a_scr, r, particles, cycles)
            b = take_cycle(b_scr, r, particles, cycles)
            for i, op in enumerate((jnp.add, jnp.subtract)):
                x, y = op(a[0], a[1]), op(b[0], b[1])
                both = [v.reshape(nb, per, LANES) for v in (x, y)]
                both = jnp.concatenate(both, axis=1).reshape(2 * particles, LANES)
                out_ref[i, r] = narrow(both).astype(BF)

    return pl.pallas_call(
        body,
        out_shape=VM((2, cycles, 2 * particles, LANES), BF),
        in_specs=[spec(), spec()],
        out_specs=spec(),
        scratch_shapes=[VM((2, particles * cycles, LANES), F32)] * 2,
        compiler_params=params(),
        name="halve_images",
    )(own, here(other))


def pair_up(mine, theirs, *others):
    def body(a_ref, b_ref, *refs):
        out_ref = refs[-1]
        out_ref[0] = a_ref[...]
        out_ref[1] = b_ref[...]

    return pl.pallas_call(
        body,
        out_shape=VM((2,) + mine.shape, BF),
        in_specs=[spec()] * (2 + len(others)),
        out_specs=spec(),
        compiler_params=params(),
        name="pair_up",
    )(here(mine), here(theirs), *[here(o) for o in others])


def rotate_images(x_ref, r, nb, step):
    plus, minus = x_ref[0, r], x_ref[1, r]
    per = plus.shape[0] // nb
    turned = [turn(plus, minus, step * s) for s in range(N1)]
    return [
        jnp.concatenate(
            [t[i][j * per : (j + 1) * per] for j in range(nb) for t in turned], axis=0
        )
        for i in range(2)
    ]


def correlate(images, refs, nb, step, before=()):
    _, cycles, particles, _ = images.shape
    total = N1 * particles
    rows = total // nb
    near, far = refs[0].shape[:2]
    classes = len(refs) * near * far // cycles
    cols = N2 * classes
    angles = 2 * LANES

    def body(x_ref, *args):
        r_refs, (out_ref, scr, rr, x) = args[: len(refs)], args[-4:]
        for t, b_ref in enumerate(args[len(refs) : -4]):
            out_ref[:, t] = b_ref[:, 0]
        blocks = [r_ref[d].astype(F32) for r_ref in r_refs for d in range(near)]
        fill(scr, jnp.concatenate(blocks, axis=0))
        square = jnp.zeros((classes, LANES), F32)
        for r in range(cycles):
            plus, minus = take_cycle(scr, r, classes, cycles)
            square = square + 0.5 * (plus * plus + minus * minus)
            plus, minus = plus.astype(BF), minus.astype(BF)
            x[0, r], x[1, r] = rotate_images(x_ref, r, nb, step)
            for s in range(N2):
                p, m = turn(plus, minus, angles - step * N1 * s)
                rr[0, r, s * classes : (s + 1) * classes, :] = p
                rr[1, r, s * classes : (s + 1) * classes, :] = m
        norm = jnp.broadcast_to(jnp.sum(square, axis=1, keepdims=True), (classes, cols))
        k = lax.broadcasted_iota(jnp.int32, (classes, cols), 0)
        lane = lax.broadcasted_iota(jnp.int32, (classes, cols), 1)
        norm = jnp.sum(jnp.where(lane % classes == k, norm, 0.0), axis=0, keepdims=True)
        for i in range(2):
            left = jnp.concatenate([x[i, r] for r in range(cycles)], axis=1)
            right = jnp.concatenate([rr[i, r] for r in range(cycles)], axis=1)
            part = lax.dot_general(
                left, right, (((1,), (1,)), ((), ())), preferred_element_type=F32
            )
            if i == 0:
                part = part - norm
            at = slice(i * rows, (i + 1) * rows)
            out_ref[:, len(before), at, :] = part.astype(BF).reshape(nb, rows, LANES)

    return pl.pallas_call(
        body,
        out_shape=VM((nb, 1 + len(before), 2 * rows, LANES), BF),
        in_specs=[spec()] * (1 + len(refs) + len(before)),
        out_specs=spec(),
        scratch_shapes=[
            VM((2, classes * cycles, LANES), F32),
            VM((2, cycles, cols, LANES), BF),
            VM((2, cycles, total, LANES), BF),
        ],
        compiler_params=params(),
        name="correlate",
    )(here(images), *[here(r) for r in (*refs, *before)])


def local_softmax(me, scores, precision, others):
    nb, tiles, rows, _ = scores.shape
    cols = tiles * LANES
    half = rows // 2
    group = half // N1
    own = group // 2

    def across(op, x):
        pieces = [x[i * group : (i + 1) * group] for i in range(N1)]
        return op(op(pieces[0], pieces[1]), op(pieces[2], pieces[3]))

    def body(me_ref, x_ref, a_ref, b_ref, e_ref, stat_ref):
        total = x_ref[0].astype(F32)
        for i in range(1, nb):
            total = total + x_ref[i].astype(F32)
        total = jnp.concatenate([total[t] for t in range(tiles)], axis=1)
        plus, minus = total[:half], total[half:]
        wide = (own, nb * own)
        row = lax.broadcasted_iota(jnp.int32, wide, 0) + me_ref[0] % nb * own
        mine = row == lax.broadcasted_iota(jnp.int32, wide, 1)
        scale = [
            jnp.sum(jnp.where(mine, ref[...], 0.0), axis=1, keepdims=True)
            for ref in (a_ref, b_ref)
        ]
        scale = jnp.concatenate(scale * N1, axis=0) * 0.5
        near, far = scale * (plus + minus), scale * (plus - minus)
        top = jnp.max(jnp.maximum(near, far), axis=1, keepdims=True)
        top = across(jnp.maximum, top)
        tops = jnp.concatenate([top] * N1, axis=0)
        near, far = jnp.exp(near - tops), jnp.exp(far - tops)
        e_ref[0] = near
        e_ref[1] = far
        amount = across(jnp.add, jnp.sum(near + far, axis=1, keepdims=True))
        stat_ref[0] = jnp.broadcast_to(top, (group, LANES))
        stat_ref[1] = jnp.broadcast_to(amount, (group, LANES))

    return pl.pallas_call(
        body,
        out_shape=(VM((2, half, cols), F32), VM((2, group, LANES), F32)),
        in_specs=[spec(pltpu.SMEM), spec(), spec(), spec()],
        out_specs=(spec(), spec()),
        compiler_params=params(),
        name="local_softmax",
    )(me, here(scores), here(precision), here(others))


def normalize(e, mine, theirs, copies):
    _, half, cols = e.shape
    group = mine.shape[1]

    def body(e_ref, a_ref, b_ref, out_ref):
        def flipped(x):
            return jnp.concatenate([x[group // 2 :], x[: group // 2]], axis=0)

        top_a, sum_a = a_ref[0], a_ref[1]
        top_b, sum_b = flipped(b_ref[0]), flipped(b_ref[1])
        top = jnp.maximum(top_a, top_b)
        part = jnp.exp(top_a - top)
        factor = part / (sum_a * part + sum_b * jnp.exp(top_b - top))
        factor = jnp.concatenate([jnp.concatenate([factor] * N1, axis=0)] * (cols // LANES), axis=1)
        near, far = e_ref[0] * factor, e_ref[1] * factor
        w = jnp.concatenate([near + far, near - far], axis=0).T.astype(BF)
        for c in range(copies):
            out_ref[c] = w

    return pl.pallas_call(
        body,
        out_shape=VM((copies, cols, 2 * half), BF),
        in_specs=[spec(), spec(), spec()],
        out_specs=spec(),
        compiler_params=params(),
        name="normalize",
    )(here(e), here(mine), here(theirs))


def accumulate(me, weights, images, ny, nz, step):
    owners = ny * nz
    nb, cols, lanes = weights.shape
    cycles = images.shape[1]
    classes = cols // N2
    per = LANES // N2
    pair = 2 * LANES

    def body(me_ref, w_ref, x_ref, out_ref, scr, x):
        for r in range(cycles):
            x[0, r], x[1, r] = rotate_images(x_ref, r, nb, step)
        left = lax.broadcasted_iota(jnp.int32, (cols, lanes), 1) < lanes // 2
        near, far = [], []
        for j in range(0, nb, 2):
            a, b = w_ref[j], w_ref[j + 1]
            near.append(jnp.where(left, a, pltpu.roll(b, lanes // 2, 1)))
            far.append(jnp.where(left, pltpu.roll(a, lanes // 2, 1), b))
        w = [jnp.concatenate(v, axis=1) for v in (near, far)]
        for c in range(0, cycles, 2):
            spread = []
            for i in range(2):
                both = jnp.concatenate([x[i, c], x[i, c + 1]], axis=1)
                spread.append(jnp.dot(w[i], both, preferred_element_type=F32))
            for d in range(2):
                plus = minus = None
                for s in range(N2):
                    p, m = (
                        jnp.concatenate(
                            [
                                v[t + s * per : t + (s + 1) * per, d * LANES : (d + 1) * LANES]
                                for t in range(0, cols, LANES)
                            ],
                            axis=0,
                        )
                        for v in spread
                    )
                    p, m = turn(p, m, step * N1 * s)
                    plus = plus + p if s else p
                    minus = minus + m if s else m
                rows = pl.ds(c + d, classes, stride=cycles)
                scr.at[0][rows, :] = 0.5 * (plus + minus)
                scr.at[1][rows, :] = 0.5 * (plus - minus)
        whole = jnp.concatenate([scr[0], scr[1]], axis=1)
        whole = whole.reshape(out_ref.shape).astype(BF)
        place = me_ref[0] // (2 * nb)
        y, z = place // nz, place % nz
        for slot in range(owners):
            dz, dy = PARTNERS[slot // ny], slot % ny
            out_ref[(y ^ dy) * nz + (z ^ dz)] = whole[slot]

    return pl.pallas_call(
        body,
        out_shape=VM((owners, classes // owners * cycles, pair), BF),
        in_specs=[spec(pltpu.SMEM), spec(), spec()],
        out_specs=spec(),
        scratch_shapes=[
            VM((2, classes * cycles, LANES), F32),
            VM((2, cycles, N1 * images.shape[2], LANES), BF),
        ],
        compiler_params=params(),
        name="accumulate",
    )(me, here(weights), here(images))


def add_up(parts):
    def body(x_ref, out_ref):
        total = x_ref[0].astype(F32)
        for i in range(1, parts.shape[0]):
            total = total + x_ref[i].astype(F32)
        out_ref[...] = total

    return pl.pallas_call(
        body,
        out_shape=jax.ShapeDtypeStruct(parts.shape[1:], F32),
        in_specs=[spec()],
        out_specs=spec(),
        compiler_params=params(),
        name="add_up",
    )(here(parts))


def solution(mesh):
    dom, nb = mesh.devices.shape
    ny, nz = 2, dom // 4
    view = Mesh(mesh.devices.reshape(ny, nz, 2, nb), ("yh", "z", "core", "blk"))
    swap = [(0, 1), (1, 0)]

    def shards(images, ref_store, block_owner, class_gain, precision):
        particles, cycles, angles = images.shape
        kb = ref_store.shape[2]
        rot = angles // (2 * N1 * N2)
        other = lax.ppermute(images, "core", swap)
        other_precision = lax.ppermute(precision, "core", swap)
        y, z = lax.axis_index("yh"), lax.axis_index("z")
        me = ((y * nz + z) * 2 + lax.axis_index("core")) * nb + lax.axis_index("blk")
        me = me[None].astype(jnp.int32)
        mine = pick_block(me, nb, block_owner, class_gain, ref_store[0])
        theirs = lax.ppermute(mine, "yh", swap)
        halves = halve_images(images, other, nb)
        refs = [pair_up(mine, theirs, halves, other_precision)]
        for d in PARTNERS[1:]:
            ring = [(i, i ^ d) for i in range(nz)]
            refs.append(lax.ppermute(refs[0], "z", ring))
        early = correlate(halves, refs[:2], nb, rot)
        scores = correlate(halves, refs[2:], nb, rot, (early,))
        scores = lax.all_to_all(scores, "blk", 0, 0)
        flat = (1, particles)
        e, stats = local_softmax(
            me, scores, precision.reshape(flat), other_precision.reshape(flat)
        )
        theirs = lax.ppermute(stats, "core", swap)
        weights = normalize(e, stats, theirs, nb)
        weights = lax.all_to_all(weights, "blk", 0, 0)
        totals = accumulate(me, weights, halves, ny, nz, rot)
        totals = lax.all_to_all(totals, ("yh", "z"), 0, 0)
        return add_up(totals).reshape(1, 1, kb, cycles, angles)

    dom_axes = ("yh", "z", "core")
    return jax.shard_map(
        shards,
        mesh=view,
        in_specs=(
            P(dom_axes, "blk", None),
            P(dom_axes, None, None, "blk", None),
            P(),
            P(),
            P(dom_axes),
        ),
        out_specs=P(dom_axes, None, None, "blk", None),
        check_vma=False,
    )
```

```python
import jax
import jax.numpy as jnp
from jax import lax
from jax.experimental import pallas as pl
from jax.experimental.pallas import tpu as pltpu
from jax.sharding import Mesh, PartitionSpec as P


BF = jnp.bfloat16
F32 = jnp.float32
VM = pltpu.VMEM
LANES = 128
N1 = 4
N2 = 8
PARTNERS = (0, 1, 3, 2)


def spec(space=VM):
    return pl.BlockSpec(memory_space=space)


def params(mib=24):
    return pltpu.CompilerParams(vmem_limit_bytes=mib * 1024 * 1024)


def here(x):
    return pltpu.with_memory_space_constraint(x, VM)


def away(x):
    return pltpu.with_memory_space_constraint(x, pltpu.HBM)


def fill(scr, value):
    for h in range(scr.shape[0]):
        scr[h] = value[:, h * LANES : (h + 1) * LANES]


def take_cycle(scr, r, rows, cycles):
    return [scr.at[h][pl.ds(r, rows, stride=cycles), :] for h in range(2)]


def narrow(x):
    wide = x * 65537.0
    return wide - (wide - x)


def narrow_sum(x):
    near = narrow(x)
    lane = lax.broadcasted_iota(jnp.int32, x.shape, 1)
    rest = jnp.sum(x - near, axis=1, keepdims=True)
    return jnp.where(lane == 0, near + rest, near)


def turn(plus, minus, t):
    t = t % (2 * LANES)
    if t == 0:
        return plus, minus
    if t >= LANES:
        return turn(plus, -minus, t - LANES)
    lane = lax.broadcasted_iota(jnp.int32, minus.shape, 1)
    minus = pltpu.roll(minus, t, 1)
    return pltpu.roll(plus, t, 1), jnp.where(lane < t, -minus, minus)


def pick_block(me, nb, block_owner, class_gain, ref_store):
    nblk, kb, cycles, angles = ref_store.shape

    def body(me_ref, owner_ref, gain_ref, store_ref, out_ref):
        block = jnp.int32(0)
        for b in range(nblk):
            block = jnp.where(owner_ref[b] == me_ref[0] // nb, jnp.int32(b), block)
        for i in range(kb):
            piece = (store_ref[block, i].astype(F32) * gain_ref[block * kb + i]).astype(BF).astype(F32)
            a, b = piece[:, :LANES], piece[:, LANES:]
            piece = jnp.concatenate([narrow_sum(a + b), narrow(a - b)], axis=1).astype(BF)
            out_ref[i * cycles : (i + 1) * cycles, :] = piece

    return pl.pallas_call(
        body,
        out_shape=VM((kb * cycles, angles), BF),
        in_specs=[spec(pltpu.SMEM), spec(pltpu.SMEM), spec(pltpu.SMEM), spec()],
        out_specs=spec(),
        compiler_params=params(60),
        name="pick_block",
    )(me, block_owner, class_gain, away(ref_store))


def halve_images(own, other, nb):
    particles, cycles, angles = own.shape
    per = particles // nb

    def body(own_ref, other_ref, out_ref, a_scr, b_scr):
        fill(a_scr, own_ref[...].astype(F32).reshape(particles * cycles, angles))
        fill(b_scr, other_ref[...].astype(F32).reshape(particles * cycles, angles))
        for r in range(cycles):
            a = take_cycle(a_scr, r, particles, cycles)
            b = take_cycle(b_scr, r, particles, cycles)
            for i, op in enumerate((jnp.add, jnp.subtract)):
                x, y = op(a[0], a[1]), op(b[0], b[1])
                both = [v.reshape(nb, per, LANES) for v in (x, y)]
                both = jnp.concatenate(both, axis=1).reshape(2 * particles, LANES)
                out_ref[i, r] = narrow(both).astype(BF)

    return pl.pallas_call(
        body,
        out_shape=VM((2, cycles, 2 * particles, LANES), BF),
        in_specs=[spec(), spec()],
        out_specs=spec(),
        scratch_shapes=[VM((2, particles * cycles, LANES), F32)] * 2,
        compiler_params=params(),
        name="halve_images",
    )(own, here(other))


def pair_up(mine, theirs, *others):
    def body(a_ref, b_ref, *refs):
        out_ref = refs[-1]
        out_ref[0] = a_ref[...]
        out_ref[1] = b_ref[...]

    return pl.pallas_call(
        body,
        out_shape=VM((2,) + mine.shape, BF),
        in_specs=[spec()] * (2 + len(others)),
        out_specs=spec(),
        compiler_params=params(),
        name="pair_up",
    )(here(mine), here(theirs), *[here(o) for o in others])


def rotate_images(x_ref, r, nb, step):
    plus, minus = x_ref[0, r], x_ref[1, r]
    per = plus.shape[0] // nb
    turned = [turn(plus, minus, step * s) for s in range(N1)]
    return [
        jnp.concatenate(
            [t[i][j * per : (j + 1) * per] for j in range(nb) for t in turned], axis=0
        )
        for i in range(2)
    ]


def turn_images(images, nb, step):
    _, cycles, particles, _ = images.shape

    def body(x_ref, out_ref):
        for r in range(cycles):
            out_ref[0, r], out_ref[1, r] = rotate_images(x_ref, r, nb, step)

    return pl.pallas_call(
        body,
        out_shape=VM((2, cycles, N1 * particles, LANES), BF),
        in_specs=[spec()],
        out_specs=spec(),
        compiler_params=params(),
        name="turn_images",
    )(here(images))


def correlate(turned, refs, nb, step, before=()):
    _, cycles, total, _ = turned.shape
    rows = total // nb
    near, far = refs[0].shape[:2]
    classes = len(refs) * near * far // cycles
    cols = N2 * classes
    angles = 2 * LANES
    tiles = 1 + len(before)

    def body(x_ref, *args):
        r_refs, (out_ref, scr, rr) = args[: len(refs)], args[-3:]
        for t, b_ref in enumerate(args[len(refs) : -3]):
            out_ref[:, t] = b_ref[:, 0]
        blocks = [r_ref[d].astype(F32) for r_ref in r_refs for d in range(near)]
        fill(scr, jnp.concatenate(blocks, axis=0))
        square = jnp.zeros((classes, LANES), F32)
        for r in range(cycles):
            plus, minus = take_cycle(scr, r, classes, cycles)
            square = square + 0.5 * (plus * plus + minus * minus)
            plus, minus = plus.astype(BF), minus.astype(BF)
            for s in range(N2):
                p, m = turn(plus, minus, angles - step * N1 * s)
                rr[0, r, s * classes : (s + 1) * classes, :] = p
                rr[1, r, s * classes : (s + 1) * classes, :] = m
        norm = jnp.broadcast_to(jnp.sum(square, axis=1, keepdims=True), (classes, cols))
        k = lax.broadcasted_iota(jnp.int32, (classes, cols), 0)
        lane = lax.broadcasted_iota(jnp.int32, (classes, cols), 1)
        norm = jnp.sum(jnp.where(lane % classes == k, norm, 0.0), axis=0, keepdims=True)
        for i in range(2):
            left = jnp.concatenate([x_ref[i, r] for r in range(cycles)], axis=1)
            right = jnp.concatenate([rr[i, r] for r in range(cycles)], axis=1)
            part = lax.dot_general(
                left, right, (((1,), (1,)), ((), ())), preferred_element_type=F32
            )
            if i == 0:
                part = part - norm
            at = slice(i * rows, (i + 1) * rows)
            out_ref[:, tiles - 1, at, :] = part.astype(BF).reshape(nb, rows, LANES)

    return pl.pallas_call(
        body,
        out_shape=VM((nb, tiles, 2 * rows, LANES), BF),
        in_specs=[spec()] * (len(refs) + tiles),
        out_specs=spec(),
        scratch_shapes=[
            VM((2, classes * cycles, LANES), F32),
            VM((2, cycles, cols, LANES), BF),
        ],
        compiler_params=params(),
        name="correlate",
    )(here(turned), *[here(r) for r in (*refs, *before)])


def local_softmax(me, scores, precision, others):
    nb, tiles, rows, _ = scores.shape
    cols = tiles * LANES
    half = rows // 2
    group = half // N1
    own = group // 2

    def across(op, x):
        pieces = [x[i * group : (i + 1) * group] for i in range(N1)]
        return op(op(pieces[0], pieces[1]), op(pieces[2], pieces[3]))

    def body(me_ref, x_ref, a_ref, b_ref, e_ref, stat_ref):
        total = x_ref[0].astype(F32)
        for i in range(1, nb):
            total = total + x_ref[i].astype(F32)
        total = jnp.concatenate([total[t] for t in range(tiles)], axis=1)
        plus, minus = total[:half], total[half:]
        wide = (own, nb * own)
        row = lax.broadcasted_iota(jnp.int32, wide, 0) + me_ref[0] % nb * own
        mine = row == lax.broadcasted_iota(jnp.int32, wide, 1)
        scale = [
            jnp.sum(jnp.where(mine, ref[...], 0.0), axis=1, keepdims=True)
            for ref in (a_ref, b_ref)
        ]
        scale = jnp.concatenate(scale * N1, axis=0) * 0.5
        near, far = scale * (plus + minus), scale * (plus - minus)
        top = jnp.max(jnp.maximum(near, far), axis=1, keepdims=True)
        top = across(jnp.maximum, top)
        tops = jnp.concatenate([top] * N1, axis=0)
        near, far = jnp.exp(near - tops), jnp.exp(far - tops)
        e_ref[0] = near
        e_ref[1] = far
        amount = across(jnp.add, jnp.sum(near + far, axis=1, keepdims=True))
        stat_ref[0] = jnp.broadcast_to(top, (group, LANES))
        stat_ref[1] = jnp.broadcast_to(amount, (group, LANES))

    return pl.pallas_call(
        body,
        out_shape=(VM((2, half, cols), F32), VM((2, group, LANES), F32)),
        in_specs=[spec(pltpu.SMEM), spec(), spec(), spec()],
        out_specs=(spec(), spec()),
        compiler_params=params(),
        name="local_softmax",
    )(me, here(scores), here(precision), here(others))


def normalize(e, mine, theirs, copies):
    _, half, cols = e.shape
    group = mine.shape[1]

    def body(e_ref, a_ref, b_ref, out_ref):
        def flipped(x):
            return jnp.concatenate([x[group // 2 :], x[: group // 2]], axis=0)

        top_a, sum_a = a_ref[0], a_ref[1]
        top_b, sum_b = flipped(b_ref[0]), flipped(b_ref[1])
        top = jnp.maximum(top_a, top_b)
        part = jnp.exp(top_a - top)
        factor = part / (sum_a * part + sum_b * jnp.exp(top_b - top))
        factor = jnp.concatenate([jnp.concatenate([factor] * N1, axis=0)] * (cols // LANES), axis=1)
        near, far = e_ref[0] * factor, e_ref[1] * factor
        w = jnp.concatenate([near + far, near - far], axis=0).T.astype(BF)
        for c in range(copies):
            out_ref[c] = w

    return pl.pallas_call(
        body,
        out_shape=VM((copies, cols, 2 * half), BF),
        in_specs=[spec(), spec(), spec()],
        out_specs=spec(),
        compiler_params=params(),
        name="normalize",
    )(here(e), here(mine), here(theirs))


def accumulate(me, weights, turned, ny, nz, step):
    owners = ny * nz
    nb, cols, lanes = weights.shape
    cycles = turned.shape[1]
    classes = cols // N2
    per = LANES // N2
    pair = 2 * LANES

    def body(me_ref, w_ref, x_ref, out_ref, scr):
        left = lax.broadcasted_iota(jnp.int32, (cols, lanes), 1) < lanes // 2
        near, far = [], []
        for j in range(0, nb, 2):
            a, b = w_ref[j], w_ref[j + 1]
            near.append(jnp.where(left, a, pltpu.roll(b, lanes // 2, 1)))
            far.append(jnp.where(left, pltpu.roll(a, lanes // 2, 1), b))
        w = [jnp.concatenate(v, axis=1) for v in (near, far)]
        for c in range(0, cycles, 2):
            spread = []
            for i in range(2):
                both = jnp.concatenate([x_ref[i, c], x_ref[i, c + 1]], axis=1)
                spread.append(jnp.dot(w[i], both, preferred_element_type=F32))
            for d in range(2):
                plus = minus = None
                for s in range(N2):
                    p, m = (
                        jnp.concatenate(
                            [
                                v[t + s * per : t + (s + 1) * per, d * LANES : (d + 1) * LANES]
                                for t in range(0, cols, LANES)
                            ],
                            axis=0,
                        )
                        for v in spread
                    )
                    p, m = turn(p, m, step * N1 * s)
                    plus = plus + p if s else p
                    minus = minus + m if s else m
                rows = pl.ds(c + d, classes, stride=cycles)
                scr.at[0][rows, :] = 0.5 * (plus + minus)
                scr.at[1][rows, :] = 0.5 * (plus - minus)
        whole = jnp.concatenate([scr[0], scr[1]], axis=1)
        whole = whole.reshape(out_ref.shape).astype(BF)
        place = me_ref[0] // (2 * nb)
        y, z = place // nz, place % nz
        for slot in range(owners):
            dz, dy = PARTNERS[slot // ny], slot % ny
            out_ref[(y ^ dy) * nz + (z ^ dz)] = whole[slot]

    return pl.pallas_call(
        body,
        out_shape=VM((owners, classes // owners * cycles, pair), BF),
        in_specs=[spec(pltpu.SMEM), spec(), spec()],
        out_specs=spec(),
        scratch_shapes=[
            VM((2, classes * cycles, LANES), F32),
        ],
        compiler_params=params(),
        name="accumulate",
    )(me, here(weights), here(turned))


def add_up(parts):
    def body(x_ref, out_ref):
        total = x_ref[0].astype(F32)
        for i in range(1, parts.shape[0]):
            total = total + x_ref[i].astype(F32)
        out_ref[...] = total

    return pl.pallas_call(
        body,
        out_shape=jax.ShapeDtypeStruct(parts.shape[1:], F32),
        in_specs=[spec()],
        out_specs=spec(),
        compiler_params=params(),
        name="add_up",
    )(here(parts))


def solution(mesh):
    dom, nb = mesh.devices.shape
    ny, nz = 2, dom // 4
    view = Mesh(mesh.devices.reshape(ny, nz, 2, nb), ("yh", "z", "core", "blk"))
    swap = [(0, 1), (1, 0)]

    def shards(images, ref_store, block_owner, class_gain, precision):
        particles, cycles, angles = images.shape
        kb = ref_store.shape[2]
        rot = angles // (2 * N1 * N2)
        other = lax.ppermute(images, "core", swap)
        other_precision = lax.ppermute(precision, "core", swap)
        y, z = lax.axis_index("yh"), lax.axis_index("z")
        me = ((y * nz + z) * 2 + lax.axis_index("core")) * nb + lax.axis_index("blk")
        me = me[None].astype(jnp.int32)
        mine = pick_block(me, nb, block_owner, class_gain, ref_store[0])
        theirs = lax.ppermute(mine, "yh", swap)
        halves = halve_images(images, other, nb)
        refs = [pair_up(mine, theirs, halves, other_precision)]
        for d in PARTNERS[1:]:
            ring = [(i, i ^ d) for i in range(nz)]
            refs.append(lax.ppermute(refs[0], "z", ring))
        turned = turn_images(halves, nb, rot)
        early = correlate(turned, refs[:2], nb, rot)
        scores = correlate(turned, refs[2:], nb, rot, (early,))
        scores = lax.all_to_all(scores, "blk", 0, 0)
        flat = (1, particles)
        e, stats = local_softmax(
            me, scores, precision.reshape(flat), other_precision.reshape(flat)
        )
        theirs = lax.ppermute(stats, "core", swap)
        weights = normalize(e, stats, theirs, nb)
        weights = lax.all_to_all(weights, "blk", 0, 0)
        totals = accumulate(me, weights, turned, ny, nz, rot)
        totals = lax.all_to_all(totals, ("yh", "z"), 0, 0)
        return add_up(totals).reshape(1, 1, kb, cycles, angles)

    dom_axes = ("yh", "z", "core")
    return jax.shard_map(
        shards,
        mesh=view,
        in_specs=(
            P(dom_axes, "blk", None),
            P(dom_axes, None, None, "blk", None),
            P(),
            P(),
            P(dom_axes),
        ),
        out_specs=P(dom_axes, None, None, "blk", None),
        check_vma=False,
    )
```

```python
import jax
import jax.numpy as jnp
from jax import lax
from jax.experimental import pallas as pl
from jax.experimental.pallas import tpu as pltpu
from jax.sharding import Mesh, PartitionSpec as P


BF = jnp.bfloat16
F32 = jnp.float32
VM = pltpu.VMEM
LANES = 128
N1 = 4
N2 = 8
PARTNERS = (0, 1, 3, 2)


def spec(space=VM):
    return pl.BlockSpec(memory_space=space)


def params(mib=24):
    return pltpu.CompilerParams(vmem_limit_bytes=mib * 1024 * 1024)


def here(x):
    return pltpu.with_memory_space_constraint(x, VM)


def away(x):
    return pltpu.with_memory_space_constraint(x, pltpu.HBM)


def fill(scr, value):
    for h in range(scr.shape[0]):
        scr[h] = value[:, h * LANES : (h + 1) * LANES]


def take_cycle(scr, r, rows, cycles):
    return [scr.at[h][pl.ds(r, rows, stride=cycles), :] for h in range(2)]


def narrow(x):
    wide = x * 65537.0
    return wide - (wide - x)


def narrow_sum(x):
    near = narrow(x)
    lane = lax.broadcasted_iota(jnp.int32, x.shape, 1)
    rest = jnp.sum(x - near, axis=1, keepdims=True)
    return jnp.where(lane == 0, near + rest, near)


def turn(plus, minus, t):
    t = t % (2 * LANES)
    if t == 0:
        return plus, minus
    if t >= LANES:
        return turn(plus, -minus, t - LANES)
    lane = lax.broadcasted_iota(jnp.int32, minus.shape, 1)
    minus = pltpu.roll(minus, t, 1)
    return pltpu.roll(plus, t, 1), jnp.where(lane < t, -minus, minus)


def pick_block(me, nb, block_owner, class_gain, ref_store):
    nblk, kb, cycles, angles = ref_store.shape

    def body(me_ref, owner_ref, gain_ref, store_ref, out_ref):
        block = jnp.int32(0)
        for b in range(nblk):
            block = jnp.where(owner_ref[b] == me_ref[0] // nb, jnp.int32(b), block)
        for i in range(kb):
            piece = (store_ref[block, i].astype(F32) * gain_ref[block * kb + i]).astype(BF).astype(F32)
            a, b = piece[:, :LANES], piece[:, LANES:]
            piece = jnp.concatenate([narrow_sum(a + b), narrow(a - b)], axis=1).astype(BF)
            out_ref[i * cycles : (i + 1) * cycles, :] = piece

    return pl.pallas_call(
        body,
        out_shape=VM((kb * cycles, angles), BF),
        in_specs=[spec(pltpu.SMEM), spec(pltpu.SMEM), spec(pltpu.SMEM), spec()],
        out_specs=spec(),
        compiler_params=params(60),
        name="pick_block",
    )(me, block_owner, class_gain, away(ref_store))


def halve_images(own, other, nb):
    particles, cycles, angles = own.shape
    per = particles // nb

    def body(own_hbm, other_ref, out_ref, a_scr, b_scr, own_ref, sem):
        copy = pltpu.make_async_copy(own_hbm, own_ref, sem)
        copy.start()
        fill(b_scr, other_ref[...].astype(F32).reshape(particles * cycles, angles))
        copy.wait()
        fill(a_scr, own_ref[...].astype(F32).reshape(particles * cycles, angles))
        for r in range(cycles):
            a = take_cycle(a_scr, r, particles, cycles)
            b = take_cycle(b_scr, r, particles, cycles)
            for i, op in enumerate((jnp.add, jnp.subtract)):
                x, y = op(a[0], a[1]), op(b[0], b[1])
                both = [v.reshape(nb, per, LANES) for v in (x, y)]
                both = jnp.concatenate(both, axis=1).reshape(2 * particles, LANES)
                out_ref[i, r] = narrow(both).astype(BF)

    return pl.pallas_call(
        body,
        out_shape=VM((2, cycles, 2 * particles, LANES), BF),
        in_specs=[spec(pltpu.HBM), spec()],
        out_specs=spec(),
        scratch_shapes=[VM((2, particles * cycles, LANES), F32)] * 2
        + [VM(own.shape, BF), pltpu.SemaphoreType.DMA],
        compiler_params=params(),
        name="halve_images",
    )(away(own), here(other))


def pair_up(mine, theirs, *others):
    def body(a_ref, b_ref, *refs):
        out_ref = refs[-1]
        out_ref[0] = a_ref[...]
        out_ref[1] = b_ref[...]

    return pl.pallas_call(
        body,
        out_shape=VM((2,) + mine.shape, BF),
        in_specs=[spec()] * (2 + len(others)),
        out_specs=spec(),
        compiler_params=params(),
        name="pair_up",
    )(here(mine), here(theirs), *[here(o) for o in others])


def rotate_images(x_ref, r, nb, step):
    plus, minus = x_ref[0, r], x_ref[1, r]
    per = plus.shape[0] // nb
    turned = [turn(plus, minus, step * s) for s in range(N1)]
    return [
        jnp.concatenate(
            [t[i][j * per : (j + 1) * per] for j in range(nb) for t in turned], axis=0
        )
        for i in range(2)
    ]


def turn_images(images, nb, step):
    _, cycles, particles, _ = images.shape

    def body(x_ref, out_ref):
        for r in range(cycles):
            out_ref[0, r], out_ref[1, r] = rotate_images(x_ref, r, nb, step)

    return pl.pallas_call(
        body,
        out_shape=VM((2, cycles, N1 * particles, LANES), BF),
        in_specs=[spec()],
        out_specs=spec(),
        compiler_params=params(),
        name="turn_images",
    )(here(images))


def correlate(turned, refs, nb, step, before=()):
    _, cycles, total, _ = turned.shape
    rows = total // nb
    near, far = refs[0].shape[:2]
    classes = len(refs) * near * far // cycles
    cols = N2 * classes
    angles = 2 * LANES
    tiles = 1 + len(before)

    def body(x_ref, *args):
        r_refs, (out_ref, scr, rr) = args[: len(refs)], args[-3:]
        for t, b_ref in enumerate(args[len(refs) : -3]):
            out_ref[:, t] = b_ref[:, 0]
        blocks = [r_ref[d].astype(F32) for r_ref in r_refs for d in range(near)]
        fill(scr, jnp.concatenate(blocks, axis=0))
        square = jnp.zeros((classes, LANES), F32)
        for r in range(cycles):
            plus, minus = take_cycle(scr, r, classes, cycles)
            square = square + 0.5 * (plus * plus + minus * minus)
            plus, minus = plus.astype(BF), minus.astype(BF)
            for s in range(N2):
                p, m = turn(plus, minus, angles - step * N1 * s)
                rr[0, r, s * classes : (s + 1) * classes, :] = p
                rr[1, r, s * classes : (s + 1) * classes, :] = m
        norm = jnp.broadcast_to(jnp.sum(square, axis=1, keepdims=True), (classes, cols))
        k = lax.broadcasted_iota(jnp.int32, (classes, cols), 0)
        lane = lax.broadcasted_iota(jnp.int32, (classes, cols), 1)
        norm = jnp.sum(jnp.where(lane % classes == k, norm, 0.0), axis=0, keepdims=True)
        for i in range(2):
            left = jnp.concatenate([x_ref[i, r] for r in range(cycles)], axis=1)
            right = jnp.concatenate([rr[i, r] for r in range(cycles)], axis=1)
            part = lax.dot_general(
                left, right, (((1,), (1,)), ((), ())), preferred_element_type=F32
            )
            if i == 0:
                part = part - norm
            at = slice(i * rows, (i + 1) * rows)
            out_ref[:, tiles - 1, at, :] = part.astype(BF).reshape(nb, rows, LANES)

    return pl.pallas_call(
        body,
        out_shape=VM((nb, tiles, 2 * rows, LANES), BF),
        in_specs=[spec()] * (len(refs) + tiles),
        out_specs=spec(),
        scratch_shapes=[
            VM((2, classes * cycles, LANES), F32),
            VM((2, cycles, cols, LANES), BF),
        ],
        compiler_params=params(),
        name="correlate",
    )(here(turned), *[here(r) for r in (*refs, *before)])


def local_softmax(me, scores, precision, others):
    nb, tiles, rows, _ = scores.shape
    cols = tiles * LANES
    half = rows // 2
    group = half // N1
    own = group // 2

    def across(op, x):
        pieces = [x[i * group : (i + 1) * group] for i in range(N1)]
        return op(op(pieces[0], pieces[1]), op(pieces[2], pieces[3]))

    def body(me_ref, x_ref, a_ref, b_ref, e_ref, stat_ref):
        total = x_ref[0].astype(F32)
        for i in range(1, nb):
            total = total + x_ref[i].astype(F32)
        total = jnp.concatenate([total[t] for t in range(tiles)], axis=1)
        plus, minus = total[:half], total[half:]
        wide = (own, nb * own)
        row = lax.broadcasted_iota(jnp.int32, wide, 0) + me_ref[0] % nb * own
        mine = row == lax.broadcasted_iota(jnp.int32, wide, 1)
        scale = [
            jnp.sum(jnp.where(mine, ref[...], 0.0), axis=1, keepdims=True)
            for ref in (a_ref, b_ref)
        ]
        scale = jnp.concatenate(scale * N1, axis=0) * 0.5
        near, far = scale * (plus + minus), scale * (plus - minus)
        top = jnp.max(jnp.maximum(near, far), axis=1, keepdims=True)
        top = across(jnp.maximum, top)
        tops = jnp.concatenate([top] * N1, axis=0)
        near, far = jnp.exp(near - tops), jnp.exp(far - tops)
        e_ref[0] = near
        e_ref[1] = far
        amount = across(jnp.add, jnp.sum(near + far, axis=1, keepdims=True))
        stat_ref[0] = jnp.broadcast_to(top, (group, LANES))
        stat_ref[1] = jnp.broadcast_to(amount, (group, LANES))

    return pl.pallas_call(
        body,
        out_shape=(VM((2, half, cols), F32), VM((2, group, LANES), F32)),
        in_specs=[spec(pltpu.SMEM), spec(), spec(), spec()],
        out_specs=(spec(), spec()),
        compiler_params=params(),
        name="local_softmax",
    )(me, here(scores), here(precision), here(others))


def normalize(e, mine, theirs, copies):
    _, half, cols = e.shape
    group = mine.shape[1]

    def body(e_ref, a_ref, b_ref, out_ref):
        def flipped(x):
            return jnp.concatenate([x[group // 2 :], x[: group // 2]], axis=0)

        top_a, sum_a = a_ref[0], a_ref[1]
        top_b, sum_b = flipped(b_ref[0]), flipped(b_ref[1])
        top = jnp.maximum(top_a, top_b)
        part = jnp.exp(top_a - top)
        factor = part / (sum_a * part + sum_b * jnp.exp(top_b - top))
        factor = jnp.concatenate([jnp.concatenate([factor] * N1, axis=0)] * (cols // LANES), axis=1)
        near, far = e_ref[0] * factor, e_ref[1] * factor
        w = jnp.concatenate([near + far, near - far], axis=0).T.astype(BF)
        for c in range(copies):
            out_ref[c] = w

    return pl.pallas_call(
        body,
        out_shape=VM((copies, cols, 2 * half), BF),
        in_specs=[spec(), spec(), spec()],
        out_specs=spec(),
        compiler_params=params(),
        name="normalize",
    )(here(e), here(mine), here(theirs))


def accumulate(me, weights, turned, ny, nz, step):
    owners = ny * nz
    nb, cols, lanes = weights.shape
    cycles = turned.shape[1]
    classes = cols // N2
    per = LANES // N2
    pair = 2 * LANES

    def body(me_ref, w_ref, x_ref, out_ref, scr):
        left = lax.broadcasted_iota(jnp.int32, (cols, lanes), 1) < lanes // 2
        near, far = [], []
        for j in range(0, nb, 2):
            a, b = w_ref[j], w_ref[j + 1]
            near.append(jnp.where(left, a, pltpu.roll(b, lanes // 2, 1)))
            far.append(jnp.where(left, pltpu.roll(a, lanes // 2, 1), b))
        w = [jnp.concatenate(v, axis=1) for v in (near, far)]
        for c in range(0, cycles, 2):
            spread = []
            for i in range(2):
                both = jnp.concatenate([x_ref[i, c], x_ref[i, c + 1]], axis=1)
                spread.append(jnp.dot(w[i], both, preferred_element_type=F32))
            for d in range(2):
                plus = minus = None
                for s in range(N2):
                    p, m = (
                        jnp.concatenate(
                            [
                                v[t + s * per : t + (s + 1) * per, d * LANES : (d + 1) * LANES]
                                for t in range(0, cols, LANES)
                            ],
                            axis=0,
                        )
                        for v in spread
                    )
                    p, m = turn(p, m, step * N1 * s)
                    plus = plus + p if s else p
                    minus = minus + m if s else m
                rows = pl.ds(c + d, classes, stride=cycles)
                scr.at[0][rows, :] = 0.5 * (plus + minus)
                scr.at[1][rows, :] = 0.5 * (plus - minus)
        whole = jnp.concatenate([scr[0], scr[1]], axis=1)
        whole = whole.reshape(out_ref.shape).astype(BF)
        place = me_ref[0] // (2 * nb)
        y, z = place // nz, place % nz
        for slot in range(owners):
            dz, dy = PARTNERS[slot // ny], slot % ny
            out_ref[(y ^ dy) * nz + (z ^ dz)] = whole[slot]

    return pl.pallas_call(
        body,
        out_shape=VM((owners, classes // owners * cycles, pair), BF),
        in_specs=[spec(pltpu.SMEM), spec(), spec()],
        out_specs=spec(),
        scratch_shapes=[
            VM((2, classes * cycles, LANES), F32),
        ],
        compiler_params=params(),
        name="accumulate",
    )(me, here(weights), here(turned))


def add_up(parts):
    def body(x_ref, out_ref):
        total = x_ref[0].astype(F32)
        for i in range(1, parts.shape[0]):
            total = total + x_ref[i].astype(F32)
        out_ref[...] = total

    return pl.pallas_call(
        body,
        out_shape=jax.ShapeDtypeStruct(parts.shape[1:], F32),
        in_specs=[spec()],
        out_specs=spec(),
        compiler_params=params(),
        name="add_up",
    )(here(parts))


def solution(mesh):
    dom, nb = mesh.devices.shape
    ny, nz = 2, dom // 4
    view = Mesh(mesh.devices.reshape(ny, nz, 2, nb), ("yh", "z", "core", "blk"))
    swap = [(0, 1), (1, 0)]

    def shards(images, ref_store, block_owner, class_gain, precision):
        particles, cycles, angles = images.shape
        kb = ref_store.shape[2]
        rot = angles // (2 * N1 * N2)
        other = lax.ppermute(images, "core", swap)
        other_precision = lax.ppermute(precision, "core", swap)
        y, z = lax.axis_index("yh"), lax.axis_index("z")
        me = ((y * nz + z) * 2 + lax.axis_index("core")) * nb + lax.axis_index("blk")
        me = me[None].astype(jnp.int32)
        mine = pick_block(me, nb, block_owner, class_gain, ref_store[0])
        theirs = lax.ppermute(mine, "yh", swap)
        halves = halve_images(images, other, nb)
        refs = [pair_up(mine, theirs, halves, other_precision)]
        for d in PARTNERS[1:]:
            ring = [(i, i ^ d) for i in range(nz)]
            refs.append(lax.ppermute(refs[0], "z", ring))
        turned = turn_images(halves, nb, rot)
        early = correlate(turned, refs[:2], nb, rot)
        scores = correlate(turned, refs[2:], nb, rot, (early,))
        scores = lax.all_to_all(scores, "blk", 0, 0)
        flat = (1, particles)
        e, stats = local_softmax(
            me, scores, precision.reshape(flat), other_precision.reshape(flat)
        )
        theirs = lax.ppermute(stats, "core", swap)
        weights = normalize(e, stats, theirs, nb)
        weights = lax.all_to_all(weights, "blk", 0, 0)
        totals = accumulate(me, weights, turned, ny, nz, rot)
        totals = lax.all_to_all(totals, ("yh", "z"), 0, 0)
        return add_up(totals).reshape(1, 1, kb, cycles, angles)

    dom_axes = ("yh", "z", "core")
    return jax.shard_map(
        shards,
        mesh=view,
        in_specs=(
            P(dom_axes, "blk", None),
            P(dom_axes, None, None, "blk", None),
            P(),
            P(),
            P(dom_axes),
        ),
        out_specs=P(dom_axes, None, None, "blk", None),
        check_vma=False,
    )
```

```python
import jax
import jax.numpy as jnp
from jax import lax
from jax.experimental import pallas as pl
from jax.experimental.pallas import tpu as pltpu
from jax.sharding import Mesh, PartitionSpec as P


BF = jnp.bfloat16
F32 = jnp.float32
VM = pltpu.VMEM
LANES = 128
N1 = 4
N2 = 8
PARTNERS = (0, 1, 3, 2)


def spec(space=VM):
    return pl.BlockSpec(memory_space=space)


def params(mib=24):
    return pltpu.CompilerParams(vmem_limit_bytes=mib * 1024 * 1024)


def here(x):
    return pltpu.with_memory_space_constraint(x, VM)


def away(x):
    return pltpu.with_memory_space_constraint(x, pltpu.HBM)


def fill(scr, value):
    for h in range(scr.shape[0]):
        scr[h] = value[:, h * LANES : (h + 1) * LANES]


def take_cycle(scr, r, rows, cycles):
    return [scr.at[h][pl.ds(r, rows, stride=cycles), :] for h in range(2)]


def narrow(x):
    wide = x * 65537.0
    return wide - (wide - x)


def narrow_sum(x):
    near = narrow(x)
    lane = lax.broadcasted_iota(jnp.int32, x.shape, 1)
    rest = jnp.sum(x - near, axis=1, keepdims=True)
    return jnp.where(lane == 0, near + rest, near)


def turn(plus, minus, t):
    t = t % (2 * LANES)
    if t == 0:
        return plus, minus
    if t >= LANES:
        return turn(plus, -minus, t - LANES)
    lane = lax.broadcasted_iota(jnp.int32, minus.shape, 1)
    minus = pltpu.roll(minus, t, 1)
    return pltpu.roll(plus, t, 1), jnp.where(lane < t, -minus, minus)


def pick_block(me, nb, block_owner, class_gain, ref_store):
    nblk, kb, cycles, angles = ref_store.shape

    def body(me_ref, owner_ref, gain_ref, store_ref, out_ref):
        block = jnp.int32(0)
        for b in range(nblk):
            block = jnp.where(owner_ref[b] == me_ref[0] // nb, jnp.int32(b), block)
        for i in range(kb):
            piece = (store_ref[block, i].astype(F32) * gain_ref[block * kb + i]).astype(BF).astype(F32)
            a, b = piece[:, :LANES], piece[:, LANES:]
            piece = jnp.concatenate([narrow_sum(a + b), narrow(a - b)], axis=1).astype(BF)
            out_ref[i * cycles : (i + 1) * cycles, :] = piece

    return pl.pallas_call(
        body,
        out_shape=VM((kb * cycles, angles), BF),
        in_specs=[spec(pltpu.SMEM), spec(pltpu.SMEM), spec(pltpu.SMEM), spec()],
        out_specs=spec(),
        compiler_params=params(60),
        name="pick_block",
    )(me, block_owner, class_gain, away(ref_store))


def halve_images(own, other, nb):
    particles, cycles, angles = own.shape
    per = particles // nb

    def body(own_hbm, other_ref, out_ref, a_scr, b_scr, own_ref, sem):
        copy = pltpu.make_async_copy(own_hbm, own_ref, sem)
        copy.start()
        for h, ref, scr in ((1, other_ref, b_scr), (0, own_ref, a_scr)):
            if h == 0:
                copy.wait()
            fill(scr, ref[...].astype(F32).reshape(particles * cycles, angles))
            for r in range(cycles):
                a, b = take_cycle(scr, r, particles, cycles)
                for i, v in enumerate((a + b, a - b)):
                    v = narrow(v)
                    for j in range(nb):
                        at = (2 * j + h) * per
                        piece = v[j * per : (j + 1) * per]
                        out_ref[i, r, at : at + per, :] = piece.astype(BF)

    return pl.pallas_call(
        body,
        out_shape=VM((2, cycles, 2 * particles, LANES), BF),
        in_specs=[spec(pltpu.HBM), spec()],
        out_specs=spec(),
        scratch_shapes=[VM((2, particles * cycles, LANES), F32)] * 2
        + [VM(own.shape, BF), pltpu.SemaphoreType.DMA],
        compiler_params=params(),
        name="halve_images",
    )(away(own), here(other))


def pair_up(mine, theirs, *others):
    def body(a_ref, b_ref, *refs):
        out_ref = refs[-1]
        out_ref[0] = a_ref[...]
        out_ref[1] = b_ref[...]

    return pl.pallas_call(
        body,
        out_shape=VM((2,) + mine.shape, BF),
        in_specs=[spec()] * (2 + len(others)),
        out_specs=spec(),
        compiler_params=params(),
        name="pair_up",
    )(here(mine), here(theirs), *[here(o) for o in others])


def rotate_images(x_ref, r, nb, step):
    plus, minus = x_ref[0, r], x_ref[1, r]
    per = plus.shape[0] // nb
    turned = [turn(plus, minus, step * s) for s in range(N1)]
    return [
        jnp.concatenate(
            [t[i][j * per : (j + 1) * per] for j in range(nb) for t in turned], axis=0
        )
        for i in range(2)
    ]


def turn_images(images, nb, step):
    _, cycles, particles, _ = images.shape

    def body(x_ref, out_ref):
        for r in range(cycles):
            out_ref[0, r], out_ref[1, r] = rotate_images(x_ref, r, nb, step)

    return pl.pallas_call(
        body,
        out_shape=VM((2, cycles, N1 * particles, LANES), BF),
        in_specs=[spec()],
        out_specs=spec(),
        compiler_params=params(),
        name="turn_images",
    )(here(images))


def correlate(turned, refs, nb, step, before=()):
    _, cycles, total, _ = turned.shape
    rows = total // nb
    near, far = refs[0].shape[:2]
    classes = len(refs) * near * far // cycles
    cols = N2 * classes
    angles = 2 * LANES
    tiles = 1 + len(before)

    def body(x_ref, *args):
        r_refs, (out_ref, scr) = args[: len(refs)], args[-2:]
        for t, b_ref in enumerate(args[len(refs) : -2]):
            out_ref[:, t] = b_ref[:, 0]
        blocks = [r_ref[d].astype(F32) for r_ref in r_refs for d in range(near)]
        fill(scr, jnp.concatenate(blocks, axis=0))
        square = jnp.zeros((classes, LANES), F32)
        for r in range(cycles):
            plus, minus = take_cycle(scr, r, classes, cycles)
            square = square + 0.5 * (plus * plus + minus * minus)
        norm = jnp.broadcast_to(jnp.sum(square, axis=1, keepdims=True), (classes, cols))
        k = lax.broadcasted_iota(jnp.int32, (classes, cols), 0)
        lane = lax.broadcasted_iota(jnp.int32, (classes, cols), 1)
        norm = jnp.sum(jnp.where(lane % classes == k, norm, 0.0), axis=0, keepdims=True)
        for i in range(2):
            left = jnp.concatenate([x_ref[i, r] for r in range(cycles)], axis=1)
            right = []
            for r in range(cycles):
                v = take_cycle(scr, r, classes, cycles)[i].astype(BF)
                v = [turn(v, v, angles - step * N1 * s)[i] for s in range(N2)]
                right.append(jnp.concatenate(v, axis=0))
            right = jnp.concatenate(right, axis=1)
            part = lax.dot_general(
                left, right, (((1,), (1,)), ((), ())), preferred_element_type=F32
            )
            if i == 0:
                part = part - norm
            at = slice(i * rows, (i + 1) * rows)
            out_ref[:, tiles - 1, at, :] = part.astype(BF).reshape(nb, rows, LANES)

    return pl.pallas_call(
        body,
        out_shape=VM((nb, tiles, 2 * rows, LANES), BF),
        in_specs=[spec()] * (len(refs) + tiles),
        out_specs=spec(),
        scratch_shapes=[VM((2, classes * cycles, LANES), F32)],
        compiler_params=params(),
        name="correlate",
    )(here(turned), *[here(r) for r in (*refs, *before)])


def local_softmax(me, scores, precision, others):
    nb, tiles, rows, _ = scores.shape
    cols = tiles * LANES
    half = rows // 2
    group = half // N1
    own = group // 2

    def across(op, x):
        pieces = [x[i * group : (i + 1) * group] for i in range(N1)]
        return op(op(pieces[0], pieces[1]), op(pieces[2], pieces[3]))

    def body(me_ref, x_ref, a_ref, b_ref, e_ref, stat_ref):
        total = x_ref[0].astype(F32)
        for i in range(1, nb):
            total = total + x_ref[i].astype(F32)
        total = jnp.concatenate([total[t] for t in range(tiles)], axis=1)
        plus, minus = total[:half], total[half:]
        wide = (own, nb * own)
        row = lax.broadcasted_iota(jnp.int32, wide, 0) + me_ref[0] % nb * own
        mine = row == lax.broadcasted_iota(jnp.int32, wide, 1)
        scale = [
            jnp.sum(jnp.where(mine, ref[...], 0.0), axis=1, keepdims=True)
            for ref in (a_ref, b_ref)
        ]
        scale = jnp.concatenate(scale * N1, axis=0) * 0.5
        near, far = scale * (plus + minus), scale * (plus - minus)
        top = jnp.max(jnp.maximum(near, far), axis=1, keepdims=True)
        top = across(jnp.maximum, top)
        tops = jnp.concatenate([top] * N1, axis=0)
        near, far = jnp.exp(near - tops), jnp.exp(far - tops)
        e_ref[0] = near
        e_ref[1] = far
        amount = across(jnp.add, jnp.sum(near + far, axis=1, keepdims=True))
        stat_ref[0] = jnp.broadcast_to(top, (group, LANES))
        stat_ref[1] = jnp.broadcast_to(amount, (group, LANES))

    return pl.pallas_call(
        body,
        out_shape=(VM((2, half, cols), F32), VM((2, group, LANES), F32)),
        in_specs=[spec(pltpu.SMEM), spec(), spec(), spec()],
        out_specs=(spec(), spec()),
        compiler_params=params(),
        name="local_softmax",
    )(me, here(scores), here(precision), here(others))


def normalize(e, mine, theirs, copies):
    _, half, cols = e.shape
    group = mine.shape[1]

    def body(e_ref, a_ref, b_ref, out_ref):
        def flipped(x):
            return jnp.concatenate([x[group // 2 :], x[: group // 2]], axis=0)

        top_a, sum_a = a_ref[0], a_ref[1]
        top_b, sum_b = flipped(b_ref[0]), flipped(b_ref[1])
        top = jnp.maximum(top_a, top_b)
        part = jnp.exp(top_a - top)
        factor = part / (sum_a * part + sum_b * jnp.exp(top_b - top))
        factor = jnp.concatenate([jnp.concatenate([factor] * N1, axis=0)] * (cols // LANES), axis=1)
        near, far = e_ref[0] * factor, e_ref[1] * factor
        w = jnp.concatenate([near + far, near - far], axis=0).T.astype(BF)
        for c in range(copies):
            out_ref[c] = w

    return pl.pallas_call(
        body,
        out_shape=VM((copies, cols, 2 * half), BF),
        in_specs=[spec(), spec(), spec()],
        out_specs=spec(),
        compiler_params=params(),
        name="normalize",
    )(here(e), here(mine), here(theirs))


def accumulate(me, weights, turned, ny, nz, step):
    owners = ny * nz
    nb, cols, lanes = weights.shape
    cycles = turned.shape[1]
    classes = cols // N2
    per = LANES // N2
    pair = 2 * LANES

    def body(me_ref, w_ref, x_ref, out_ref, scr):
        left = lax.broadcasted_iota(jnp.int32, (cols, lanes), 1) < lanes // 2
        near, far = [], []
        for j in range(0, nb, 2):
            a, b = w_ref[j], w_ref[j + 1]
            near.append(jnp.where(left, a, pltpu.roll(b, lanes // 2, 1)))
            far.append(jnp.where(left, pltpu.roll(a, lanes // 2, 1), b))
        w = [jnp.concatenate(v, axis=1) for v in (near, far)]
        for c in range(0, cycles, 2):
            spread = []
            for i in range(2):
                both = jnp.concatenate([x_ref[i, c], x_ref[i, c + 1]], axis=1)
                spread.append(jnp.dot(w[i], both, preferred_element_type=F32))
            for d in range(2):
                plus = minus = None
                for s in range(N2):
                    p, m = (
                        jnp.concatenate(
                            [
                                v[t + s * per : t + (s + 1) * per, d * LANES : (d + 1) * LANES]
                                for t in range(0, cols, LANES)
                            ],
                            axis=0,
                        )
                        for v in spread
                    )
                    p, m = turn(p, m, step * N1 * s)
                    plus = plus + p if s else p
                    minus = minus + m if s else m
                rows = pl.ds(c + d, classes, stride=cycles)
                scr.at[0][rows, :] = 0.5 * (plus + minus)
                scr.at[1][rows, :] = 0.5 * (plus - minus)
        whole = jnp.concatenate([scr[0], scr[1]], axis=1)
        whole = whole.reshape(out_ref.shape).astype(BF)
        place = me_ref[0] // (2 * nb)
        y, z = place // nz, place % nz
        for slot in range(owners):
            dz, dy = PARTNERS[slot // ny], slot % ny
            out_ref[(y ^ dy) * nz + (z ^ dz)] = whole[slot]

    return pl.pallas_call(
        body,
        out_shape=VM((owners, classes // owners * cycles, pair), BF),
        in_specs=[spec(pltpu.SMEM), spec(), spec()],
        out_specs=spec(),
        scratch_shapes=[
            VM((2, classes * cycles, LANES), F32),
        ],
        compiler_params=params(),
        name="accumulate",
    )(me, here(weights), here(turned))


def add_up(parts):
    def body(x_ref, out_ref):
        total = x_ref[0].astype(F32)
        for i in range(1, parts.shape[0]):
            total = total + x_ref[i].astype(F32)
        out_ref[...] = total

    return pl.pallas_call(
        body,
        out_shape=jax.ShapeDtypeStruct(parts.shape[1:], F32),
        in_specs=[spec()],
        out_specs=spec(),
        compiler_params=params(),
        name="add_up",
    )(here(parts))


def solution(mesh):
    dom, nb = mesh.devices.shape
    ny, nz = 2, dom // 4
    view = Mesh(mesh.devices.reshape(ny, nz, 2, nb), ("yh", "z", "core", "blk"))
    swap = [(0, 1), (1, 0)]

    def shards(images, ref_store, block_owner, class_gain, precision):
        particles, cycles, angles = images.shape
        kb = ref_store.shape[2]
        rot = angles // (2 * N1 * N2)
        other = lax.ppermute(images, "core", swap)
        other_precision = lax.ppermute(precision, "core", swap)
        y, z = lax.axis_index("yh"), lax.axis_index("z")
        me = ((y * nz + z) * 2 + lax.axis_index("core")) * nb + lax.axis_index("blk")
        me = me[None].astype(jnp.int32)
        mine = pick_block(me, nb, block_owner, class_gain, ref_store[0])
        theirs = lax.ppermute(mine, "yh", swap)
        halves = halve_images(images, other, nb)
        refs = [pair_up(mine, theirs, halves, other_precision)]
        for d in PARTNERS[1:]:
            ring = [(i, i ^ d) for i in range(nz)]
            refs.append(lax.ppermute(refs[0], "z", ring))
        turned = turn_images(halves, nb, rot)
        early = correlate(turned, refs[:2], nb, rot)
        scores = correlate(turned, refs[2:], nb, rot, (early,))
        scores = lax.all_to_all(scores, "blk", 0, 0)
        flat = (1, particles)
        e, stats = local_softmax(
            me, scores, precision.reshape(flat), other_precision.reshape(flat)
        )
        theirs = lax.ppermute(stats, "core", swap)
        weights = normalize(e, stats, theirs, nb)
        weights = lax.all_to_all(weights, "blk", 0, 0)
        totals = accumulate(me, weights, turned, ny, nz, rot)
        totals = lax.all_to_all(totals, ("yh", "z"), 0, 0)
        return add_up(totals).reshape(1, 1, kb, cycles, angles)

    dom_axes = ("yh", "z", "core")
    return jax.shard_map(
        shards,
        mesh=view,
        in_specs=(
            P(dom_axes, "blk", None),
            P(dom_axes, None, None, "blk", None),
            P(),
            P(),
            P(dom_axes),
        ),
        out_specs=P(dom_axes, None, None, "blk", None),
        check_vma=False,
    )
```
